32 devices in a mesh: rows: 4 (over y, x), cols: 8 (over z, core).
Axes of the slice: x: 2, y: 2, z: 4, core: 2. Of those that a mesh axis runs over, the one named last changes fastest.
Arguments:
- pixels: bfloat16 [128, 256, 768], P('rows', 'cols'), may hold values from -6 to 6
- tissue: int32 [128, 256], P('rows', 'cols'), may hold values 0 or 1
- patch_weight: bfloat16 [768, 1024], replicated, may hold values from -0.21875 to 0.21875
- conv_weight: bfloat16 [9, 32, 1024], replicated, may hold values from -0.375 to 0.375
- kv_weight: bfloat16 [1024, 2048], replicated, may hold values from -0.1875 to 0.1875
- query_weight: bfloat16 [1024, 1024], replicated, may hold values from -0.1875 to 0.1875
- out_weight: bfloat16 [1024, 1024], replicated, may hold values from -0.1875 to 0.1875
- latents: bfloat16 [512, 1024], replicated, may hold values from -240 to 240
Outputs:
- features: bfloat16 [128, 256, 1024], P('rows', 'cols')
- latents_out: bfloat16 [512, 1024], P(('rows', 'cols'))
The draws below stay inside these ranges and needn't reach their ends.
Inputs may be any that keep to these rules, and one draw needn't show every extreme that they name: 1 marks a patch tile that holds tissue, and at least one tile of the slab holds tissue.
All inputs are finite; a program needn't handle non-finite values. No bound on the sum of `tissue` on one device may be relied on, other than what follows from the above.
Results may differ from the reference program's by a relative error of at most 0.03.
Values may be sent and summed in bfloat16 or wider, within the bound.
A program may use at most 128 MiB of HBM per device.

```python
import jax
import jax.numpy as jnp
from jax import lax

D = 1024
HEADS = 16
LAT = 512
PATCH_IN = 768
NR = 128
NC = 256
GW = 32


def draw_latents(key, part):
    first_key = jax.random.fold_in(key, 0)
    drawn = jax.random.normal(first_key, (LAT, D), jnp.float32)
    drawn = jnp.clip(drawn, -6.0, 6.0)
    return drawn.astype(jnp.bfloat16)


def touch_ends(values, own_key, smallest, high):
    extent = values.shape
    index_at = [jax.random.randint(jax.random.fold_in(own_key, axis), (), 0, extent[axis]) for axis in range(len(extent))]
    values = values.at[tuple(index_at)].set(smallest)
    longest = extent.index(max(extent))
    index_at[longest] = (index_at[longest] + 1) % extent[longest]
    return values.at[tuple(index_at)].set(high)


def block_scale(stream_key, dims, cuts, least, largest):
    gain = 1.0
    for position, blocks in cuts:
        steps = jax.random.uniform(jax.random.fold_in(jax.random.fold_in(stream_key, 6), position), (blocks,), jnp.float32, least / len(cuts), largest / len(cuts))
        gain = gain * jnp.repeat(jnp.exp(steps), dims[position] // blocks).reshape((-1,) + (1,) * (len(dims) - 1 - position))
    return gain


def gaussian(rng, extent, width, bound, pieces=(), kind=jnp.bfloat16):
    result = jax.random.normal(rng, extent, jnp.float32) * width
    if len(pieces) > 0:
        result = block_scale(rng, extent, pieces, -0.22, 0.18) * result
    return jnp.clip(result, min=-bound, max=bound).astype(kind)


def setup_inputs(seed: int = 0) -> dict:
    key_of = jax.random.split(jax.random.key(seed), 9)
    pixels = gaussian(key_of[0], (NR, NC, PATCH_IN), 1.0, 6.0, ((0, 4), (1, 8)))
    tissue = touch_ends((jax.random.randint(key_of[1], (NR, NC), 0, 5) < 3).astype(jnp.int32), jax.random.fold_in(key_of[1], 1), 0, 1)
    patch_weight = gaussian(key_of[2], (PATCH_IN, D), PATCH_IN ** -0.5, 0.21875)
    conv_weight = gaussian(key_of[3], (9, GW, D), (9 * GW) ** -0.5, 0.375)
    kv_weight = gaussian(key_of[4], (D, 2 * D), D ** -0.5, 0.1875)
    query_weight = gaussian(key_of[5], (D, D), D ** -0.5, 0.1875)
    out_weight = gaussian(key_of[6], (D, D), D ** -0.5, 0.1875)
    latents = draw_latents(jax.random.fold_in(key_of[8], 71), 0)
    return dict(pixels=pixels, tissue=tissue, patch_weight=patch_weight, conv_weight=conv_weight, kv_weight=kv_weight, query_weight=query_weight, out_weight=out_weight, latents=latents)


def reference(pixels, tissue, patch_weight, conv_weight, kv_weight, query_weight, out_weight, latents):
    rows_all, cols_all, patch_in = pixels.shape
    channels = patch_weight.shape[1]
    token_count = rows_all * cols_all
    embedded = jnp.dot(pixels.reshape(token_count, patch_in), patch_weight, preferred_element_type=jnp.float32)
    embedded = embedded.astype(jnp.bfloat16).reshape(rows_all, cols_all, channels)
    padded = jnp.pad(embedded, ((1, 1), (1, 1), (0, 0)))
    group_width = conv_weight.shape[1]
    group_count = channels // group_width
    kernel = conv_weight.astype(jnp.float32).reshape(9, group_width, group_count, group_width)
    convolved = jnp.zeros((rows_all, cols_all, group_count, group_width), jnp.float32)
    for row_shift in range(3):
        for col_shift in range(3):
            window = padded[row_shift:row_shift + rows_all, col_shift:col_shift + cols_all]
            window = window.astype(jnp.float32).reshape(rows_all, cols_all, group_count, group_width)
            convolved = convolved + jnp.einsum('hwgi,igo->hwgo', window, kernel[3 * row_shift + col_shift])
    summed = embedded.astype(jnp.float32) + convolved.reshape(rows_all, cols_all, channels)
    average = lax.optimization_barrier(jnp.mean(summed, axis=-1, keepdims=True))
    centred = summed - average
    variance = lax.optimization_barrier(jnp.mean(centred * centred, axis=-1, keepdims=True))
    features = (centred * lax.rsqrt(variance + 1e-05)).astype(jnp.bfloat16)
    projected = jnp.dot(features.reshape(token_count, channels), kv_weight, preferred_element_type=jnp.float32).astype(jnp.bfloat16)
    head_dim = channels // HEADS
    key_vectors = projected[:, :channels].reshape(token_count, HEADS, head_dim).transpose(1, 0, 2)
    value_vectors = projected[:, channels:].reshape(token_count, HEADS, head_dim).transpose(1, 0, 2)
    queries = jnp.dot(latents, query_weight, preferred_element_type=jnp.float32).astype(jnp.bfloat16)
    latent_count = latents.shape[0]
    queries = queries.reshape(latent_count, HEADS, head_dim).transpose(1, 0, 2)
    tissue_live = tissue.reshape(token_count) > 0

    def one_head(operands):
        query_head, key_head, value_head = operands
        scores = jnp.dot(query_head, key_head.T, preferred_element_type=jnp.float32) * head_dim ** (-0.5)
        scores = jnp.where(tissue_live[None, :], scores, -1e+30)
        highest = lax.optimization_barrier(jnp.max(scores, axis=1, keepdims=True))
        weights = jnp.where(tissue_live[None, :], jnp.exp(scores - highest), 0.0)
        denominator = lax.optimization_barrier(jnp.sum(weights, axis=1, keepdims=True))
        numerator = jnp.dot(weights.astype(jnp.bfloat16), value_head, preferred_element_type=jnp.float32)
        return numerator / denominator
    attended = lax.map(one_head, (queries, key_vectors, value_vectors))
    attended = attended.transpose(1, 0, 2).reshape(latent_count, channels)
    normed = (attended * lax.rsqrt(lax.optimization_barrier(jnp.mean(attended * attended, axis=-1, keepdims=True)) + 1e-06)).astype(jnp.bfloat16)
    latents_out = jnp.dot(normed, out_weight, preferred_element_type=jnp.float32).astype(jnp.bfloat16)
    return (features, latents_out)
```

```python
import functools

import jax
import jax.numpy as jnp
from jax import lax
from jax.experimental import pallas as pl
from jax.experimental.pallas import tpu as pltpu
from jax.sharding import PartitionSpec as P

HEADS = 16
BLOCK = 256
LANES = 128
PAD = 8
CORNER = 16
F32 = jnp.float32
BF16 = jnp.bfloat16
LOW = -1e30
LAG = 4
LOG2_E = 1.4426950408889634
MESH = pl.DeviceIdType.MESH


def dot(a, b):
    return jnp.dot(a, b, preferred_element_type=F32)


def core(
    tile_rows, tile_cols,
    top_ref, bottom_ref, left_ref, right_ref,
    main_hbm, patch_hbm, conv_hbm, kv_hbm,
    features_hbm, keys_hbm,
    main_ref, patch_ref, conv_ref, kv_ref,
    wide_ref, taps_ref, summed_ref, keys_ref, features_ref, load_sem, key_sem,
):
    loads = [
        pltpu.make_async_copy(source, target, load_sem.at[number])
        for number, (source, target) in enumerate(
            (
                (main_hbm, main_ref), (patch_hbm, patch_ref), (conv_hbm, conv_ref),
                (kv_hbm, kv_ref),
            )
        )
    ]
    for load in loads:
        load.start()
    tokens = tile_rows * tile_cols
    channels = patch_ref.shape[1]
    group = conv_ref.shape[1]
    rows_ext = tile_rows + 2
    col_ext = tile_cols + PAD
    same = (
        lax.broadcasted_iota(jnp.int32, (BLOCK, BLOCK), 0) // group
        == lax.broadcasted_iota(jnp.int32, (BLOCK, BLOCK), 1) // group
    )
    side_slot = lax.broadcasted_iota(jnp.int32, (rows_ext, PAD, BLOCK), 1)
    tall = (1, PAD, BLOCK)

    def border(values, upper, lower):
        return (
            jnp.broadcast_to(values[upper : upper + 1][:, None, :], tall),
            jnp.broadcast_to(values[:tile_rows][:, None, :], (tile_rows, PAD, BLOCK)),
            jnp.broadcast_to(values[lower : lower + 1][:, None, :], tall),
        )

    for load in loads[:3]:
        load.wait()
    for block in range(channels // BLOCK):
        lanes = slice(block * BLOCK, (block + 1) * BLOCK)
        patch = patch_ref[:, lanes]
        inner = jnp.concatenate(
            [dot(top_ref[...], patch), dot(main_ref[...], patch), dot(bottom_ref[...], patch)], 0
        )
        upper, middle, lower = border(
            dot(left_ref[...], patch), tile_rows + CORNER - 1, tile_rows + 2 * CORNER - 1
        )
        from_left = jnp.concatenate([middle, lower, upper], 0)
        upper, middle, lower = border(
            dot(right_ref[...], patch), tile_rows, tile_rows + CORNER
        )
        from_right = jnp.concatenate([upper, middle, lower], 0)
        side = jnp.where(side_slot == PAD - 1, from_left, from_right)
        full = jnp.concatenate(
            [inner.reshape(rows_ext, tile_cols, BLOCK), side], 1
        ).reshape(rows_ext * col_ext, BLOCK)
        for col_shift, amount in ((0, 1), (2, rows_ext * col_ext - 1)):
            moved = pltpu.roll(full, amount, 0).reshape(rows_ext, col_ext, BLOCK)
            moved = moved[:, :tile_cols].reshape(rows_ext * tile_cols, BLOCK)
            wide_ref[:, col_shift * BLOCK : (col_shift + 1) * BLOCK] = moved.astype(BF16)
        wide_ref[:, BLOCK : 2 * BLOCK] = inner.astype(BF16)
        for tap in range(9):
            small = conv_ref[tap, :, lanes]
            tiled = jnp.concatenate([small] * (BLOCK // group), 0)
            row_shift, col_shift = tap // 3, tap % 3
            taps_ref[row_shift, col_shift * BLOCK : (col_shift + 1) * BLOCK, :] = jnp.where(
                same, tiled, jnp.zeros_like(tiled)
            )
        total = wide_ref[tile_cols : tile_cols + tokens, BLOCK : 2 * BLOCK].astype(F32)
        for row_shift in range(3):
            first = row_shift * tile_cols
            total = total + dot(wide_ref[first : first + tokens, :], taps_ref[row_shift])
        summed_ref[:, lanes] = total

    chunk = 128
    inverse = 1.0 / channels

    def normalise(step, _):
        at = pl.ds(pl.multiple_of(step * chunk, chunk), chunk)
        values = summed_ref[at, :]
        centred = values - jnp.sum(values, axis=-1, keepdims=True) * inverse
        variance = jnp.sum(centred * centred, axis=-1, keepdims=True) * inverse
        features_ref[at, :] = (centred * lax.rsqrt(variance + 1e-05)).astype(BF16)
        return 0

    lax.fori_loop(0, tokens // chunk, normalise, 0)
    store = pltpu.make_async_copy(features_ref, features_hbm, load_sem.at[len(loads)])
    store.start()
    loads[3].wait()

    def stored(step):
        at = pl.ds(pl.multiple_of(step * BLOCK, BLOCK), BLOCK)
        return pltpu.make_async_copy(keys_ref.at[:, at], keys_hbm.at[:, at], key_sem.at[step])

    def project(step, _):
        at = pl.ds(pl.multiple_of(step * BLOCK, BLOCK), BLOCK)
        keys_ref[:, at] = dot(features_ref[...], kv_ref[:, at]).astype(BF16)
        stored(step).start()
        return 0

    lax.fori_loop(0, keys_ref.shape[1] // BLOCK, project, 0)

    def finish(step, _):
        stored(step).wait()
        return 0

    lax.fori_loop(0, keys_ref.shape[1] // BLOCK, finish, 0)
    store.wait()


def local_work(borders, pixels, patch_weight, conv_weight, kv_weight):
    tile_rows, tile_cols, patch_in = pixels.shape
    channels = patch_weight.shape[1]
    tokens = tile_rows * tile_cols
    rows_ext = tile_rows + 2
    vmem = pl.BlockSpec(memory_space=pltpu.VMEM)
    leave = pl.BlockSpec(memory_space=pl.ANY)
    loaded = (pixels.reshape(tokens, patch_in), patch_weight, conv_weight, kv_weight)
    return pl.pallas_call(
        functools.partial(core, tile_rows, tile_cols),
        out_shape=(
            jax.ShapeDtypeStruct((tokens, channels), BF16),
            jax.ShapeDtypeStruct((tokens, 2 * channels), BF16),
        ),
        in_specs=[vmem] * 4 + [leave] * len(loaded),
        out_specs=(leave, leave),
        scratch_shapes=[pltpu.VMEM(array.shape, BF16) for array in loaded]
        + [
            pltpu.VMEM((rows_ext * tile_cols, 3 * BLOCK), BF16),
            pltpu.VMEM((3, 3 * BLOCK, BLOCK), BF16),
            pltpu.VMEM((tokens, channels), F32),
            pltpu.VMEM((tokens, 2 * channels), BF16),
            pltpu.VMEM((tokens, channels), BF16),
            pltpu.SemaphoreType.DMA((len(loaded) + 1,)),
            pltpu.SemaphoreType.DMA((2 * channels // BLOCK,)),
        ],
        compiler_params=pltpu.CompilerParams(vmem_limit_bytes=60 * 1024 * 1024),
        name="local_work",
    )(*borders, *loaded)


def greet(
    pixels_ref, first_ref, last_ref, latent_hbm, weight_hbm,
    top_ref, bottom_ref, left_ref, right_ref, query_ref,
    latent_ref, weight_ref, send_sem, recv_sem, load_sem,
):
    loads = [
        pltpu.make_async_copy(latent_hbm.at[:, :, 0], latent_ref.at[0], load_sem.at[0]),
        pltpu.make_async_copy(latent_hbm.at[:, :, 1], latent_ref.at[1], load_sem.at[1]),
        pltpu.make_async_copy(weight_hbm, weight_ref, load_sem.at[2]),
    ]
    for load in loads:
        load.start()
    channels = query_ref.shape[1]
    tile_rows, tile_cols, _ = pixels_ref.shape
    row_count, col_count = lax.axis_size("rows"), lax.axis_size("cols")
    row, col = lax.axis_index("rows"), lax.axis_index("cols")
    low, high = slice(0, CORNER), slice(tile_cols - CORNER, tile_cols)
    column = slice(0, tile_rows)
    above = slice(tile_rows, tile_rows + CORNER)
    below = slice(tile_rows + CORNER, tile_rows + 2 * CORNER)
    end = tile_rows - 1
    moves = (
        (1, 0, pixels_ref.at[end], top_ref),
        (-1, 0, pixels_ref.at[0], bottom_ref),
        (0, 1, last_ref, left_ref.at[column]),
        (0, -1, first_ref, right_ref.at[column]),
        (1, 1, pixels_ref.at[end, high], left_ref.at[above]),
        (1, -1, pixels_ref.at[end, low], right_ref.at[above]),
        (-1, 1, pixels_ref.at[0, high], left_ref.at[below]),
        (-1, -1, pixels_ref.at[0, low], right_ref.at[below]),
    )

    def inside(down, across):
        ok = None
        for at, step, count in ((row, down, row_count), (col, across, col_count)):
            if step:
                here = at + step < count if step > 0 else at + step >= 0
                ok = here if ok is None else jnp.logical_and(ok, here)
        return ok

    barrier = pltpu.get_barrier_semaphore()
    for down, across, _, _ in moves:
        @pl.when(inside(down, across))
        def _(down=down, across=across):
            pl.semaphore_signal(
                barrier, inc=1, device_id=(row + down, col + across), device_id_type=MESH
            )
    tall = 1 + (row > 0).astype(jnp.int32) + (row < row_count - 1).astype(jnp.int32)
    wide = 1 + (col > 0).astype(jnp.int32) + (col < col_count - 1).astype(jnp.int32)
    pl.semaphore_wait(barrier, tall * wide - 1)

    def make(number):
        down, across, source, target = moves[number]
        return pltpu.make_async_remote_copy(
            src_ref=source, dst_ref=target,
            send_sem=send_sem.at[number], recv_sem=recv_sem.at[number],
            device_id=(row + down, col + across), device_id_type=MESH,
        )

    for number, (down, across, _, _) in enumerate(moves):
        @pl.when(inside(down, across))
        def _(number=number):
            make(number).start()
    for load in loads:
        load.wait()

    def ask(step, _):
        at = pl.ds(pl.multiple_of(step * BLOCK, BLOCK), BLOCK)
        asked = latent_ref[...].reshape(query_ref.shape[0], weight_ref.shape[0])
        query_ref[:, at] = dot(asked, weight_ref[:, at]).astype(BF16)
        return 0

    lax.fori_loop(0, channels // BLOCK, ask, 0)
    for number, (down, across, _, target) in enumerate(moves):
        @pl.when(inside(-down, -across))
        def _(number=number):
            make(number).wait_recv()

        @pl.when(jnp.logical_not(inside(-down, -across)))
        def _(target=target):
            target[...] = jnp.zeros(target.shape, BF16)
    for number, (down, across, _, _) in enumerate(moves):
        @pl.when(inside(down, across))
        def _(number=number):
            make(number).wait_send()


def borders_of(pixels, latents, query_weight):
    tile_rows, tile_cols, patch_in = pixels.shape
    vmem = pl.BlockSpec(memory_space=pltpu.VMEM)
    flat = jax.ShapeDtypeStruct((tile_cols, patch_in), BF16)
    tall = jax.ShapeDtypeStruct((tile_rows + 2 * CORNER, patch_in), BF16)
    latent_count, channels = latents.shape[0], query_weight.shape[1]
    row_count, col_count = lax.axis_size("rows"), lax.axis_size("cols")
    own = latent_count // (row_count * col_count)
    latents = latents.reshape(row_count, col_count // 2, 2, own, latents.shape[1])
    ordered = (2, row_count, col_count // 2, own, latents.shape[-1])
    leave = pl.BlockSpec(memory_space=pl.ANY)
    *borders, queries = pl.pallas_call(
        greet,
        out_shape=(flat, flat, tall, tall, jax.ShapeDtypeStruct((latent_count, channels), BF16)),
        in_specs=[leave, vmem, vmem, leave, leave],
        out_specs=(vmem,) * 5,
        scratch_shapes=[
            pltpu.VMEM(ordered, BF16),
            pltpu.VMEM(query_weight.shape, BF16),
            pltpu.SemaphoreType.DMA((8,)),
            pltpu.SemaphoreType.DMA((8,)),
            pltpu.SemaphoreType.DMA((3,)),
        ],
        compiler_params=pltpu.CompilerParams(
            collective_id=2, has_side_effects=True, vmem_limit_bytes=60 * 1024 * 1024
        ),
        name="borders",
    )(pixels, pixels[:, 0], pixels[:, -1], latents, query_weight)
    return borders, queries


def merge(items, gain):
    top = functools.reduce(jnp.maximum, [peak for _, peak, _ in items])
    number, total = 0.0, 0.0
    for values, peak, whole in items:
        share = jnp.exp2((peak - top) * gain)
        number = number + share * values
        total = total + share * whole
    return number, top, total


def attend(
    heads,
    tissue_ref, query_hbm, keys_hbm, weight_hbm,
    out_ref,
    query_ref, keys_ref, values_ref, weight_ref, bias_ref, mask_ref,
    score_ref, turned_ref, peak_ref,
    part_ref, twin_ref, row_num, row_stat, got_num, got_stat,
    build_num, build_stat, col_num, col_stat, end_num, end_stat,
    load_sem, pair_sem, twin_send, twin_recv, row_send, row_recv, col_send, col_recv,
):
    latent_count, channels = query_ref.shape
    tile_rows, tile_cols = tissue_ref.shape
    tokens = tile_rows * tile_cols
    pairs = heads // 2
    head_dim = channels // heads
    gain = LOG2_E * head_dim ** -0.5
    row_count, half = lax.axis_size("rows"), lax.axis_size("cols") // 2
    own = out_ref.shape[0]
    side_count = latent_count // 2
    per_row = side_count // row_count
    groups = col_num.shape[0]
    per_group = pairs // groups
    row, col = lax.axis_index("rows"), lax.axis_index("cols")
    side, slot = lax.rem(col, 2), lax.div(col, 2)
    twin = (row, slot * 2 + (1 - side))
    row_peers = [(lax.rem(row + step, row_count), col) for step in range(1, row_count)]
    col_peers = [(row, lax.rem(slot + step, half) * 2 + side) for step in range(1, half)]

    load = pltpu.make_async_copy(query_hbm, query_ref, load_sem.at[0])
    late = pltpu.make_async_copy(weight_hbm, weight_ref, load_sem.at[1])

    def fetch(pair, which):
        at = pl.ds(pl.multiple_of(which * channels + pair * LANES, LANES), LANES)
        target = (keys_ref, values_ref)[which]
        return pltpu.make_async_copy(keys_hbm.at[:, at], target.at[pair], pair_sem.at[which, pair])

    load.start()
    for pair in range(pairs):
        fetch(pair, 0).start()
        fetch(pair, 1).start()
    late.start()
    barrier = pltpu.get_barrier_semaphore()
    for peer in [twin] + row_peers + col_peers:
        pl.semaphore_signal(barrier, inc=1, device_id=peer, device_id_type=MESH)

    mask_ref[...] = jnp.zeros_like(mask_ref)
    mask_ref[:, :tile_cols] = jnp.where(tissue_ref[...] > 0, 0.0, LOW)
    spot = lax.broadcasted_iota(jnp.int32, (tile_cols, LANES), 0)
    spot = spot == lax.broadcasted_iota(jnp.int32, (tile_cols, LANES), 1)
    for tile_row in range(tile_rows):
        line = jnp.broadcast_to(mask_ref[tile_row : tile_row + 1, :], (tile_cols, LANES))
        bias_ref[tile_row * tile_cols : (tile_row + 1) * tile_cols, :] = jnp.where(
            spot, line, 0.0
        ).astype(BF16)
    turned_ref[:, head_dim:, :] = jnp.ones((2, CORNER, tokens), BF16)
    build_num[...] = jnp.zeros_like(build_num)
    build_stat[...] = jnp.zeros_like(build_stat)

    lane = lax.broadcasted_iota(jnp.int32, (1, LANES), 1)
    low = lane < head_dim
    query_low = lax.broadcasted_iota(jnp.int32, (latent_count, LANES), 1) < head_dim
    ones = jnp.ones((latent_count, LANES), BF16)
    chunk = tokens // 2
    fresh = jnp.full((8, latent_count), -3e38, F32)

    def asked(pair, which):
        queries = query_ref[:, pl.ds(pl.multiple_of(pair * LANES, LANES), LANES)]
        mine = query_low if which == 0 else jnp.logical_not(query_low)
        return jnp.concatenate([jnp.where(mine, queries, jnp.zeros_like(queries)), ones], 1)

    def score(pair, part, queries, which, peak):
        at = slice(part * chunk, (part + 1) * chunk)
        keys = jnp.concatenate([keys_ref[pair, at, :], bias_ref[at, :]], 1)
        scores = lax.dot_general(
            keys, queries, (((1,), (1,)), ((), ())), preferred_element_type=F32
        )
        score_ref[which, at, :] = scores
        return jnp.maximum(peak, jnp.max(scores.reshape(chunk // 8, 8, latent_count), 0))

    def weigh(part, which, peak, total):
        at = slice(part * chunk, (part + 1) * chunk)
        weights = jnp.exp2((score_ref[which, at, :] - peak) * gain).astype(BF16)
        return total + dot(turned_ref[which, :, at], weights)

    def remote(source, target, send, recv, peer):
        return pltpu.make_async_remote_copy(
            src_ref=source, dst_ref=target, send_sem=send, recv_sem=recv,
            device_id=peer, device_id_type=MESH,
        )

    def to_twin(pair):
        return remote(
            part_ref.at[pair, 1 - side], twin_ref.at[pair],
            twin_send.at[pair], twin_recv.at[pair], twin,
        )

    def to_row(pair, step):
        target = lax.rem(row + step, row_count)
        return [
            remote(
                source.at[pair, target], landing.at[pair, step - 1],
                row_send.at[pair, step - 1, kind], row_recv.at[pair, step - 1, kind],
                row_peers[step - 1],
            )
            for kind, (source, landing) in enumerate(((row_num, got_num), (row_stat, got_stat)))
        ]

    def to_col(group, step):
        target = lax.rem(slot + step, half)
        return [
            remote(
                source.at[group, target], landing.at[group, step - 1],
                col_send.at[group, step - 1, kind], col_recv.at[group, step - 1, kind],
                col_peers[step - 1],
            )
            for kind, (source, landing) in enumerate(((col_num, end_num), (col_stat, end_stat)))
        ]

    first_line = lax.broadcasted_iota(jnp.int32, (8, LANES), 0) == 0
    extent = head_dim + 8

    def with_twin(pair):
        to_twin(pair).wait_recv()
        merged = []
        for which in range(2):
            base = which * extent
            items = []
            for values in (part_ref.at[pair, side], twin_ref.at[pair]):
                stat = values[base + head_dim : base + extent, :]
                items.append((values[base : base + head_dim, :], stat[0:1], stat[1:2]))
            merged.append(merge(items, gain))
        for target in range(row_count):
            tile = target * per_row // LANES
            at = slice(tile * LANES, (tile + 1) * LANES)

            def joined(one, two, target=target, at=at):
                one, two = one[:, at], two[:, at]
                if target * per_row % LANES == 0:
                    return jnp.where(low, one, pltpu.roll(two, per_row, 1))
                return jnp.where(low, pltpu.roll(one, per_row, 1), two)

            number, peak, total = [joined(one, two) for one, two in zip(*merged)]
            row_num[pair, target] = number.astype(BF16)
            row_stat[pair, target] = jnp.where(first_line, peak, total)
        for step in range(1, row_count):
            for copy in to_row(pair, step):
                copy.start()

    def with_rows(pair):
        for step in range(1, row_count):
            for copy in to_row(pair, step):
                copy.wait_recv()
        items = []
        for values, stat in [(row_num[pair, row], row_stat[pair, row])] + [
            (got_num[pair, step], got_stat[pair, step]) for step in range(row_count - 1)
        ]:
            items.append((values.astype(F32), stat[0:1], stat[1:2]))
        number, peak, total = merge(items, gain)
        stat = jnp.where(first_line, peak, total)
        place = lax.rem(pair, per_group) * (2 * own)
        for target in range(half):
            for which in range(2):
                begin = place + which * own
                source = which * head_dim + target * own
                shift = lax.rem(begin - source + LANES, LANES)
                here = jnp.logical_and(lane >= begin, lane < begin + own)
                build_num[target] = jnp.where(
                    here, pltpu.roll(number, shift, 1), build_num[target]
                )
                build_stat[target] = jnp.where(
                    here, pltpu.roll(stat, shift, 1), build_stat[target]
                )

        @pl.when(lax.rem(pair, per_group) == per_group - 1)
        def _():
            group = lax.div(pair, per_group)
            col_num[group] = build_num[...].astype(BF16)
            col_stat[group] = build_stat[...]
            for step in range(1, half):
                for copy in to_col(group, step):
                    copy.start()

    load.wait()
    fetch(0, 0).wait()
    peak = fresh
    queries = asked(0, 0)
    for part in range(2):
        peak = score(0, part, queries, 0, peak)
    peak_ref[...] = peak
    pl.semaphore_wait(barrier, 1 + len(row_peers) + len(col_peers))

    def step(pair, _):
        @pl.when(pair < pairs - 1)
        def _():
            fetch(pair + 1, 0).wait()

        fetch(pair, 1).wait()
        turned = values_ref[pair].T
        for which in range(2):
            turned_ref[which, :head_dim, :] = turned[which * head_dim : (which + 1) * head_dim]
        current = peak_ref[...]
        for which in range(2):
            following = pair if which == 0 else jnp.minimum(pair + 1, pairs - 1)
            queries = asked(following, 1 - which)
            top = jnp.max(current, 0, keepdims=True)
            total = jnp.zeros((head_dim + CORNER, latent_count), F32)
            peak = fresh
            for part in range(2):
                peak = score(following, part, queries, 1 - which, peak)
                total = weigh(part, which, top, total)
            line = lax.broadcasted_iota(jnp.int32, (8, latent_count), 0) == 0
            stat = jnp.where(line, top, total[head_dim : head_dim + 8])
            for half_at in range(2):
                at = slice(half_at * side_count, (half_at + 1) * side_count)
                part_ref[pair, half_at, which * extent : which * extent + head_dim, :] = total[
                    :head_dim, at
                ]
                part_ref[
                    pair, half_at, which * extent + head_dim : (which + 1) * extent, :
                ] = stat[:, at]
            current = peak
        peak_ref[...] = current
        to_twin(pair).start()

        @pl.when(pair >= 1)
        def _():
            with_twin(pair - 1)

        @pl.when(pair >= LAG)
        def _():
            with_rows(pair - LAG)

        return 0

    lax.fori_loop(0, pairs, step, 0)
    for pair in range(pairs - LAG, pairs - 2):
        with_rows(pair)
    with_twin(pairs - 1)
    for pair in range(pairs - 2, pairs):
        with_rows(pair)

    pieces = []
    for group in range(groups):
        items = []
        for step in range(1, half):
            for copy in to_col(group, step):
                copy.wait_recv()
        for values, stat in [(col_num[group, slot], col_stat[group, slot])] + [
            (end_num[group, step], end_stat[group, step]) for step in range(half - 1)
        ]:
            items.append((values.astype(F32), stat[0:1], stat[1:2]))
        number, _, total = merge(items, gain)
        tile = (number / total).T
        for place in range(per_group):
            base = place * 2 * own
            pieces.append(
                jnp.concatenate([tile[base : base + own], tile[base + own : base + 2 * own]], 1)
            )
    attended = jnp.concatenate(pieces, 1)
    mean = jnp.sum(attended * attended, axis=-1, keepdims=True) * (1.0 / channels)
    normed = (attended * lax.rsqrt(mean + 1e-06)).astype(BF16)
    late.wait()
    out_ref[...] = dot(normed, weight_ref[...]).astype(BF16)

    def drain(pair, _):
        to_twin(pair).wait_send()
        for step in range(1, row_count):
            for copy in to_row(pair, step):
                copy.wait_send()
        return 0

    lax.fori_loop(0, pairs, drain, 0)
    for group in range(groups):
        for step in range(1, half):
            for copy in to_col(group, step):
                copy.wait_send()


def attention(tissue, queries, keys, out_weight):
    row_count, col_count = lax.axis_size("rows"), lax.axis_size("cols")
    half = col_count // 2
    latent_count, channels = queries.shape
    tokens = tissue.shape[0] * tissue.shape[1]
    own = latent_count // (row_count * col_count)
    pairs = HEADS // 2
    head_dim = channels // HEADS
    groups = max(1, pairs * 2 * own // LANES)
    side_count = latent_count // 2
    leave = pl.BlockSpec(memory_space=pl.ANY)

    def blocks(*extent):
        return [
            pltpu.VMEM(extent + (head_dim, LANES), BF16), pltpu.VMEM(extent + (8, LANES), F32)
        ]

    def sems(*extent):
        return [pltpu.SemaphoreType.DMA(extent)] * 2

    return pl.pallas_call(
        functools.partial(attend, HEADS),
        out_shape=jax.ShapeDtypeStruct((own, out_weight.shape[1]), BF16),
        in_specs=[pl.BlockSpec(memory_space=pltpu.VMEM)] + [leave] * 3,
        out_specs=pl.BlockSpec(memory_space=pltpu.VMEM),
        scratch_shapes=[
            pltpu.VMEM(queries.shape, BF16),
            pltpu.VMEM((pairs, tokens, LANES), BF16),
            pltpu.VMEM((pairs, tokens, LANES), BF16),
            pltpu.VMEM(out_weight.shape, BF16),
            pltpu.VMEM((tokens, LANES), BF16),
            pltpu.VMEM((tissue.shape[0], LANES), F32),
            pltpu.VMEM((2, tokens, latent_count), F32),
            pltpu.VMEM((2, head_dim + CORNER, tokens), BF16),
            pltpu.VMEM((8, latent_count), F32),
            pltpu.VMEM((pairs, 2, 2 * (head_dim + 8), side_count), F32),
            pltpu.VMEM((pairs, 2 * (head_dim + 8), side_count), F32),
        ]
        + blocks(pairs, row_count)
        + blocks(pairs, row_count - 1)
        + [pltpu.VMEM((half, head_dim, LANES), F32), pltpu.VMEM((half, 8, LANES), F32)]
        + blocks(groups, half)
        + blocks(groups, half - 1)
        + [pltpu.SemaphoreType.DMA((2,)), pltpu.SemaphoreType.DMA((2, pairs))]
        + sems(pairs)
        + sems(pairs, row_count - 1, 2)
        + sems(groups, half - 1, 2),
        compiler_params=pltpu.CompilerParams(
            collective_id=1, has_side_effects=True, vmem_limit_bytes=60 * 1024 * 1024
        ),
        name="attention",
    )(tissue, queries, keys, out_weight)


def shards(pixels, tissue, patch_weight, conv_weight, kv_weight, query_weight, out_weight, latents):
    tile_rows, tile_cols, _ = pixels.shape
    channels = patch_weight.shape[1]
    borders, queries = borders_of(pixels, latents, query_weight)
    features, keys = local_work(borders, pixels, patch_weight, conv_weight, kv_weight)
    latents_out = attention(tissue, queries, keys, out_weight)
    return (features.reshape(tile_rows, tile_cols, channels), latents_out)


def solution(mesh):
    return jax.shard_map(
        shards,
        mesh=mesh,
        in_specs=(P("rows", "cols", None), P("rows", "cols"), P(), P(), P(), P(), P(), P()),
        out_specs=(P("rows", "cols", None), P(("rows", "cols"), None)),
        check_vma=False,
    )
```

```python
import functools

import jax
import jax.numpy as jnp
from jax import lax
from jax.experimental import pallas as pl
from jax.experimental.pallas import tpu as pltpu
from jax.sharding import PartitionSpec as P

HEADS = 16
BLOCK = 256
LANES = 128
PAD = 8
CORNER = 16
LAG = 4
LOG2_E = 1.4426950408889634
F32 = jnp.float32
BF16 = jnp.bfloat16
LOW = -1e30
MESH = pl.DeviceIdType.MESH


def dot(a, b):
    return jnp.dot(a, b, preferred_element_type=F32)


def merge(items, gain):
    top = functools.reduce(jnp.maximum, [peak for _, peak, _ in items])
    number, total = 0.0, 0.0
    for values, peak, whole in items:
        share = jnp.exp2((peak - top) * gain)
        number = number + share * values
        total = total + share * whole
    return number, top, total


def slide(
    heads,
    pixels_hbm, tissue_hbm, patch_hbm, conv_hbm, kv_hbm, ask_hbm, latent_hbm,
    features_hbm, normed_ref,
    pixels_ref, tissue_ref, patch_ref, conv_ref, kv_ref, ask_ref, latent_ref,
    border_ref, side_ref, embedded_ref, wide_ref, taps_ref, summed_ref, features_ref,
    query_ref, keys_ref, turned_ref, bias_ref, mask_ref, score_ref, peak_ref,
    part_ref, twin_ref, row_num, row_stat, got_num, got_stat,
    build_num, build_stat, col_num, col_stat, end_num, end_stat,
    load_sem, halo_send, halo_recv,
    twin_send, twin_recv, row_send, row_recv, col_send, col_recv,
):
    tile_rows, tile_cols, patch_in = pixels_ref.shape
    tokens = tile_rows * tile_cols
    latent_count, channels = query_ref.shape
    pairs = heads // 2
    head_dim = channels // heads
    gain = LOG2_E * head_dim ** -0.5
    group_width = conv_ref.shape[1]
    row_count, col_count = lax.axis_size("rows"), lax.axis_size("cols")
    half = col_count // 2
    own = normed_ref.shape[0]
    side_count = latent_count // 2
    per_row = side_count // row_count
    groups = col_num.shape[0]
    per_group = pairs // groups
    row, col = lax.axis_index("rows"), lax.axis_index("cols")
    side, slot = lax.rem(col, 2), lax.div(col, 2)
    twin = (row, slot * 2 + (1 - side))
    row_peers = [(lax.rem(row + step, row_count), col) for step in range(1, row_count)]
    col_peers = [(row, lax.rem(slot + step, half) * 2 + side) for step in range(1, half)]

    loads = [
        pltpu.make_async_copy(source, target, load_sem.at[number])
        for number, (source, target) in enumerate(
            (
                (pixels_hbm, pixels_ref), (patch_hbm, patch_ref),
                (latent_hbm.at[:, :, 0], latent_ref.at[0]),
                (latent_hbm.at[:, :, 1], latent_ref.at[1]),
                (ask_hbm, ask_ref), (conv_hbm, conv_ref), (tissue_hbm, tissue_ref),
                (kv_hbm, kv_ref),
            )
        )
    ]
    for load in loads:
        load.start()

    low_cols, high_cols = slice(0, CORNER), slice(tile_cols - CORNER, tile_cols)
    top, bottom = 0, tile_cols
    left = 2 * tile_cols
    right = left + tile_rows + 2 * CORNER
    end = tile_rows - 1

    def landing(start, extent):
        return border_ref.at[start : start + extent]

    moves = (
        (1, 0, pixels_hbm.at[end], landing(top, tile_cols)),
        (-1, 0, pixels_hbm.at[0], landing(bottom, tile_cols)),
        (1, 1, pixels_hbm.at[end, high_cols], landing(left + tile_rows, CORNER)),
        (1, -1, pixels_hbm.at[end, low_cols], landing(right + tile_rows, CORNER)),
        (-1, 1, pixels_hbm.at[0, high_cols], landing(left + tile_rows + CORNER, CORNER)),
        (-1, -1, pixels_hbm.at[0, low_cols], landing(right + tile_rows + CORNER, CORNER)),
        (0, 1, side_ref.at[1], landing(left, tile_rows)),
        (0, -1, side_ref.at[0], landing(right, tile_rows)),
    )

    def inside(down, across):
        ok = None
        for at, step, count in ((row, down, row_count), (col, across, col_count)):
            if step:
                here = at + step < count if step > 0 else at + step >= 0
                ok = here if ok is None else jnp.logical_and(ok, here)
        return ok

    def shift(number):
        down, across, source, target = moves[number]
        return pltpu.make_async_remote_copy(
            src_ref=source, dst_ref=target,
            send_sem=halo_send.at[number], recv_sem=halo_recv.at[number],
            device_id=(row + down, col + across), device_id_type=MESH,
        )

    barrier = pltpu.get_barrier_semaphore()
    for down, across, _, _ in moves:
        @pl.when(inside(down, across))
        def _(down=down, across=across):
            pl.semaphore_signal(
                barrier, inc=1, device_id=(row + down, col + across), device_id_type=MESH
            )
    for peer in [twin] + row_peers + col_peers:
        pl.semaphore_signal(barrier, inc=1, device_id=peer, device_id_type=MESH)
    tall = 1 + (row > 0).astype(jnp.int32) + (row < row_count - 1).astype(jnp.int32)
    broad = 1 + (col > 0).astype(jnp.int32) + (col < col_count - 1).astype(jnp.int32)
    turned_ref[:, :, head_dim:, :] = jnp.ones((pairs, 2, CORNER, tokens), BF16)
    build_num[...] = jnp.zeros_like(build_num)
    build_stat[...] = jnp.zeros_like(build_stat)
    pl.semaphore_wait(barrier, tall * broad - 1 + 1 + len(row_peers) + len(col_peers))
    for number in range(6):
        @pl.when(inside(*moves[number][:2]))
        def _(number=number):
            shift(number).start()
    loads[0].wait()
    side_ref[0] = pixels_ref[:, 0, :]
    side_ref[1] = pixels_ref[:, tile_cols - 1, :]
    for number in range(6, 8):
        @pl.when(inside(*moves[number][:2]))
        def _(number=number):
            shift(number).start()
    loads[1].wait()

    def embed(step, _):
        at = pl.ds(pl.multiple_of(step * BLOCK, BLOCK), BLOCK)
        pixels = pixels_ref[...].reshape(tokens, patch_in)
        embedded_ref[:, at] = dot(pixels, patch_ref[:, at])
        return 0

    lax.fori_loop(0, channels // BLOCK, embed, 0)
    for load in loads[2:5]:
        load.wait()

    def ask(step, _):
        at = pl.ds(pl.multiple_of(step * BLOCK, BLOCK), BLOCK)
        latents = latent_ref[...].reshape(latent_count, ask_ref.shape[0])
        query_ref[:, at] = dot(latents, ask_ref[:, at]).astype(BF16)
        return 0

    lax.fori_loop(0, channels // BLOCK, ask, 0)
    for load in loads[5:7]:
        load.wait()
    mask_ref[...] = jnp.zeros_like(mask_ref)
    mask_ref[:, :tile_cols] = jnp.where(tissue_ref[...] > 0, 0.0, LOW)
    spot = lax.broadcasted_iota(jnp.int32, (tile_cols, LANES), 0)
    spot = spot == lax.broadcasted_iota(jnp.int32, (tile_cols, LANES), 1)
    for tile_row in range(tile_rows):
        line = jnp.broadcast_to(mask_ref[tile_row : tile_row + 1, :], (tile_cols, LANES))
        bias_ref[tile_row * tile_cols : (tile_row + 1) * tile_cols, :] = jnp.where(
            spot, line, 0.0
        ).astype(BF16)
    for number, (down, across, _, target) in enumerate(moves):
        @pl.when(inside(-down, -across))
        def _(number=number):
            shift(number).wait_recv()

        @pl.when(jnp.logical_not(inside(-down, -across)))
        def _(target=target):
            target[...] = jnp.zeros(target.shape, BF16)

    rows_ext = tile_rows + 2
    col_ext = tile_cols + PAD
    same = (
        lax.broadcasted_iota(jnp.int32, (BLOCK, BLOCK), 0) // group_width
        == lax.broadcasted_iota(jnp.int32, (BLOCK, BLOCK), 1) // group_width
    )
    side_slot = lax.broadcasted_iota(jnp.int32, (rows_ext, PAD, BLOCK), 1)
    thin = (1, PAD, BLOCK)

    def border(values, upper, lower):
        return (
            jnp.broadcast_to(values[upper : upper + 1][:, None, :], thin),
            jnp.broadcast_to(values[:tile_rows][:, None, :], (tile_rows, PAD, BLOCK)),
            jnp.broadcast_to(values[lower : lower + 1][:, None, :], thin),
        )

    for block in range(channels // BLOCK):
        lanes = slice(block * BLOCK, (block + 1) * BLOCK)
        edges = dot(border_ref[...], patch_ref[:, lanes])
        inner = jnp.concatenate(
            [edges[top:bottom], embedded_ref[:, lanes], edges[bottom:left]], 0
        )
        upper, middle, lower = border(
            edges[left:right], tile_rows + CORNER - 1, tile_rows + 2 * CORNER - 1
        )
        from_left = jnp.concatenate([middle, lower, upper], 0)
        upper, middle, lower = border(edges[right:], tile_rows, tile_rows + CORNER)
        from_right = jnp.concatenate([upper, middle, lower], 0)
        flank = jnp.where(side_slot == PAD - 1, from_left, from_right)
        full = jnp.concatenate(
            [inner.reshape(rows_ext, tile_cols, BLOCK), flank], 1
        ).reshape(rows_ext * col_ext, BLOCK)
        for col_shift, amount in ((0, 1), (2, rows_ext * col_ext - 1)):
            moved = pltpu.roll(full, amount, 0).reshape(rows_ext, col_ext, BLOCK)
            moved = moved[:, :tile_cols].reshape(rows_ext * tile_cols, BLOCK)
            wide_ref[:, col_shift * BLOCK : (col_shift + 1) * BLOCK] = moved.astype(BF16)
        wide_ref[:, BLOCK : 2 * BLOCK] = inner.astype(BF16)
        for tap in range(9):
            small = conv_ref[tap, :, lanes]
            tiled = jnp.concatenate([small] * (BLOCK // group_width), 0)
            row_shift, col_shift = tap // 3, tap % 3
            taps_ref[row_shift, col_shift * BLOCK : (col_shift + 1) * BLOCK, :] = jnp.where(
                same, tiled, jnp.zeros_like(tiled)
            )
        total = wide_ref[tile_cols : tile_cols + tokens, BLOCK : 2 * BLOCK].astype(F32)
        for row_shift in range(3):
            first = row_shift * tile_cols
            total = total + dot(wide_ref[first : first + tokens, :], taps_ref[row_shift])
        summed_ref[:, lanes] = total

    piece = 128
    inverse = 1.0 / channels

    def normalise(step, _):
        at = pl.ds(pl.multiple_of(step * piece, piece), piece)
        values = summed_ref[at, :]
        centred = values - jnp.sum(values, axis=-1, keepdims=True) * inverse
        variance = jnp.sum(centred * centred, axis=-1, keepdims=True) * inverse
        features_ref[at, :] = (centred * lax.rsqrt(variance + 1e-05)).astype(BF16)
        return 0

    lax.fori_loop(0, tokens // piece, normalise, 0)
    store = pltpu.make_async_copy(features_ref, features_hbm, load_sem.at[len(loads)])
    store.start()
    loads[7].wait()

    def project(step, _):
        for base in (0, channels):
            at = pl.ds(pl.multiple_of(base + step * BLOCK, BLOCK), BLOCK)
            found = dot(features_ref[...], kv_ref[:, at]).astype(BF16)
            for inner in range(BLOCK // LANES):
                pair = step * (BLOCK // LANES) + inner
                mine = found[:, inner * LANES : (inner + 1) * LANES]
                if base == 0:
                    keys_ref[pair] = mine
                else:
                    mine = mine.T
                    for which in range(2):
                        turned_ref[pair, which, :head_dim, :] = mine[
                            which * head_dim : (which + 1) * head_dim
                        ]
        return 0

    lax.fori_loop(0, channels // BLOCK, project, 0)

    lane = lax.broadcasted_iota(jnp.int32, (1, LANES), 1)
    low = lane < head_dim
    query_low = lax.broadcasted_iota(jnp.int32, (latent_count, LANES), 1) < head_dim
    ones = jnp.ones((latent_count, LANES), BF16)
    chunk = tokens // 2
    fresh = jnp.full((8, latent_count), -3e38, F32)

    def asked(pair, which):
        queries = query_ref[:, pl.ds(pl.multiple_of(pair * LANES, LANES), LANES)]
        mine = query_low if which == 0 else jnp.logical_not(query_low)
        return jnp.concatenate([jnp.where(mine, queries, jnp.zeros_like(queries)), ones], 1)

    def score(pair, part, queries, which, peak):
        at = slice(part * chunk, (part + 1) * chunk)
        keys = jnp.concatenate([keys_ref[pair, at, :], bias_ref[at, :]], 1)
        scores = lax.dot_general(
            keys, queries, (((1,), (1,)), ((), ())), preferred_element_type=F32
        )
        score_ref[which, at, :] = scores
        return jnp.maximum(peak, jnp.max(scores.reshape(chunk // 8, 8, latent_count), 0))

    def weigh(pair, part, which, peak, total):
        at = slice(part * chunk, (part + 1) * chunk)
        weights = jnp.exp2((score_ref[which, at, :] - peak) * gain).astype(BF16)
        return total + dot(turned_ref[pair, which, :, at], weights)

    def remote(source, target, send, recv, peer):
        return pltpu.make_async_remote_copy(
            src_ref=source, dst_ref=target, send_sem=send, recv_sem=recv,
            device_id=peer, device_id_type=MESH,
        )

    def to_twin(pair):
        return remote(
            part_ref.at[pair, 1 - side], twin_ref.at[pair],
            twin_send.at[pair], twin_recv.at[pair], twin,
        )

    def to_row(pair, step):
        target = lax.rem(row + step, row_count)
        return [
            remote(
                source.at[pair, target], landing.at[pair, step - 1],
                row_send.at[pair, step - 1, kind], row_recv.at[pair, step - 1, kind],
                row_peers[step - 1],
            )
            for kind, (source, landing) in enumerate(((row_num, got_num), (row_stat, got_stat)))
        ]

    def to_col(group, step):
        target = lax.rem(slot + step, half)
        return [
            remote(
                source.at[group, target], landing.at[group, step - 1],
                col_send.at[group, step - 1, kind], col_recv.at[group, step - 1, kind],
                col_peers[step - 1],
            )
            for kind, (source, landing) in enumerate(((col_num, end_num), (col_stat, end_stat)))
        ]

    first_line = lax.broadcasted_iota(jnp.int32, (8, LANES), 0) == 0
    extent = head_dim + 8

    def with_twin(pair):
        to_twin(pair).wait_recv()
        merged = []
        for which in range(2):
            base = which * extent
            items = []
            for values in (part_ref.at[pair, side], twin_ref.at[pair]):
                stat = values[base + head_dim : base + extent, :]
                items.append((values[base : base + head_dim, :], stat[0:1], stat[1:2]))
            merged.append(merge(items, gain))
        for target in range(row_count):
            tile = target * per_row // LANES
            at = slice(tile * LANES, (tile + 1) * LANES)

            def joined(one, two, target=target, at=at):
                one, two = one[:, at], two[:, at]
                if target * per_row % LANES == 0:
                    return jnp.where(low, one, pltpu.roll(two, per_row, 1))
                return jnp.where(low, pltpu.roll(one, per_row, 1), two)

            number, peak, total = [joined(one, two) for one, two in zip(*merged)]
            row_num[pair, target] = number.astype(BF16)
            row_stat[pair, target] = jnp.where(first_line, peak, total)
        for step in range(1, row_count):
            for copy in to_row(pair, step):
                copy.start()

    def with_rows(pair):
        for step in range(1, row_count):
            for copy in to_row(pair, step):
                copy.wait_recv()
        items = []
        for values, stat in [(row_num[pair, row], row_stat[pair, row])] + [
            (got_num[pair, step], got_stat[pair, step]) for step in range(row_count - 1)
        ]:
            items.append((values.astype(F32), stat[0:1], stat[1:2]))
        number, peak, total = merge(items, gain)
        stat = jnp.where(first_line, peak, total)
        place = lax.rem(pair, per_group) * (2 * own)
        for target in range(half):
            for which in range(2):
                begin = place + which * own
                source = which * head_dim + target * own
                shift = lax.rem(begin - source + LANES, LANES)
                here = jnp.logical_and(lane >= begin, lane < begin + own)
                build_num[target] = jnp.where(
                    here, pltpu.roll(number, shift, 1), build_num[target]
                )
                build_stat[target] = jnp.where(
                    here, pltpu.roll(stat, shift, 1), build_stat[target]
                )

        @pl.when(lax.rem(pair, per_group) == per_group - 1)
        def _():
            group = lax.div(pair, per_group)
            col_num[group] = build_num[...].astype(BF16)
            col_stat[group] = build_stat[...]
            for step in range(1, half):
                for copy in to_col(group, step):
                    copy.start()

    peak = fresh
    queries = asked(0, 0)
    for part in range(2):
        peak = score(0, part, queries, 0, peak)
    peak_ref[...] = peak

    def step(pair, _):
        current = peak_ref[...]
        for which in range(2):
            following = pair if which == 0 else jnp.minimum(pair + 1, pairs - 1)
            queries = asked(following, 1 - which)
            top = jnp.max(current, 0, keepdims=True)
            total = jnp.zeros((head_dim + CORNER, latent_count), F32)
            peak = fresh
            for part in range(2):
                peak = score(following, part, queries, 1 - which, peak)
                total = weigh(pair, part, which, top, total)
            line = lax.broadcasted_iota(jnp.int32, (8, latent_count), 0) == 0
            stat = jnp.where(line, top, total[head_dim : head_dim + 8])
            for half_at in range(2):
                at = slice(half_at * side_count, (half_at + 1) * side_count)
                part_ref[pair, half_at, which * extent : which * extent + head_dim, :] = total[
                    :head_dim, at
                ]
                part_ref[
                    pair, half_at, which * extent + head_dim : (which + 1) * extent, :
                ] = stat[:, at]
            current = peak
        peak_ref[...] = current
        to_twin(pair).start()

        @pl.when(pair >= 1)
        def _():
            with_twin(pair - 1)

        @pl.when(pair >= LAG)
        def _():
            with_rows(pair - LAG)

        return 0

    lax.fori_loop(0, pairs, step, 0)
    for pair in range(pairs - LAG, pairs - 2):
        with_rows(pair)
    with_twin(pairs - 1)
    for pair in range(pairs - 2, pairs):
        with_rows(pair)

    pieces = []
    for group in range(groups):
        items = []
        for step in range(1, half):
            for copy in to_col(group, step):
                copy.wait_recv()
        for values, stat in [(col_num[group, slot], col_stat[group, slot])] + [
            (end_num[group, step], end_stat[group, step]) for step in range(half - 1)
        ]:
            items.append((values.astype(F32), stat[0:1], stat[1:2]))
        number, _, total = merge(items, gain)
        tile = (number / total).T
        for place in range(per_group):
            base = place * 2 * own
            pieces.append(
                jnp.concatenate([tile[base : base + own], tile[base + own : base + 2 * own]], 1)
            )
    attended = jnp.concatenate(pieces, 1)
    mean = jnp.sum(attended * attended, axis=-1, keepdims=True) * (1.0 / channels)
    normed = (attended * lax.rsqrt(mean + 1e-06)).astype(BF16)
    normed_ref[...] = normed

    def drain(pair, _):
        to_twin(pair).wait_send()
        for step in range(1, row_count):
            for copy in to_row(pair, step):
                copy.wait_send()
        return 0

    lax.fori_loop(0, pairs, drain, 0)
    for group in range(groups):
        for step in range(1, half):
            for copy in to_col(group, step):
                copy.wait_send()
    store.wait()
    for number, (down, across, _, _) in enumerate(moves):
        @pl.when(inside(down, across))
        def _(number=number):
            shift(number).wait_send()


def embed_attend(pixels, tissue, patch_weight, conv_weight, kv_weight, query_weight, latents):
    tile_rows, tile_cols, patch_in = pixels.shape
    tokens = tile_rows * tile_cols
    row_count, col_count = lax.axis_size("rows"), lax.axis_size("cols")
    half = col_count // 2
    latent_count = latents.shape[0]
    channels = query_weight.shape[1]
    own = latent_count // (row_count * col_count)
    pairs = HEADS // 2
    head_dim = channels // HEADS
    groups = max(1, pairs * 2 * own // LANES)
    side_count = latent_count // 2
    leave = pl.BlockSpec(memory_space=pl.ANY)
    latents = latents.reshape(row_count, half, 2, own, latents.shape[1])
    borders = 2 * tile_cols + 2 * (tile_rows + 2 * CORNER)

    def like(array):
        return pltpu.VMEM(array.shape, array.dtype)

    def blocks(*extent):
        return [
            pltpu.VMEM(extent + (head_dim, LANES), BF16), pltpu.VMEM(extent + (8, LANES), F32)
        ]

    def sems(*extent):
        return [pltpu.SemaphoreType.DMA(extent)] * 2

    return pl.pallas_call(
        functools.partial(slide, HEADS),
        out_shape=(
            jax.ShapeDtypeStruct((tokens, channels), BF16),
            jax.ShapeDtypeStruct((own, channels), BF16),
        ),
        in_specs=[leave] * 7,
        out_specs=(leave, pl.BlockSpec(memory_space=pltpu.VMEM)),
        scratch_shapes=[
            like(array)
            for array in (pixels, tissue, patch_weight, conv_weight, kv_weight, query_weight)
        ]
        + [
            pltpu.VMEM((2, row_count, half, own, latents.shape[-1]), BF16),
            pltpu.VMEM((borders, patch_in), BF16),
            pltpu.VMEM((2, tile_rows, patch_in), BF16),
            pltpu.VMEM((tokens, channels), F32),
            pltpu.VMEM(((tile_rows + 2) * tile_cols, 3 * BLOCK), BF16),
            pltpu.VMEM((3, 3 * BLOCK, BLOCK), BF16),
            pltpu.VMEM((tokens, channels), F32),
            pltpu.VMEM((tokens, channels), BF16),
            pltpu.VMEM((latent_count, channels), BF16),
            pltpu.VMEM((pairs, tokens, LANES), BF16),
            pltpu.VMEM((pairs, 2, head_dim + CORNER, tokens), BF16),
            pltpu.VMEM((tokens, LANES), BF16),
            pltpu.VMEM((tile_rows, LANES), F32),
            pltpu.VMEM((2, tokens, latent_count), F32),
            pltpu.VMEM((8, latent_count), F32),
            pltpu.VMEM((pairs, 2, 2 * (head_dim + 8), side_count), F32),
            pltpu.VMEM((pairs, 2 * (head_dim + 8), side_count), F32),
        ]
        + blocks(pairs, row_count)
        + blocks(pairs, row_count - 1)
        + [pltpu.VMEM((half, head_dim, LANES), F32), pltpu.VMEM((half, 8, LANES), F32)]
        + blocks(groups, half)
        + blocks(groups, half - 1)
        + [pltpu.SemaphoreType.DMA((9,))]
        + sems(8)
        + sems(pairs)
        + sems(pairs, row_count - 1, 2)
        + sems(groups, half - 1, 2),
        compiler_params=pltpu.CompilerParams(
            collective_id=1, has_side_effects=True, vmem_limit_bytes=60 * 1024 * 1024
        ),
        name="slide",
    )(pixels, tissue, patch_weight, conv_weight, kv_weight, query_weight, latents)


def finish(
    features_hbm, normed_ref, weight_hbm,
    copied_hbm, out_ref,
    features_ref, weight_ref, in_sem, out_sem, load_sem,
):
    parts = in_sem.shape[0]
    extent = features_ref.shape[0] // parts
    load = pltpu.make_async_copy(weight_hbm, weight_ref, load_sem)

    def fetch(part):
        at = pl.ds(part * extent, extent)
        return pltpu.make_async_copy(features_hbm.at[at], features_ref.at[at], in_sem.at[part])

    def store(part):
        at = pl.ds(part * extent, extent)
        return pltpu.make_async_copy(features_ref.at[at], copied_hbm.at[at], out_sem.at[part])

    for part in range(parts):
        fetch(part).start()
    load.start()
    for part in range(parts):
        fetch(part).wait()
        store(part).start()
    load.wait()
    out_ref[...] = dot(normed_ref[...], weight_ref[...]).astype(BF16)
    for part in range(parts):
        store(part).wait()


def place(features, normed, out_weight):
    leave = pl.BlockSpec(memory_space=pl.ANY)
    vmem = pl.BlockSpec(memory_space=pltpu.VMEM)
    parts = 4
    return pl.pallas_call(
        finish,
        out_shape=(
            jax.ShapeDtypeStruct(features.shape, BF16),
            jax.ShapeDtypeStruct((normed.shape[0], out_weight.shape[1]), BF16),
        ),
        in_specs=[leave, vmem, leave],
        out_specs=(leave, vmem),
        scratch_shapes=[
            pltpu.VMEM(features.shape, BF16),
            pltpu.VMEM(out_weight.shape, BF16),
            pltpu.SemaphoreType.DMA((parts,)),
            pltpu.SemaphoreType.DMA((parts,)),
            pltpu.SemaphoreType.DMA,
        ],
        compiler_params=pltpu.CompilerParams(vmem_limit_bytes=32 * 1024 * 1024),
        name="place",
    )(features, normed, out_weight)


def shards(pixels, tissue, patch_weight, conv_weight, kv_weight, query_weight, out_weight, latents):
    tile_rows, tile_cols, _ = pixels.shape
    features, normed = embed_attend(
        pixels, tissue, patch_weight, conv_weight, kv_weight, query_weight, latents
    )
    features, latents_out = place(features, normed, out_weight)
    return (features.reshape(tile_rows, tile_cols, features.shape[1]), latents_out)


def solution(mesh):
    return jax.shard_map(
        shards,
        mesh=mesh,
        in_specs=(P("rows", "cols", None), P("rows", "cols"), P(), P(), P(), P(), P(), P()),
        out_specs=(P("rows", "cols", None), P(("rows", "cols"), None)),
        check_vma=False,
    )
```

```python
import functools

import jax
import jax.numpy as jnp
from jax import lax
from jax.experimental import pallas as pl
from jax.experimental.pallas import tpu as pltpu
from jax.sharding import PartitionSpec as P

HEADS = 16
BLOCK = 256
LANES = 128
PAD = 8
CORNER = 16
LAG = 4
LOG2_E = 1.4426950408889634
F32 = jnp.float32
BF16 = jnp.bfloat16
LOW = -1e30
MESH = pl.DeviceIdType.MESH


def dot(a, b):
    return jnp.dot(a, b, preferred_element_type=F32)


def merge(items, gain):
    top = functools.reduce(jnp.maximum, [peak for _, peak, _ in items])
    number, total = 0.0, 0.0
    for values, peak, whole in items:
        share = jnp.exp2((peak - top) * gain)
        number = number + share * values
        total = total + share * whole
    return number, top, total


def slide(
    heads,
    pixels_hbm, tissue_hbm, patch_hbm, conv_hbm, kv_hbm, ask_hbm, latent_hbm,
    features_ref, normed_ref,
    pixels_ref, tissue_ref, patch_ref, conv_ref, kv_ref, ask_ref, latent_ref,
    border_ref, side_ref, embedded_ref, wide_ref, taps_ref, summed_ref,
    query_ref, keys_ref, turned_ref, bias_ref, mask_ref, score_ref, peak_ref,
    part_ref, twin_ref, row_num, row_stat, got_num, got_stat,
    build_num, build_stat, col_num, col_stat, end_num, end_stat,
    load_sem, patch_sem, ask_send, ask_recv, halo_send, halo_recv,
    twin_send, twin_recv, row_send, row_recv, col_send, col_recv,
):
    tile_rows, tile_cols, patch_in = pixels_ref.shape
    tokens = tile_rows * tile_cols
    latent_count, channels = query_ref.shape
    pairs = heads // 2
    head_dim = channels // heads
    gain = LOG2_E * head_dim ** -0.5
    group_width = conv_ref.shape[1]
    row_count, col_count = lax.axis_size("rows"), lax.axis_size("cols")
    half = col_count // 2
    own = normed_ref.shape[0]
    side_count = latent_count // 2
    per_row = side_count // row_count
    groups = col_num.shape[0]
    per_group = pairs // groups
    row, col = lax.axis_index("rows"), lax.axis_index("cols")
    side, slot = lax.rem(col, 2), lax.div(col, 2)
    twin = (row, slot * 2 + (1 - side))
    row_peers = [(lax.rem(row + step, row_count), col) for step in range(1, row_count)]
    col_peers = [(row, lax.rem(slot + step, half) * 2 + side) for step in range(1, half)]

    fetches = {
        name: pltpu.make_async_copy(source, target, load_sem.at[number])
        for number, (name, source, target) in enumerate(
            (
                ("pixels", pixels_hbm, pixels_ref),
                ("low", latent_hbm.at[:, :, 0], latent_ref.at[0]),
                ("high", latent_hbm.at[:, :, 1], latent_ref.at[1]),
                ("ask", ask_hbm, ask_ref), ("conv", conv_hbm, conv_ref),
                ("tissue", tissue_hbm, tissue_ref), ("kv", kv_hbm, kv_ref),
            )
        )
    }
    blocks = channels // BLOCK

    def patch_load(step):
        at = pl.ds(pl.multiple_of(step * BLOCK, BLOCK), BLOCK)
        return pltpu.make_async_copy(
            patch_hbm.at[:, at], patch_ref.at[:, at], patch_sem.at[step]
        )

    fetches["pixels"].start()
    for block in range(blocks):
        patch_load(block).start()

    low_cols, high_cols = slice(0, CORNER), slice(tile_cols - CORNER, tile_cols)
    top, bottom = 0, tile_cols
    left = 2 * tile_cols
    right = left + tile_rows + 2 * CORNER
    end = tile_rows - 1

    def landing(start, extent):
        return border_ref.at[start : start + extent]

    moves = (
        (1, 0, pixels_hbm.at[end], landing(top, tile_cols)),
        (-1, 0, pixels_hbm.at[0], landing(bottom, tile_cols)),
        (1, 1, pixels_hbm.at[end, high_cols], landing(left + tile_rows, CORNER)),
        (1, -1, pixels_hbm.at[end, low_cols], landing(right + tile_rows, CORNER)),
        (-1, 1, pixels_hbm.at[0, high_cols], landing(left + tile_rows + CORNER, CORNER)),
        (-1, -1, pixels_hbm.at[0, low_cols], landing(right + tile_rows + CORNER, CORNER)),
        (0, 1, side_ref.at[1], landing(left, tile_rows)),
        (0, -1, side_ref.at[0], landing(right, tile_rows)),
    )

    def inside(down, across):
        ok = None
        for at, step, count in ((row, down, row_count), (col, across, col_count)):
            if step:
                here = at + step < count if step > 0 else at + step >= 0
                ok = here if ok is None else jnp.logical_and(ok, here)
        return ok

    def shift(number):
        down, across, source, target = moves[number]
        return pltpu.make_async_remote_copy(
            src_ref=source, dst_ref=target,
            send_sem=halo_send.at[number], recv_sem=halo_recv.at[number],
            device_id=(row + down, col + across), device_id_type=MESH,
        )

    def remote(source, target, send, recv, peer):
        return pltpu.make_async_remote_copy(
            src_ref=source, dst_ref=target, send_sem=send, recv_sem=recv,
            device_id=peer, device_id_type=MESH,
        )

    barrier = pltpu.get_barrier_semaphore()
    for down, across, _, _ in moves:
        @pl.when(inside(down, across))
        def _(down=down, across=across):
            pl.semaphore_signal(
                barrier, inc=1, device_id=(row + down, col + across), device_id_type=MESH
            )
    for peer in [twin] + row_peers + col_peers:
        pl.semaphore_signal(barrier, inc=1, device_id=peer, device_id_type=MESH)
    tall = 1 + (row > 0).astype(jnp.int32) + (row < row_count - 1).astype(jnp.int32)
    broad = 1 + (col > 0).astype(jnp.int32) + (col < col_count - 1).astype(jnp.int32)
    turned_ref[:, head_dim:, :] = jnp.ones((2, CORNER, tokens), BF16)
    build_num[...] = jnp.zeros_like(build_num)
    build_stat[...] = jnp.zeros_like(build_stat)
    pl.semaphore_wait(barrier, tall * broad - 1 + 1 + len(row_peers) + len(col_peers))
    for number in range(6):
        @pl.when(inside(*moves[number][:2]))
        def _(number=number):
            shift(number).start()
    fetches["pixels"].wait()
    side_ref[0] = pixels_ref[:, 0, :]
    side_ref[1] = pixels_ref[:, tile_cols - 1, :]
    for number in range(6, 8):
        @pl.when(inside(*moves[number][:2]))
        def _(number=number):
            shift(number).start()
    for name in ("low", "high", "ask", "conv", "tissue", "kv"):
        fetches[name].start()

    def embed(step, _):
        at = pl.ds(pl.multiple_of(step * BLOCK, BLOCK), BLOCK)
        patch_load(step).wait()
        pixels = pixels_ref[...].reshape(tokens, patch_in)
        embedded_ref[:, at] = dot(pixels, patch_ref[:, at])
        return 0

    lax.fori_loop(0, blocks, embed, 0)
    for name in ("low", "high", "ask"):
        fetches[name].wait()
    shared = blocks - blocks // 4
    mine_from = jnp.where(side == 0, 0, shared)
    mine_to = jnp.where(side == 0, shared, blocks)

    def share(step):
        at = pl.ds(pl.multiple_of(step * BLOCK, BLOCK), BLOCK)
        return remote(
            query_ref.at[:, at], query_ref.at[:, at], ask_send.at[step], ask_recv.at[step], twin
        )

    def ask(step, _):
        at = pl.ds(pl.multiple_of(step * BLOCK, BLOCK), BLOCK)
        latents = latent_ref[...].reshape(latent_count, ask_ref.shape[0])
        query_ref[:, at] = dot(latents, ask_ref[:, at]).astype(BF16)
        share(step).start()
        return 0

    lax.fori_loop(mine_from, mine_to, ask, 0)
    for name in ("conv", "tissue"):
        fetches[name].wait()
    mask_ref[...] = jnp.zeros_like(mask_ref)
    mask_ref[:, :tile_cols] = jnp.where(tissue_ref[...] > 0, 0.0, LOW)
    spot = lax.broadcasted_iota(jnp.int32, (tile_cols, LANES), 0)
    spot = spot == lax.broadcasted_iota(jnp.int32, (tile_cols, LANES), 1)
    for tile_row in range(tile_rows):
        line = jnp.broadcast_to(mask_ref[tile_row : tile_row + 1, :], (tile_cols, LANES))
        bias_ref[tile_row * tile_cols : (tile_row + 1) * tile_cols, :] = jnp.where(
            spot, line, 0.0
        ).astype(BF16)
    for number, (down, across, _, target) in enumerate(moves):
        @pl.when(inside(-down, -across))
        def _(number=number):
            shift(number).wait_recv()

        @pl.when(jnp.logical_not(inside(-down, -across)))
        def _(target=target):
            target[...] = jnp.zeros(target.shape, BF16)

    rows_ext = tile_rows + 2
    col_ext = tile_cols + PAD
    same = (
        lax.broadcasted_iota(jnp.int32, (BLOCK, BLOCK), 0) // group_width
        == lax.broadcasted_iota(jnp.int32, (BLOCK, BLOCK), 1) // group_width
    )
    side_slot = lax.broadcasted_iota(jnp.int32, (rows_ext, PAD, BLOCK), 1)
    thin = (1, PAD, BLOCK)

    def border(values, upper, lower):
        return (
            jnp.broadcast_to(values[upper : upper + 1][:, None, :], thin),
            jnp.broadcast_to(values[:tile_rows][:, None, :], (tile_rows, PAD, BLOCK)),
            jnp.broadcast_to(values[lower : lower + 1][:, None, :], thin),
        )

    for block in range(blocks):
        lanes = slice(block * BLOCK, (block + 1) * BLOCK)
        edges = dot(border_ref[...], patch_ref[:, lanes])
        inner = jnp.concatenate(
            [edges[top:bottom], embedded_ref[:, lanes], edges[bottom:left]], 0
        )
        upper, middle, lower = border(
            edges[left:right], tile_rows + CORNER - 1, tile_rows + 2 * CORNER - 1
        )
        from_left = jnp.concatenate([middle, lower, upper], 0)
        upper, middle, lower = border(edges[right:], tile_rows, tile_rows + CORNER)
        from_right = jnp.concatenate([upper, middle, lower], 0)
        flank = jnp.where(side_slot == PAD - 1, from_left, from_right)
        full = jnp.concatenate(
            [inner.reshape(rows_ext, tile_cols, BLOCK), flank], 1
        ).reshape(rows_ext * col_ext, BLOCK)
        for col_shift, amount in ((0, 1), (2, rows_ext * col_ext - 1)):
            moved = pltpu.roll(full, amount, 0).reshape(rows_ext, col_ext, BLOCK)
            moved = moved[:, :tile_cols].reshape(rows_ext * tile_cols, BLOCK)
            wide_ref[:, col_shift * BLOCK : (col_shift + 1) * BLOCK] = moved.astype(BF16)
        wide_ref[:, BLOCK : 2 * BLOCK] = inner.astype(BF16)
        for tap in range(9):
            small = conv_ref[tap, :, lanes]
            tiled = jnp.concatenate([small] * (BLOCK // group_width), 0)
            row_shift, col_shift = tap // 3, tap % 3
            taps_ref[row_shift, col_shift * BLOCK : (col_shift + 1) * BLOCK, :] = jnp.where(
                same, tiled, jnp.zeros_like(tiled)
            )
        total = wide_ref[tile_cols : tile_cols + tokens, BLOCK : 2 * BLOCK].astype(F32)
        for row_shift in range(3):
            first = row_shift * tile_cols
            total = total + dot(wide_ref[first : first + tokens, :], taps_ref[row_shift])
        summed_ref[:, lanes] = total

    inverse = 1.0 / channels

    def normalise(start, extent):
        at = pl.ds(pl.multiple_of(start, extent), extent)
        values = summed_ref[at, :]
        centred = values - jnp.sum(values, axis=-1, keepdims=True) * inverse
        variance = jnp.sum(centred * centred, axis=-1, keepdims=True) * inverse
        features_ref[at, :] = (centred * lax.rsqrt(variance + 1e-05)).astype(BF16)

    def project(step, start, extent):
        at = pl.ds(pl.multiple_of(step * BLOCK, BLOCK), BLOCK)
        found = dot(features_ref[start : start + extent, :], kv_ref[:, at]).astype(BF16)
        for inner in range(BLOCK // LANES):
            keys_ref[step * (BLOCK // LANES) + inner, start : start + extent, :] = found[
                :, inner * LANES : (inner + 1) * LANES
            ]

    first = tokens // 2
    steps = 2 * channels // BLOCK
    piece = first // steps

    def begin(step, _):
        normalise(step * LANES, LANES)
        return 0

    lax.fori_loop(0, first // LANES, begin, 0)
    fetches["kv"].wait()

    def middle(step, _):
        project(step, 0, first)
        normalise(first + step * piece, piece)
        return 0

    def last(step, _):
        project(step, first, first)
        return 0

    lax.fori_loop(0, steps, middle, 0)
    lax.fori_loop(0, steps, last, 0)

    lane = lax.broadcasted_iota(jnp.int32, (1, LANES), 1)
    low = lane < head_dim
    query_low = lax.broadcasted_iota(jnp.int32, (latent_count, LANES), 1) < head_dim
    ones = jnp.ones((latent_count, LANES), BF16)
    chunk = tokens // 2
    fresh = jnp.full((8, latent_count), -3e38, F32)

    def asked(pair, which):
        queries = query_ref[:, pl.ds(pl.multiple_of(pair * LANES, LANES), LANES)]
        mine = query_low if which == 0 else jnp.logical_not(query_low)
        return jnp.concatenate([jnp.where(mine, queries, jnp.zeros_like(queries)), ones], 1)

    def score(pair, part, queries, which, peak):
        at = slice(part * chunk, (part + 1) * chunk)
        keys = jnp.concatenate([keys_ref[pair, at, :], bias_ref[at, :]], 1)
        scores = lax.dot_general(
            keys, queries, (((1,), (1,)), ((), ())), preferred_element_type=F32
        )
        score_ref[which, at, :] = scores
        return jnp.maximum(peak, jnp.max(scores.reshape(chunk // 8, 8, latent_count), 0))

    def weigh(part, which, peak, total):
        at = slice(part * chunk, (part + 1) * chunk)
        weights = jnp.exp2((score_ref[which, at, :] - peak) * gain).astype(BF16)
        return total + dot(turned_ref[which, :, at], weights)

    def to_twin(pair):
        return remote(
            part_ref.at[pair, 1 - side], twin_ref.at[pair],
            twin_send.at[pair], twin_recv.at[pair], twin,
        )

    def to_row(pair, step):
        target = lax.rem(row + step, row_count)
        return [
            remote(
                source.at[pair, target], landing.at[pair, step - 1],
                row_send.at[pair, step - 1, kind], row_recv.at[pair, step - 1, kind],
                row_peers[step - 1],
            )
            for kind, (source, landing) in enumerate(((row_num, got_num), (row_stat, got_stat)))
        ]

    def to_col(group, step):
        target = lax.rem(slot + step, half)
        return [
            remote(
                source.at[group, target], landing.at[group, step - 1],
                col_send.at[group, step - 1, kind], col_recv.at[group, step - 1, kind],
                col_peers[step - 1],
            )
            for kind, (source, landing) in enumerate(((col_num, end_num), (col_stat, end_stat)))
        ]

    first_line = lax.broadcasted_iota(jnp.int32, (8, LANES), 0) == 0
    extent = head_dim + 8

    def with_twin(pair):
        to_twin(pair).wait_recv()
        merged = []
        for which in range(2):
            base = which * extent
            items = []
            for values in (part_ref.at[pair, side], twin_ref.at[pair]):
                stat = values[base + head_dim : base + extent, :]
                items.append((values[base : base + head_dim, :], stat[0:1], stat[1:2]))
            merged.append(merge(items, gain))
        for target in range(row_count):
            tile = target * per_row // LANES
            at = slice(tile * LANES, (tile + 1) * LANES)

            def joined(one, two, target=target, at=at):
                one, two = one[:, at], two[:, at]
                if target * per_row % LANES == 0:
                    return jnp.where(low, one, pltpu.roll(two, per_row, 1))
                return jnp.where(low, pltpu.roll(one, per_row, 1), two)

            number, peak, total = [joined(one, two) for one, two in zip(*merged)]
            row_num[pair, target] = number.astype(BF16)
            row_stat[pair, target] = jnp.where(first_line, peak, total)
        for step in range(1, row_count):
            for copy in to_row(pair, step):
                copy.start()

    def with_rows(pair):
        for step in range(1, row_count):
            for copy in to_row(pair, step):
                copy.wait_recv()
        items = []
        for values, stat in [(row_num[pair, row], row_stat[pair, row])] + [
            (got_num[pair, step], got_stat[pair, step]) for step in range(row_count - 1)
        ]:
            items.append((values.astype(F32), stat[0:1], stat[1:2]))
        number, peak, total = merge(items, gain)
        stat = jnp.where(first_line, peak, total)
        place = lax.rem(pair, per_group) * (2 * own)
        for target in range(half):
            for which in range(2):
                begin = place + which * own
                source = which * head_dim + target * own
                shift = lax.rem(begin - source + LANES, LANES)
                here = jnp.logical_and(lane >= begin, lane < begin + own)
                build_num[target] = jnp.where(
                    here, pltpu.roll(number, shift, 1), build_num[target]
                )
                build_stat[target] = jnp.where(
                    here, pltpu.roll(stat, shift, 1), build_stat[target]
                )

        @pl.when(lax.rem(pair, per_group) == per_group - 1)
        def _():
            group = lax.div(pair, per_group)
            col_num[group] = build_num[...].astype(BF16)
            col_stat[group] = build_stat[...]
            for step in range(1, half):
                for copy in to_col(group, step):
                    copy.start()

    def asked_wait(step, _):
        share(step).wait_recv()
        return 0

    lax.fori_loop(0, mine_from, asked_wait, 0)
    lax.fori_loop(mine_to, blocks, asked_wait, 0)
    peak = fresh
    queries = asked(0, 0)
    for part in range(2):
        peak = score(0, part, queries, 0, peak)
    peak_ref[...] = peak

    def step(pair, _):
        turned = keys_ref[pairs + pair].T
        for which in range(2):
            turned_ref[which, :head_dim, :] = turned[which * head_dim : (which + 1) * head_dim]
        current = peak_ref[...]
        for which in range(2):
            following = pair if which == 0 else jnp.minimum(pair + 1, pairs - 1)
            queries = asked(following, 1 - which)
            top = jnp.max(current, 0, keepdims=True)
            total = jnp.zeros((head_dim + CORNER, latent_count), F32)
            peak = fresh
            for part in range(2):
                peak = score(following, part, queries, 1 - which, peak)
                total = weigh(part, which, top, total)
            line = lax.broadcasted_iota(jnp.int32, (8, latent_count), 0) == 0
            stat = jnp.where(line, top, total[head_dim : head_dim + 8])
            for half_at in range(2):
                at = slice(half_at * side_count, (half_at + 1) * side_count)
                part_ref[pair, half_at, which * extent : which * extent + head_dim, :] = total[
                    :head_dim, at
                ]
                part_ref[
                    pair, half_at, which * extent + head_dim : (which + 1) * extent, :
                ] = stat[:, at]
            current = peak
        peak_ref[...] = current
        to_twin(pair).start()

        @pl.when(pair >= 1)
        def _():
            with_twin(pair - 1)

        @pl.when(pair >= LAG)
        def _():
            with_rows(pair - LAG)

        return 0

    lax.fori_loop(0, pairs, step, 0)
    for pair in range(pairs - LAG, pairs - 2):
        with_rows(pair)
    with_twin(pairs - 1)
    for pair in range(pairs - 2, pairs):
        with_rows(pair)

    pieces = []
    for group in range(groups):
        items = []
        for step in range(1, half):
            for copy in to_col(group, step):
                copy.wait_recv()
        for values, stat in [(col_num[group, slot], col_stat[group, slot])] + [
            (end_num[group, step], end_stat[group, step]) for step in range(half - 1)
        ]:
            items.append((values.astype(F32), stat[0:1], stat[1:2]))
        number, _, total = merge(items, gain)
        tile = (number / total).T
        for place in range(per_group):
            base = place * 2 * own
            pieces.append(
                jnp.concatenate([tile[base : base + own], tile[base + own : base + 2 * own]], 1)
            )
    attended = jnp.concatenate(pieces, 1)
    mean = jnp.sum(attended * attended, axis=-1, keepdims=True) * (1.0 / channels)
    normed = (attended * lax.rsqrt(mean + 1e-06)).astype(BF16)
    normed_ref[...] = normed

    def drain(pair, _):
        to_twin(pair).wait_send()
        for step in range(1, row_count):
            for copy in to_row(pair, step):
                copy.wait_send()
        return 0

    lax.fori_loop(0, pairs, drain, 0)

    def asked_drain(step, _):
        share(step).wait_send()
        return 0

    lax.fori_loop(mine_from, mine_to, asked_drain, 0)
    for group in range(groups):
        for step in range(1, half):
            for copy in to_col(group, step):
                copy.wait_send()
    for number, (down, across, _, _) in enumerate(moves):
        @pl.when(inside(down, across))
        def _(number=number):
            shift(number).wait_send()


def embed_attend(pixels, tissue, patch_weight, conv_weight, kv_weight, query_weight, latents):
    tile_rows, tile_cols, patch_in = pixels.shape
    tokens = tile_rows * tile_cols
    row_count, col_count = lax.axis_size("rows"), lax.axis_size("cols")
    half = col_count // 2
    latent_count = latents.shape[0]
    channels = query_weight.shape[1]
    own = latent_count // (row_count * col_count)
    pairs = HEADS // 2
    head_dim = channels // HEADS
    groups = max(1, pairs * 2 * own // LANES)
    side_count = latent_count // 2
    leave = pl.BlockSpec(memory_space=pl.ANY)
    latents = latents.reshape(row_count, half, 2, own, latents.shape[1])
    borders = 2 * tile_cols + 2 * (tile_rows + 2 * CORNER)

    def like(array):
        return pltpu.VMEM(array.shape, array.dtype)

    def blocks(*extent):
        return [
            pltpu.VMEM(extent + (head_dim, LANES), BF16), pltpu.VMEM(extent + (8, LANES), F32)
        ]

    def sems(*extent):
        return [pltpu.SemaphoreType.DMA(extent)] * 2

    return pl.pallas_call(
        functools.partial(slide, HEADS),
        out_shape=(
            pltpu.VMEM((tokens, channels), BF16),
            pltpu.VMEM((own, channels), BF16),
        ),
        in_specs=[pl.BlockSpec(memory_space=pltpu.HBM)] * 7,
        out_specs=(pl.BlockSpec(memory_space=pltpu.VMEM),) * 2,
        scratch_shapes=[
            like(array)
            for array in (pixels, tissue, patch_weight, conv_weight, kv_weight, query_weight)
        ]
        + [
            pltpu.VMEM((2, row_count, half, own, latents.shape[-1]), BF16),
            pltpu.VMEM((borders, patch_in), BF16),
            pltpu.VMEM((2, tile_rows, patch_in), BF16),
            pltpu.VMEM((tokens, channels), F32),
            pltpu.VMEM(((tile_rows + 2) * tile_cols, 3 * BLOCK), BF16),
            pltpu.VMEM((3, 3 * BLOCK, BLOCK), BF16),
            pltpu.VMEM((tokens, channels), F32),
            pltpu.VMEM((latent_count, channels), BF16),
            pltpu.VMEM((2 * pairs, tokens, LANES), BF16),
            pltpu.VMEM((2, head_dim + CORNER, tokens), BF16),
            pltpu.VMEM((tokens, LANES), BF16),
            pltpu.VMEM((tile_rows, LANES), F32),
            pltpu.VMEM((2, tokens, latent_count), F32),
            pltpu.VMEM((8, latent_count), F32),
            pltpu.VMEM((pairs, 2, 2 * (head_dim + 8), side_count), F32),
            pltpu.VMEM((pairs, 2 * (head_dim + 8), side_count), F32),
        ]
        + blocks(pairs, row_count)
        + blocks(pairs, row_count - 1)
        + [pltpu.VMEM((half, head_dim, LANES), F32), pltpu.VMEM((half, 8, LANES), F32)]
        + blocks(groups, half)
        + blocks(groups, half - 1)
        + [pltpu.SemaphoreType.DMA((7,)), pltpu.SemaphoreType.DMA((channels // BLOCK,))]
        + sems(channels // BLOCK)
        + sems(8)
        + sems(pairs)
        + sems(pairs, row_count - 1, 2)
        + sems(groups, half - 1, 2),
        compiler_params=pltpu.CompilerParams(
            collective_id=1, has_side_effects=True, vmem_limit_bytes=50 * 1024 * 1024
        ),
        name="slide",
    )(
        *(
            pltpu.with_memory_space_constraint(array, pltpu.HBM)
            for array in (
                pixels, tissue, patch_weight, conv_weight, kv_weight, query_weight, latents
            )
        )
    )


def finish(features_ref, normed_ref, weight_ref, features_hbm, out_ref, sem):
    store = pltpu.make_async_copy(features_ref, features_hbm, sem)
    store.start()
    out_ref[...] = dot(normed_ref[...], weight_ref[...]).astype(BF16)
    store.wait()


def place(features, normed, out_weight):
    vmem = pl.BlockSpec(memory_space=pltpu.VMEM)
    return pl.pallas_call(
        finish,
        out_shape=(
            jax.ShapeDtypeStruct(features.shape, BF16),
            jax.ShapeDtypeStruct((normed.shape[0], out_weight.shape[1]), BF16),
        ),
        in_specs=[vmem] * 3,
        out_specs=(pl.BlockSpec(memory_space=pl.ANY), vmem),
        scratch_shapes=[pltpu.SemaphoreType.DMA],
        compiler_params=pltpu.CompilerParams(vmem_limit_bytes=24 * 1024 * 1024),
        name="place",
    )(
        pltpu.with_memory_space_constraint(features, pltpu.VMEM),
        pltpu.with_memory_space_constraint(normed, pltpu.VMEM),
        pltpu.with_memory_space_constraint(out_weight, pltpu.VMEM),
    )


def shards(pixels, tissue, patch_weight, conv_weight, kv_weight, query_weight, out_weight, latents):
    tile_rows, tile_cols, _ = pixels.shape
    features, normed = embed_attend(
        pixels, tissue, patch_weight, conv_weight, kv_weight, query_weight, latents
    )
    features, latents_out = place(features, normed, out_weight)
    return (features.reshape(tile_rows, tile_cols, features.shape[1]), latents_out)


def solution(mesh):
    return jax.shard_map(
        shards,
        mesh=mesh,
        in_specs=(P("rows", "cols", None), P("rows", "cols"), P(), P(), P(), P(), P(), P()),
        out_specs=(P("rows", "cols", None), P(("rows", "cols"), None)),
        check_vma=False,
    )
```

```python
import functools

import jax
import jax.numpy as jnp
from jax import lax
from jax.experimental import pallas as pl
from jax.experimental.pallas import tpu as pltpu
from jax.sharding import PartitionSpec as P

HEADS = 16
BLOCK = 256
LANES = 128
PAD = 8
CORNER = 16
LAG = 6
LOG2_E = 1.4426950408889634
F32 = jnp.float32
BF16 = jnp.bfloat16
LOW = -1e30
MESH = pl.DeviceIdType.MESH


def dot(a, b):
    return jnp.dot(a, b, preferred_element_type=F32)


def merge(items, gain):
    top = functools.reduce(jnp.maximum, [peak for _, peak, _ in items])
    number, total = 0.0, 0.0
    for values, peak, whole in items:
        share = jnp.exp2((peak - top) * gain)
        number = number + share * values
        total = total + share * whole
    return number, top, total


def slide(
    heads,
    pixels_hbm, tissue_hbm, patch_hbm, conv_hbm, kv_hbm, ask_hbm, latent_hbm,
    features_ref, normed_ref,
    pixels_ref, tissue_ref, patch_ref, conv_ref, kv_ref, ask_ref, latent_ref,
    border_ref, side_ref, embedded_ref, wide_ref, taps_ref, summed_ref,
    query_ref, keys_ref, turned_ref, bias_ref, mask_ref, score_ref, peak_ref,
    part_ref, twin_ref, row_num, row_stat, got_num, got_stat,
    build_num, build_stat, spread_ref, col_num, col_stat, end_num, end_stat,
    load_sem, patch_sem, ask_send, ask_recv, halo_send, halo_recv,
    twin_send, twin_recv, row_send, row_recv, col_send, col_recv,
):
    tile_rows, tile_cols, patch_in = pixels_ref.shape
    tokens = tile_rows * tile_cols
    latent_count, channels = query_ref.shape
    pairs = heads // 2
    head_dim = channels // heads
    gain = LOG2_E * head_dim ** -0.5
    group_width = conv_ref.shape[1]
    row_count, col_count = lax.axis_size("rows"), lax.axis_size("cols")
    half = col_count // 2
    own = normed_ref.shape[0]
    side_count = latent_count // 2
    per_row = side_count // row_count
    groups = col_num.shape[0]
    per_group = pairs // groups
    row, col = lax.axis_index("rows"), lax.axis_index("cols")
    side, slot = lax.rem(col, 2), lax.div(col, 2)
    twin = (row, slot * 2 + (1 - side))
    row_peers = [(lax.rem(row + step, row_count), col) for step in range(1, row_count)]
    col_peers = [(row, lax.rem(slot + step, half) * 2 + side) for step in range(1, half)]

    fetches = {
        name: pltpu.make_async_copy(source, target, load_sem.at[number])
        for number, (name, source, target) in enumerate(
            (
                ("pixels", pixels_hbm, pixels_ref),
                ("low", latent_hbm.at[:, :, 0], latent_ref.at[0]),
                ("high", latent_hbm.at[:, :, 1], latent_ref.at[1]),
                ("ask", ask_hbm, ask_ref), ("conv", conv_hbm, conv_ref),
                ("tissue", tissue_hbm, tissue_ref), ("kv", kv_hbm, kv_ref),
            )
        )
    }
    blocks = channels // BLOCK

    def patch_load(step):
        at = pl.ds(pl.multiple_of(step * BLOCK, BLOCK), BLOCK)
        return pltpu.make_async_copy(
            patch_hbm.at[:, at], patch_ref.at[:, at], patch_sem.at[step]
        )

    fetches["pixels"].start()
    for block in range(blocks):
        patch_load(block).start()

    low_cols, high_cols = slice(0, CORNER), slice(tile_cols - CORNER, tile_cols)
    top, bottom = 0, tile_cols
    left = 2 * tile_cols
    right = left + tile_rows + 2 * CORNER
    end = tile_rows - 1

    def landing(start, extent):
        return border_ref.at[start : start + extent]

    moves = (
        (1, 0, pixels_hbm.at[end], landing(top, tile_cols)),
        (-1, 0, pixels_hbm.at[0], landing(bottom, tile_cols)),
        (1, 1, pixels_hbm.at[end, high_cols], landing(left + tile_rows, CORNER)),
        (1, -1, pixels_hbm.at[end, low_cols], landing(right + tile_rows, CORNER)),
        (-1, 1, pixels_hbm.at[0, high_cols], landing(left + tile_rows + CORNER, CORNER)),
        (-1, -1, pixels_hbm.at[0, low_cols], landing(right + tile_rows + CORNER, CORNER)),
        (0, 1, side_ref.at[1], landing(left, tile_rows)),
        (0, -1, side_ref.at[0], landing(right, tile_rows)),
    )

    def inside(down, across):
        ok = None
        for at, step, count in ((row, down, row_count), (col, across, col_count)):
            if step:
                here = at + step < count if step > 0 else at + step >= 0
                ok = here if ok is None else jnp.logical_and(ok, here)
        return ok

    def shift(number):
        down, across, source, target = moves[number]
        return pltpu.make_async_remote_copy(
            src_ref=source, dst_ref=target,
            send_sem=halo_send.at[number], recv_sem=halo_recv.at[number],
            device_id=(row + down, col + across), device_id_type=MESH,
        )

    def remote(source, target, send, recv, peer):
        return pltpu.make_async_remote_copy(
            src_ref=source, dst_ref=target, send_sem=send, recv_sem=recv,
            device_id=peer, device_id_type=MESH,
        )

    barrier = pltpu.get_barrier_semaphore()
    for down, across, _, _ in moves:
        @pl.when(inside(down, across))
        def _(down=down, across=across):
            pl.semaphore_signal(
                barrier, inc=1, device_id=(row + down, col + across), device_id_type=MESH
            )
    for peer in [twin] + row_peers + col_peers:
        pl.semaphore_signal(barrier, inc=1, device_id=peer, device_id_type=MESH)
    tall = 1 + (row > 0).astype(jnp.int32) + (row < row_count - 1).astype(jnp.int32)
    broad = 1 + (col > 0).astype(jnp.int32) + (col < col_count - 1).astype(jnp.int32)
    turned_ref[:, head_dim:, :] = jnp.ones((2, CORNER, tokens), BF16)
    build_num[...] = jnp.zeros_like(build_num)
    build_stat[...] = jnp.zeros_like(build_stat)
    pl.semaphore_wait(barrier, tall * broad - 1 + 1 + len(row_peers) + len(col_peers))
    for number in range(6):
        @pl.when(inside(*moves[number][:2]))
        def _(number=number):
            shift(number).start()
    fetches["pixels"].wait()
    side_ref[0] = pixels_ref[:, 0, :]
    side_ref[1] = pixels_ref[:, tile_cols - 1, :]
    for number in range(6, 8):
        @pl.when(inside(*moves[number][:2]))
        def _(number=number):
            shift(number).start()
    for name in ("low", "high", "ask", "conv", "tissue", "kv"):
        fetches[name].start()

    def embed(step, _):
        at = pl.ds(pl.multiple_of(step * BLOCK, BLOCK), BLOCK)
        patch_load(step).wait()
        pixels = pixels_ref[...].reshape(tokens, patch_in)
        embedded_ref[:, at] = dot(pixels, patch_ref[:, at])
        return 0

    lax.fori_loop(0, blocks, embed, 0)
    for name in ("low", "high", "ask"):
        fetches[name].wait()
    shared = blocks
    mine_from = jnp.where(side == 0, 0, shared)
    mine_to = jnp.where(side == 0, shared, blocks)

    def share(step):
        at = pl.ds(pl.multiple_of(step * BLOCK, BLOCK), BLOCK)
        return remote(
            query_ref.at[:, at], query_ref.at[:, at], ask_send.at[step], ask_recv.at[step], twin
        )

    def ask(step, _):
        at = pl.ds(pl.multiple_of(step * BLOCK, BLOCK), BLOCK)
        latents = latent_ref[...].reshape(latent_count, ask_ref.shape[0])
        query_ref[:, at] = dot(latents, ask_ref[:, at]).astype(BF16)
        share(step).start()
        return 0

    lax.fori_loop(mine_from, mine_to, ask, 0)
    for name in ("conv", "tissue"):
        fetches[name].wait()
    mask_ref[...] = jnp.zeros_like(mask_ref)
    mask_ref[:, :tile_cols] = jnp.where(tissue_ref[...] > 0, 0.0, LOW)
    spot = lax.broadcasted_iota(jnp.int32, (tile_cols, LANES), 0)
    spot = spot == lax.broadcasted_iota(jnp.int32, (tile_cols, LANES), 1)
    for tile_row in range(tile_rows):
        line = jnp.broadcast_to(mask_ref[tile_row : tile_row + 1, :], (tile_cols, LANES))
        bias_ref[tile_row * tile_cols : (tile_row + 1) * tile_cols, :] = jnp.where(
            spot, line, 0.0
        ).astype(BF16)
    for number, (down, across, _, target) in enumerate(moves):
        @pl.when(inside(-down, -across))
        def _(number=number):
            shift(number).wait_recv()

        @pl.when(jnp.logical_not(inside(-down, -across)))
        def _(target=target):
            target[...] = jnp.zeros(target.shape, BF16)

    rows_ext = tile_rows + 2
    col_ext = tile_cols + PAD
    same = (
        lax.broadcasted_iota(jnp.int32, (BLOCK, BLOCK), 0) // group_width
        == lax.broadcasted_iota(jnp.int32, (BLOCK, BLOCK), 1) // group_width
    )
    side_slot = lax.broadcasted_iota(jnp.int32, (rows_ext, PAD, BLOCK), 1)
    thin = (1, PAD, BLOCK)

    def border(values, upper, lower):
        return (
            jnp.broadcast_to(values[upper : upper + 1][:, None, :], thin),
            jnp.broadcast_to(values[:tile_rows][:, None, :], (tile_rows, PAD, BLOCK)),
            jnp.broadcast_to(values[lower : lower + 1][:, None, :], thin),
        )

    for block in range(blocks):
        lanes = slice(block * BLOCK, (block + 1) * BLOCK)
        edges = dot(border_ref[...], patch_ref[:, lanes])
        inner = jnp.concatenate(
            [edges[top:bottom], embedded_ref[:, lanes], edges[bottom:left]], 0
        )
        upper, middle, lower = border(
            edges[left:right], tile_rows + CORNER - 1, tile_rows + 2 * CORNER - 1
        )
        from_left = jnp.concatenate([middle, lower, upper], 0)
        upper, middle, lower = border(edges[right:], tile_rows, tile_rows + CORNER)
        from_right = jnp.concatenate([upper, middle, lower], 0)
        flank = jnp.where(side_slot == PAD - 1, from_left, from_right)
        full = jnp.concatenate(
            [inner.reshape(rows_ext, tile_cols, BLOCK), flank], 1
        ).reshape(rows_ext * col_ext, BLOCK)
        for col_shift, amount in ((0, 1), (2, rows_ext * col_ext - 1)):
            moved = pltpu.roll(full, amount, 0).reshape(rows_ext, col_ext, BLOCK)
            moved = moved[:, :tile_cols].reshape(rows_ext * tile_cols, BLOCK)
            wide_ref[:, col_shift * BLOCK : (col_shift + 1) * BLOCK] = moved.astype(BF16)
        wide_ref[:, BLOCK : 2 * BLOCK] = inner.astype(BF16)
        for tap in range(9):
            small = conv_ref[tap, :, lanes]
            tiled = jnp.concatenate([small] * (BLOCK // group_width), 0)
            row_shift, col_shift = tap // 3, tap % 3
            taps_ref[row_shift, col_shift * BLOCK : (col_shift + 1) * BLOCK, :] = jnp.where(
                same, tiled, jnp.zeros_like(tiled)
            )
        total = wide_ref[tile_cols : tile_cols + tokens, BLOCK : 2 * BLOCK].astype(F32)
        for row_shift in range(3):
            first = row_shift * tile_cols
            total = total + dot(wide_ref[first : first + tokens, :], taps_ref[row_shift])
        summed_ref[:, lanes] = total

    inverse = 1.0 / channels

    def normalise(start, extent):
        at = pl.ds(pl.multiple_of(start, extent), extent)
        values = summed_ref[at, :]
        centred = values - jnp.sum(values, axis=-1, keepdims=True) * inverse
        variance = jnp.sum(centred * centred, axis=-1, keepdims=True) * inverse
        features_ref[at, :] = (centred * lax.rsqrt(variance + 1e-05)).astype(BF16)

    def project(step, _):
        at = pl.ds(pl.multiple_of(step * BLOCK, BLOCK), BLOCK)
        found = dot(features_ref[...], kv_ref[:, at]).astype(BF16)
        for inner in range(BLOCK // LANES):
            keys_ref[step * (BLOCK // LANES) + inner] = found[
                :, inner * LANES : (inner + 1) * LANES
            ]
        return 0

    def begin(step, _):
        normalise(step * LANES, LANES)
        return 0

    lax.fori_loop(0, tokens // LANES, begin, 0)
    fetches["kv"].wait()
    lax.fori_loop(0, 2 * channels // BLOCK, project, 0)

    lane = lax.broadcasted_iota(jnp.int32, (1, LANES), 1)
    low = lane < head_dim
    query_low = lax.broadcasted_iota(jnp.int32, (latent_count, LANES), 1) < head_dim
    ones = jnp.ones((latent_count, LANES), BF16)
    chunk = tokens // 2
    fresh = jnp.full((8, latent_count), -3e38, F32)

    def ordered(pair, which):
        at = pl.ds(pl.multiple_of(pair * LANES, LANES), LANES)
        turn = lax.rem(pair, per_group)
        pieces = []
        for line in range(2 * row_count):
            start = (line if which == 0 else line ^ 1) * per_row
            if own % CORNER == 0:
                for place in range(half):
                    source = start + lax.rem(place - turn + half, half) * own
                    pieces.append(query_ref[pl.ds(pl.multiple_of(source, own), own), at])
            else:
                block = query_ref[start : start + per_row, at].astype(F32)
                pieces.append(pltpu.roll(block, turn * own, 0).astype(BF16))
        return jnp.concatenate(pieces, 0)

    def asked(pair, which):
        queries = ordered(pair, which)
        mine = query_low if which == 0 else jnp.logical_not(query_low)
        return jnp.concatenate([jnp.where(mine, queries, jnp.zeros_like(queries)), ones], 1)

    def score(pair, part, queries, which, peak):
        at = slice(part * chunk, (part + 1) * chunk)
        keys = jnp.concatenate([keys_ref[pair, at, :], bias_ref[at, :]], 1)
        scores = lax.dot_general(
            keys, queries, (((1,), (1,)), ((), ())), preferred_element_type=F32
        )
        score_ref[which, at, :] = scores
        return jnp.maximum(peak, jnp.max(scores.reshape(chunk // 8, 8, latent_count), 0))

    def weigh(part, which, peak, total):
        at = slice(part * chunk, (part + 1) * chunk)
        weights = jnp.exp2((score_ref[which, at, :] - peak) * gain).astype(BF16)
        return total + dot(turned_ref[which, :, at], weights)

    def to_twin(pair):
        return remote(
            part_ref.at[pair, 1 - side], twin_ref.at[pair],
            twin_send.at[pair], twin_recv.at[pair], twin,
        )

    def to_row(pair, step):
        target = lax.rem(row + step, row_count)
        return [
            remote(
                source.at[pair, target], landing.at[pair, step - 1],
                row_send.at[pair, step - 1, kind], row_recv.at[pair, step - 1, kind],
                row_peers[step - 1],
            )
            for kind, (source, landing) in enumerate(((row_num, got_num), (row_stat, got_stat)))
        ]

    def to_col(group, step):
        target = lax.rem(slot + step, half)
        return [
            remote(
                source.at[group, target], landing.at[group, step - 1],
                col_send.at[group, step - 1, kind], col_recv.at[group, step - 1, kind],
                col_peers[step - 1],
            )
            for kind, (source, landing) in enumerate(((col_num, end_num), (col_stat, end_stat)))
        ]

    first_line = lax.broadcasted_iota(jnp.int32, (2, LANES), 0) == 0
    region = lax.div(lax.rem(lane, per_row), own)
    extent = head_dim + 8

    def with_twin(pair):
        merged = []
        for which in range(2):
            base = which * extent
            items = []
            for values in (part_ref.at[pair, side], twin_ref.at[pair]):
                stat = values[base + head_dim : base + extent, :]
                items.append((values[base : base + head_dim, :], stat[0:1], stat[1:2]))
            merged.append(merge(items, gain))
        for target in range(row_count):
            tile = target * per_row // LANES
            at = slice(tile * LANES, (tile + 1) * LANES)
            begin, after = merged if target % 2 == 0 else merged[::-1]
            number, peak, total = [
                jnp.where(low, one[:, at], two[:, at]) for one, two in zip(begin, after)
            ]
            row_num[pair, target] = number.astype(BF16)
            row_stat[pair, target] = jnp.where(first_line, peak, total)

    def with_rows(pair):
        items = []
        for values, stat in [(row_num[pair, row], row_stat[pair, row])] + [
            (got_num[pair, step], got_stat[pair, step]) for step in range(row_count - 1)
        ]:
            items.append((values.astype(F32), stat[0:1], stat[1:2]))
        number, peak, total = merge(items, gain)
        stat = jnp.where(first_line, peak, total)
        turn = lax.rem(pair, per_group)
        for target in range(half):
            here = region == lax.rem(turn + target, half)
            build_num[target] = jnp.where(here, number, build_num[target])
            build_stat[target] = jnp.where(here, stat, build_stat[target])

    def send_rows(pair):
        for step in range(1, row_count):
            for copy in to_row(pair, step):
                copy.start()

    def wait_rows(pair):
        for step in range(1, row_count):
            for copy in to_row(pair, step):
                copy.wait_recv()

    def send_cols(group):
        col_num[group] = build_num[...].astype(BF16)
        col_stat[group] = build_stat[...]
        for step in range(1, half):
            for copy in to_col(group, step):
                copy.start()

    def asked_wait(step, _):
        share(step).wait_recv()
        return 0

    lax.fori_loop(0, mine_from, asked_wait, 0)
    lax.fori_loop(mine_to, blocks, asked_wait, 0)
    peak = fresh
    queries = asked(0, 0)
    for part in range(2):
        peak = score(0, part, queries, 0, peak)
    peak_ref[...] = peak

    def step(pair, _):
        @pl.when(pair >= 2)
        def _():
            to_twin(pair - 2).wait_recv()

        @pl.when(pair >= LAG)
        def _():
            wait_rows(pair - LAG)

        turned = keys_ref[pairs + pair].T
        for which in range(2):
            turned_ref[which, :head_dim, :] = turned[which * head_dim : (which + 1) * head_dim]
        current = peak_ref[...]
        for which in range(2):
            following = pair if which == 0 else jnp.minimum(pair + 1, pairs - 1)
            queries = asked(following, 1 - which)
            if which == 0:
                with_twin(jnp.where(pair >= 2, pair - 2, pairs))
            else:
                with_rows(jnp.where(pair >= LAG, pair - LAG, pairs))
            top = jnp.max(current, 0, keepdims=True)
            total = jnp.zeros((head_dim + CORNER, latent_count), F32)
            peak = fresh
            for part in range(2):
                peak = score(following, part, queries, 1 - which, peak)
                total = weigh(part, which, top, total)
            line = lax.broadcasted_iota(jnp.int32, (8, latent_count), 0) == 0
            stat = jnp.where(line, top, total[head_dim : head_dim + 8])
            for half_at in range(2):
                at = slice(half_at * side_count, (half_at + 1) * side_count)
                part_ref[pair, half_at, which * extent : which * extent + head_dim, :] = total[
                    :head_dim, at
                ]
                part_ref[
                    pair, half_at, which * extent + head_dim : (which + 1) * extent, :
                ] = stat[:, at]
            current = peak
        peak_ref[...] = current
        to_twin(pair).start()

        @pl.when(pair >= 2)
        def _():
            send_rows(pair - 2)

        @pl.when(jnp.logical_and(pair >= LAG, lax.rem(pair - LAG, per_group) == per_group - 1))
        def _():
            send_cols(lax.div(pair - LAG, per_group))

        return 0

    def late_rows(pair):
        wait_rows(pair)
        with_rows(pair)
        if pair % per_group == per_group - 1:
            send_cols(pair // per_group)

    lax.fori_loop(0, pairs, step, 0)
    to_twin(pairs - 2).wait_recv()
    with_twin(pairs - 2)
    send_rows(pairs - 2)
    for pair in range(pairs - LAG, pairs - 3):
        late_rows(pair)
    to_twin(pairs - 1).wait_recv()
    with_twin(pairs - 1)
    send_rows(pairs - 1)
    for pair in range(pairs - 3, pairs):
        late_rows(pair)

    pieces = []
    for group in range(groups):
        items = []
        for step in range(1, half):
            for copy in to_col(group, step):
                copy.wait_recv()
        for values, stat in [(col_num[group, slot], col_stat[group, slot])] + [
            (end_num[group, step], end_stat[group, step]) for step in range(half - 1)
        ]:
            items.append((values.astype(F32), stat[0:1], stat[1:2]))
        number, _, total = merge(items, gain)
        spread_ref[group] = (number / total).T
    odd = lax.rem(row, 2)
    for group in range(groups):
        for turn in range(per_group):
            place = lax.rem(slot + turn, half) * own
            heads_here = []
            for which in range(2):
                begin = jnp.where(odd == which, 0, per_row) + place
                if own % 8 == 0:
                    heads_here.append(spread_ref[group, pl.ds(pl.multiple_of(begin, own), own), :])
                else:
                    heads_here.append(pltpu.roll(spread_ref[group], LANES - begin, 0)[:own])
            pieces.append(jnp.concatenate(heads_here, 1))
    attended = jnp.concatenate(pieces, 1)
    mean = jnp.sum(attended * attended, axis=-1, keepdims=True) * (1.0 / channels)
    normed = (attended * lax.rsqrt(mean + 1e-06)).astype(BF16)
    normed_ref[...] = normed

    def drain(pair, _):
        to_twin(pair).wait_send()
        for step in range(1, row_count):
            for copy in to_row(pair, step):
                copy.wait_send()
        return 0

    lax.fori_loop(0, pairs, drain, 0)

    def asked_drain(step, _):
        share(step).wait_send()
        return 0

    lax.fori_loop(mine_from, mine_to, asked_drain, 0)
    for group in range(groups):
        for step in range(1, half):
            for copy in to_col(group, step):
                copy.wait_send()
    for number, (down, across, _, _) in enumerate(moves):
        @pl.when(inside(down, across))
        def _(number=number):
            shift(number).wait_send()


def embed_attend(pixels, tissue, patch_weight, conv_weight, kv_weight, query_weight, latents):
    tile_rows, tile_cols, patch_in = pixels.shape
    tokens = tile_rows * tile_cols
    row_count, col_count = lax.axis_size("rows"), lax.axis_size("cols")
    half = col_count // 2
    latent_count = latents.shape[0]
    channels = query_weight.shape[1]
    own = latent_count // (row_count * col_count)
    pairs = HEADS // 2
    head_dim = channels // HEADS
    groups = max(1, pairs * 2 * own // LANES)
    side_count = latent_count // 2
    leave = pl.BlockSpec(memory_space=pl.ANY)
    latents = latents.reshape(row_count, half, 2, own, latents.shape[1])
    borders = 2 * tile_cols + 2 * (tile_rows + 2 * CORNER)

    def like(array):
        return pltpu.VMEM(array.shape, array.dtype)

    def blocks(*extent):
        return [
            pltpu.VMEM(extent + (head_dim, LANES), BF16), pltpu.VMEM(extent + (2, LANES), F32)
        ]

    def sems(*extent):
        return [pltpu.SemaphoreType.DMA(extent)] * 2

    return pl.pallas_call(
        functools.partial(slide, HEADS),
        out_shape=(
            pltpu.VMEM((tokens, channels), BF16),
            pltpu.VMEM((own, channels), BF16),
        ),
        in_specs=[pl.BlockSpec(memory_space=pltpu.HBM)] * 7,
        out_specs=(pl.BlockSpec(memory_space=pltpu.VMEM),) * 2,
        scratch_shapes=[
            like(array)
            for array in (pixels, tissue, patch_weight, conv_weight, kv_weight, query_weight)
        ]
        + [
            pltpu.VMEM((2, row_count, half, own, latents.shape[-1]), BF16),
            pltpu.VMEM((borders, patch_in), BF16),
            pltpu.VMEM((2, tile_rows, patch_in), BF16),
            pltpu.VMEM((tokens, channels), F32),
            pltpu.VMEM(((tile_rows + 2) * tile_cols, 3 * BLOCK), BF16),
            pltpu.VMEM((3, 3 * BLOCK, BLOCK), BF16),
            pltpu.VMEM((tokens, channels), F32),
            pltpu.VMEM((latent_count, channels), BF16),
            pltpu.VMEM((2 * pairs, tokens, LANES), BF16),
            pltpu.VMEM((2, head_dim + CORNER, tokens), BF16),
            pltpu.VMEM((tokens, LANES), BF16),
            pltpu.VMEM((tile_rows, LANES), F32),
            pltpu.VMEM((2, tokens, latent_count), F32),
            pltpu.VMEM((8, latent_count), F32),
            pltpu.VMEM((pairs + 1, 2, 2 * (head_dim + 8), side_count), F32),
            pltpu.VMEM((pairs + 1, 2 * (head_dim + 8), side_count), F32),
        ]
        + blocks(pairs + 1, row_count)
        + blocks(pairs + 1, row_count - 1)
        + [
            pltpu.VMEM((half, head_dim, LANES), F32),
            pltpu.VMEM((half, 2, LANES), F32),
            pltpu.VMEM((groups, LANES, head_dim), F32),
        ]
        + blocks(groups, half)
        + blocks(groups, half - 1)
        + [pltpu.SemaphoreType.DMA((7,)), pltpu.SemaphoreType.DMA((channels // BLOCK,))]
        + sems(channels // BLOCK)
        + sems(8)
        + sems(pairs)
        + sems(pairs, row_count - 1, 2)
        + sems(groups, half - 1, 2),
        compiler_params=pltpu.CompilerParams(
            collective_id=1, has_side_effects=True, vmem_limit_bytes=50 * 1024 * 1024
        ),
        name="slide",
    )(
        *(
            pltpu.with_memory_space_constraint(array, pltpu.HBM)
            for array in (
                pixels, tissue, patch_weight, conv_weight, kv_weight, query_weight, latents
            )
        )
    )


def finish(features_ref, normed_ref, weight_ref, features_hbm, out_ref, sem):
    store = pltpu.make_async_copy(features_ref, features_hbm, sem)
    store.start()
    out_ref[...] = dot(normed_ref[...], weight_ref[...]).astype(BF16)
    store.wait()


def place(features, normed, out_weight):
    vmem = pl.BlockSpec(memory_space=pltpu.VMEM)
    return pl.pallas_call(
        finish,
        out_shape=(
            jax.ShapeDtypeStruct(features.shape, BF16),
            jax.ShapeDtypeStruct((normed.shape[0], out_weight.shape[1]), BF16),
        ),
        in_specs=[vmem] * 3,
        out_specs=(pl.BlockSpec(memory_space=pl.ANY), vmem),
        scratch_shapes=[pltpu.SemaphoreType.DMA],
        compiler_params=pltpu.CompilerParams(vmem_limit_bytes=24 * 1024 * 1024),
        name="place",
    )(
        pltpu.with_memory_space_constraint(features, pltpu.VMEM),
        pltpu.with_memory_space_constraint(normed, pltpu.VMEM),
        pltpu.with_memory_space_constraint(out_weight, pltpu.VMEM),
    )


def shards(pixels, tissue, patch_weight, conv_weight, kv_weight, query_weight, out_weight, latents):
    tile_rows, tile_cols, _ = pixels.shape
    features, normed = embed_attend(
        pixels, tissue, patch_weight, conv_weight, kv_weight, query_weight, latents
    )
    features, latents_out = place(features, normed, out_weight)
    return (features.reshape(tile_rows, tile_cols, features.shape[1]), latents_out)


def solution(mesh):
    return jax.shard_map(
        shards,
        mesh=mesh,
        in_specs=(P("rows", "cols", None), P("rows", "cols"), P(), P(), P(), P(), P(), P()),
        out_specs=(P("rows", "cols", None), P(("rows", "cols"), None)),
        check_vma=False,
    )
```

```python
import functools

import jax
import jax.numpy as jnp
from jax import lax
from jax.experimental import pallas as pl
from jax.experimental.pallas import tpu as pltpu
from jax.sharding import PartitionSpec as P

HEADS = 16
BLOCK = 256
LANES = 128
PAD = 8
CORNER = 16
LAG = 6
LOG2_E = 1.4426950408889634
F32 = jnp.float32
BF16 = jnp.bfloat16
LOW = -1e30
MESH = pl.DeviceIdType.MESH


def dot(a, b):
    return jnp.dot(a, b, preferred_element_type=F32)


def merge(items, gain):
    top = functools.reduce(jnp.maximum, [peak for _, peak, _ in items])
    number, total = 0.0, 0.0
    for values, peak, whole in items:
        share = jnp.exp2((peak - top) * gain)
        number = number + share * values
        total = total + share * whole
    return number, top, total


def slide(
    heads,
    pixels_hbm, tissue_hbm, patch_hbm, conv_hbm, kv_hbm, ask_hbm, latent_hbm,
    features_ref, normed_ref,
    pixels_ref, tissue_ref, patch_ref, conv_ref, kv_ref, ask_ref, latent_ref,
    border_ref, side_ref, embedded_ref, wide_ref, taps_ref, summed_ref,
    query_ref, keys_ref, turned_ref, bias_ref, mask_ref, score_ref, peak_ref,
    part_ref, twin_ref, row_num, row_stat, got_num, got_stat,
    build_num, build_stat, spread_ref, col_num, col_stat, end_num, end_stat,
    load_sem, patch_sem, ask_send, ask_recv, halo_send, halo_recv,
    twin_send, twin_recv, row_send, row_recv, col_send, col_recv,
):
    tile_rows, tile_cols, patch_in = pixels_ref.shape
    tokens = tile_rows * tile_cols
    latent_count, channels = query_ref.shape
    pairs = heads // 2
    head_dim = channels // heads
    gain = LOG2_E * head_dim ** -0.5
    group_width = conv_ref.shape[1]
    row_count, col_count = lax.axis_size("rows"), lax.axis_size("cols")
    half = col_count // 2
    own = normed_ref.shape[0]
    side_count = latent_count // 2
    per_row = side_count // row_count
    groups = col_num.shape[0]
    per_group = pairs // groups
    row, col = lax.axis_index("rows"), lax.axis_index("cols")
    side, slot = lax.rem(col, 2), lax.div(col, 2)
    twin = (row, slot * 2 + (1 - side))
    row_peers = [(lax.rem(row + step, row_count), col) for step in range(1, row_count)]
    col_peers = [(row, lax.rem(slot + step, half) * 2 + side) for step in range(1, half)]

    fetches = {
        name: pltpu.make_async_copy(source, target, load_sem.at[number])
        for number, (name, source, target) in enumerate(
            (
                ("pixels", pixels_hbm, pixels_ref),
                ("low", latent_hbm.at[:, :, 0], latent_ref.at[0]),
                ("high", latent_hbm.at[:, :, 1], latent_ref.at[1]),
                ("ask", ask_hbm, ask_ref), ("conv", conv_hbm, conv_ref),
                ("tissue", tissue_hbm, tissue_ref), ("kv", kv_hbm, kv_ref),
            )
        )
    }
    blocks = channels // BLOCK

    def patch_load(step):
        at = pl.ds(pl.multiple_of(step * BLOCK, BLOCK), BLOCK)
        return pltpu.make_async_copy(
            patch_hbm.at[:, at], patch_ref.at[:, at], patch_sem.at[step]
        )

    fetches["pixels"].start()
    for block in range(blocks):
        patch_load(block).start()

    low_cols, high_cols = slice(0, CORNER), slice(tile_cols - CORNER, tile_cols)
    top, bottom = 0, tile_cols
    left = 2 * tile_cols
    right = left + tile_rows + 2 * CORNER
    end = tile_rows - 1

    def landing(start, extent):
        return border_ref.at[start : start + extent]

    moves = (
        (1, 0, pixels_hbm.at[end], landing(top, tile_cols)),
        (-1, 0, pixels_hbm.at[0], landing(bottom, tile_cols)),
        (1, 1, pixels_hbm.at[end, high_cols], landing(left + tile_rows, CORNER)),
        (1, -1, pixels_hbm.at[end, low_cols], landing(right + tile_rows, CORNER)),
        (-1, 1, pixels_hbm.at[0, high_cols], landing(left + tile_rows + CORNER, CORNER)),
        (-1, -1, pixels_hbm.at[0, low_cols], landing(right + tile_rows + CORNER, CORNER)),
        (0, 1, side_ref.at[1], landing(left, tile_rows)),
        (0, -1, side_ref.at[0], landing(right, tile_rows)),
    )

    def inside(down, across):
        ok = None
        for at, step, count in ((row, down, row_count), (col, across, col_count)):
            if step:
                here = at + step < count if step > 0 else at + step >= 0
                ok = here if ok is None else jnp.logical_and(ok, here)
        return ok

    def shift(number):
        down, across, source, target = moves[number]
        return pltpu.make_async_remote_copy(
            src_ref=source, dst_ref=target,
            send_sem=halo_send.at[number], recv_sem=halo_recv.at[number],
            device_id=(row + down, col + across), device_id_type=MESH,
        )

    def remote(source, target, send, recv, peer):
        return pltpu.make_async_remote_copy(
            src_ref=source, dst_ref=target, send_sem=send, recv_sem=recv,
            device_id=peer, device_id_type=MESH,
        )

    barrier = pltpu.get_barrier_semaphore()
    for down, across, _, _ in moves:
        @pl.when(inside(down, across))
        def _(down=down, across=across):
            pl.semaphore_signal(
                barrier, inc=1, device_id=(row + down, col + across), device_id_type=MESH
            )
    for peer in [twin] + row_peers + col_peers:
        pl.semaphore_signal(barrier, inc=1, device_id=peer, device_id_type=MESH)
    tall = 1 + (row > 0).astype(jnp.int32) + (row < row_count - 1).astype(jnp.int32)
    broad = 1 + (col > 0).astype(jnp.int32) + (col < col_count - 1).astype(jnp.int32)
    turned_ref[:, head_dim:, :] = jnp.ones((2, CORNER, tokens), BF16)
    build_num[...] = jnp.zeros_like(build_num)
    build_stat[...] = jnp.zeros_like(build_stat)
    pl.semaphore_wait(barrier, tall * broad - 1 + 1 + len(row_peers) + len(col_peers))
    for number in range(6):
        @pl.when(inside(*moves[number][:2]))
        def _(number=number):
            shift(number).start()
    fetches["pixels"].wait()
    side_ref[0] = pixels_ref[:, 0, :]
    side_ref[1] = pixels_ref[:, tile_cols - 1, :]
    for number in range(6, 8):
        @pl.when(inside(*moves[number][:2]))
        def _(number=number):
            shift(number).start()
    for name in ("low", "high", "ask", "conv", "tissue", "kv"):
        fetches[name].start()

    def embed(step, _):
        at = pl.ds(pl.multiple_of(step * BLOCK, BLOCK), BLOCK)
        patch_load(step).wait()
        pixels = pixels_ref[...].reshape(tokens, patch_in)
        embedded_ref[:, at] = dot(pixels, patch_ref[:, at])
        return 0

    lax.fori_loop(0, blocks, embed, 0)
    for name in ("low", "high", "ask"):
        fetches[name].wait()
    shared = blocks
    mine_from = jnp.where(side == 0, 0, shared)
    mine_to = jnp.where(side == 0, shared, blocks)

    def share(step):
        at = pl.ds(pl.multiple_of(step * BLOCK, BLOCK), BLOCK)
        return remote(
            query_ref.at[:, at], query_ref.at[:, at], ask_send.at[step], ask_recv.at[step], twin
        )

    def ask(step, _):
        at = pl.ds(pl.multiple_of(step * BLOCK, BLOCK), BLOCK)
        latents = latent_ref[...].reshape(latent_count, ask_ref.shape[0])
        query_ref[:, at] = dot(latents, ask_ref[:, at]).astype(BF16)
        share(step).start()
        return 0

    lax.fori_loop(mine_from, mine_to, ask, 0)
    for name in ("conv", "tissue"):
        fetches[name].wait()
    mask_ref[...] = jnp.zeros_like(mask_ref)
    mask_ref[:, :tile_cols] = jnp.where(tissue_ref[...] > 0, 0.0, LOW)
    spot = lax.broadcasted_iota(jnp.int32, (tile_cols, LANES), 0)
    spot = spot == lax.broadcasted_iota(jnp.int32, (tile_cols, LANES), 1)
    for tile_row in range(tile_rows):
        line = jnp.broadcast_to(mask_ref[tile_row : tile_row + 1, :], (tile_cols, LANES))
        bias_ref[tile_row * tile_cols : (tile_row + 1) * tile_cols, :] = jnp.where(
            spot, line, 0.0
        ).astype(BF16)
    for number, (down, across, _, target) in enumerate(moves):
        @pl.when(inside(-down, -across))
        def _(number=number):
            shift(number).wait_recv()

        @pl.when(jnp.logical_not(inside(-down, -across)))
        def _(target=target):
            target[...] = jnp.zeros(target.shape, BF16)

    rows_ext = tile_rows + 2
    col_ext = tile_cols + PAD
    same = (
        lax.broadcasted_iota(jnp.int32, (BLOCK, BLOCK), 0) // group_width
        == lax.broadcasted_iota(jnp.int32, (BLOCK, BLOCK), 1) // group_width
    )
    side_slot = lax.broadcasted_iota(jnp.int32, (rows_ext, PAD, BLOCK), 1)
    thin = (1, PAD, BLOCK)

    def border(values, upper, lower):
        return (
            jnp.broadcast_to(values[upper : upper + 1][:, None, :], thin),
            jnp.broadcast_to(values[:tile_rows][:, None, :], (tile_rows, PAD, BLOCK)),
            jnp.broadcast_to(values[lower : lower + 1][:, None, :], thin),
        )

    for block in range(blocks):
        lanes = slice(block * BLOCK, (block + 1) * BLOCK)
        edges = dot(border_ref[...], patch_ref[:, lanes])
        inner = jnp.concatenate(
            [edges[top:bottom], embedded_ref[:, lanes], edges[bottom:left]], 0
        )
        upper, middle, lower = border(
            edges[left:right], tile_rows + CORNER - 1, tile_rows + 2 * CORNER - 1
        )
        from_left = jnp.concatenate([middle, lower, upper], 0)
        upper, middle, lower = border(edges[right:], tile_rows, tile_rows + CORNER)
        from_right = jnp.concatenate([upper, middle, lower], 0)
        flank = jnp.where(side_slot == PAD - 1, from_left, from_right)
        full = jnp.concatenate(
            [inner.reshape(rows_ext, tile_cols, BLOCK), flank], 1
        ).reshape(rows_ext * col_ext, BLOCK)
        for col_shift in range(3):
            moved = inner
            if col_shift != 1:
                moved = pltpu.roll(full, 1 if col_shift == 0 else rows_ext * col_ext - 1, 0)
                moved = moved.reshape(rows_ext, col_ext, BLOCK)[:, :tile_cols]
            moved = moved.astype(BF16).reshape(rows_ext // 2, 2, tile_cols, BLOCK)
            even, odd = moved[:, 0], moved[:, 1]
            near, far, here, after = even[:-1], even[1:], odd[:-1], odd[1:]
            if col_shift == 1:
                centres = [here, far]
            at = slice(col_shift * BLOCK, (col_shift + 1) * BLOCK)
            for number, mixed in enumerate((near - far, here + far, far - here, here - after)):
                wide_ref[number, :, at] = mixed.reshape(tokens // 2, BLOCK)
            ends = [conv_ref[3 * line + col_shift, :, lanes].astype(F32) for line in range(3)]
            outer = ends[0] + ends[2]
            for number, small in enumerate(
                (ends[0], (outer + ends[1]) * 0.5, (outer - ends[1]) * 0.5, ends[2])
            ):
                tiled = jnp.concatenate([small.astype(BF16)] * (BLOCK // group_width), 0)
                taps_ref[number, at, :] = jnp.where(same, tiled, jnp.zeros_like(tiled))
        parts = [dot(wide_ref[number], taps_ref[number]) for number in range(4)]
        upper = (parts[1] + parts[2]) + parts[0]
        lower = parts[1] - parts[2] - parts[3]
        split = (tile_rows // 2, tile_cols, BLOCK)
        both = [
            half_rows.reshape(split) + centre.astype(F32)
            for half_rows, centre in zip((upper, lower), centres)
        ]
        summed_ref[:, lanes] = jnp.stack(both, 1).reshape(tokens, BLOCK)

    inverse = 1.0 / channels

    def normalise(start, extent):
        at = pl.ds(pl.multiple_of(start, extent), extent)
        values = summed_ref[at, :]
        centred = values - jnp.sum(values, axis=-1, keepdims=True) * inverse
        variance = jnp.sum(centred * centred, axis=-1, keepdims=True) * inverse
        features_ref[at, :] = (centred * lax.rsqrt(variance + 1e-05)).astype(BF16)

    def project(step, _):
        at = pl.ds(pl.multiple_of(step * BLOCK, BLOCK), BLOCK)
        found = dot(features_ref[...], kv_ref[:, at]).astype(BF16)
        for inner in range(BLOCK // LANES):
            keys_ref[step * (BLOCK // LANES) + inner] = found[
                :, inner * LANES : (inner + 1) * LANES
            ]
        return 0

    def begin(step, _):
        normalise(step * LANES, LANES)
        return 0

    lax.fori_loop(0, tokens // LANES, begin, 0)
    fetches["kv"].wait()
    lax.fori_loop(0, 2 * channels // BLOCK, project, 0)

    lane = lax.broadcasted_iota(jnp.int32, (1, LANES), 1)
    low = lane < head_dim
    query_low = lax.broadcasted_iota(jnp.int32, (latent_count, LANES), 1) < head_dim
    ones = jnp.ones((latent_count, LANES), BF16)
    chunk = tokens // 2
    fresh = jnp.full((8, latent_count), -3e38, F32)

    def ordered(pair, which):
        at = pl.ds(pl.multiple_of(pair * LANES, LANES), LANES)
        turn = lax.rem(pair, per_group)
        pieces = []
        for line in range(2 * row_count):
            start = (line if which == 0 else line ^ 1) * per_row
            if own % CORNER == 0:
                for place in range(half):
                    source = start + lax.rem(place - turn + half, half) * own
                    pieces.append(query_ref[pl.ds(pl.multiple_of(source, own), own), at])
            else:
                block = query_ref[start : start + per_row, at].astype(F32)
                pieces.append(pltpu.roll(block, turn * own, 0).astype(BF16))
        return jnp.concatenate(pieces, 0)

    def asked(pair, which):
        queries = ordered(pair, which)
        mine = query_low if which == 0 else jnp.logical_not(query_low)
        return jnp.concatenate([jnp.where(mine, queries, jnp.zeros_like(queries)), ones], 1)

    def score(pair, part, queries, which, peak):
        at = slice(part * chunk, (part + 1) * chunk)
        keys = jnp.concatenate([keys_ref[pair, at, :], bias_ref[at, :]], 1)
        scores = lax.dot_general(
            keys, queries, (((1,), (1,)), ((), ())), preferred_element_type=F32
        )
        score_ref[which, at, :] = scores
        return jnp.maximum(peak, jnp.max(scores.reshape(chunk // 8, 8, latent_count), 0))

    def weigh(part, which, peak, total):
        at = slice(part * chunk, (part + 1) * chunk)
        weights = jnp.exp2((score_ref[which, at, :] - peak) * gain).astype(BF16)
        return total + dot(turned_ref[which, :, at], weights)

    def to_twin(pair):
        return remote(
            part_ref.at[pair, 1 - side], twin_ref.at[pair],
            twin_send.at[pair], twin_recv.at[pair], twin,
        )

    def to_row(pair, step):
        target = lax.rem(row + step, row_count)
        return [
            remote(
                source.at[pair, target], landing.at[pair, step - 1],
                row_send.at[pair, step - 1, kind], row_recv.at[pair, step - 1, kind],
                row_peers[step - 1],
            )
            for kind, (source, landing) in enumerate(((row_num, got_num), (row_stat, got_stat)))
        ]

    def to_col(group, step):
        target = lax.rem(slot + step, half)
        return [
            remote(
                source.at[group, target], landing.at[group, step - 1],
                col_send.at[group, step - 1, kind], col_recv.at[group, step - 1, kind],
                col_peers[step - 1],
            )
            for kind, (source, landing) in enumerate(((col_num, end_num), (col_stat, end_stat)))
        ]

    first_line = lax.broadcasted_iota(jnp.int32, (2, LANES), 0) == 0
    region = lax.div(lax.rem(lane, per_row), own)
    extent = head_dim + 8

    def with_twin(pair):
        merged = []
        for which in range(2):
            base = which * extent
            items = []
            for values in (part_ref.at[pair, side], twin_ref.at[pair]):
                stat = values[base + head_dim : base + extent, :]
                items.append((values[base : base + head_dim, :], stat[0:1], stat[1:2]))
            merged.append(merge(items, gain))
        for target in range(row_count):
            tile = target * per_row // LANES
            at = slice(tile * LANES, (tile + 1) * LANES)
            begin, after = merged if target % 2 == 0 else merged[::-1]
            number, peak, total = [
                jnp.where(low, one[:, at], two[:, at]) for one, two in zip(begin, after)
            ]
            row_num[pair, target] = number.astype(BF16)
            row_stat[pair, target] = jnp.where(first_line, peak, total)

    def with_rows(pair):
        items = []
        for values, stat in [(row_num[pair, row], row_stat[pair, row])] + [
            (got_num[pair, step], got_stat[pair, step]) for step in range(row_count - 1)
        ]:
            items.append((values.astype(F32), stat[0:1], stat[1:2]))
        number, peak, total = merge(items, gain)
        stat = jnp.where(first_line, peak, total)
        turn = lax.rem(pair, per_group)
        for target in range(half):
            here = region == lax.rem(turn + target, half)
            build_num[target] = jnp.where(here, number, build_num[target])
            build_stat[target] = jnp.where(here, stat, build_stat[target])

    def send_rows(pair):
        for step in range(1, row_count):
            for copy in to_row(pair, step):
                copy.start()

    def wait_rows(pair):
        for step in range(1, row_count):
            for copy in to_row(pair, step):
                copy.wait_recv()

    def send_cols(group):
        col_num[group] = build_num[...].astype(BF16)
        col_stat[group] = build_stat[...]
        for step in range(1, half):
            for copy in to_col(group, step):
                copy.start()

    def asked_wait(step, _):
        share(step).wait_recv()
        return 0

    lax.fori_loop(0, mine_from, asked_wait, 0)
    lax.fori_loop(mine_to, blocks, asked_wait, 0)
    peak = fresh
    queries = asked(0, 0)
    for part in range(2):
        peak = score(0, part, queries, 0, peak)
    peak_ref[...] = peak

    def step(pair, _):
        @pl.when(pair >= 2)
        def _():
            to_twin(pair - 2).wait_recv()

        @pl.when(pair >= LAG)
        def _():
            wait_rows(pair - LAG)

        turned = keys_ref[pairs + pair].T
        for which in range(2):
            turned_ref[which, :head_dim, :] = turned[which * head_dim : (which + 1) * head_dim]
        current = peak_ref[...]
        for which in range(2):
            following = pair if which == 0 else jnp.minimum(pair + 1, pairs - 1)
            queries = asked(following, 1 - which)
            if which == 0:
                with_twin(jnp.where(pair >= 2, pair - 2, pairs))
            else:
                with_rows(jnp.where(pair >= LAG, pair - LAG, pairs))
            top = jnp.max(current, 0, keepdims=True)
            total = jnp.zeros((head_dim + CORNER, latent_count), F32)
            peak = fresh
            for part in range(2):
                peak = score(following, part, queries, 1 - which, peak)
                total = weigh(part, which, top, total)
            line = lax.broadcasted_iota(jnp.int32, (8, latent_count), 0) == 0
            stat = jnp.where(line, top, total[head_dim : head_dim + 8])
            for half_at in range(2):
                at = slice(half_at * side_count, (half_at + 1) * side_count)
                part_ref[pair, half_at, which * extent : which * extent + head_dim, :] = total[
                    :head_dim, at
                ]
                part_ref[
                    pair, half_at, which * extent + head_dim : (which + 1) * extent, :
                ] = stat[:, at]
            current = peak
        peak_ref[...] = current
        to_twin(pair).start()

        @pl.when(pair >= 2)
        def _():
            send_rows(pair - 2)

        @pl.when(jnp.logical_and(pair >= LAG, lax.rem(pair - LAG, per_group) == per_group - 1))
        def _():
            send_cols(lax.div(pair - LAG, per_group))

        return 0

    def late_rows(pair):
        wait_rows(pair)
        with_rows(pair)
        if pair % per_group == per_group - 1:
            send_cols(pair // per_group)

    lax.fori_loop(0, pairs, step, 0)
    to_twin(pairs - 2).wait_recv()
    with_twin(pairs - 2)
    send_rows(pairs - 2)
    for pair in range(pairs - LAG, pairs - 3):
        late_rows(pair)
    to_twin(pairs - 1).wait_recv()
    with_twin(pairs - 1)
    send_rows(pairs - 1)
    for pair in range(pairs - 3, pairs):
        late_rows(pair)

    pieces = []
    for group in range(groups):
        items = []
        for step in range(1, half):
            for copy in to_col(group, step):
                copy.wait_recv()
        for values, stat in [(col_num[group, slot], col_stat[group, slot])] + [
            (end_num[group, step], end_stat[group, step]) for step in range(half - 1)
        ]:
            items.append((values.astype(F32), stat[0:1], stat[1:2]))
        number, _, total = merge(items, gain)
        spread_ref[group] = (number / total).T
    odd = lax.rem(row, 2)
    for group in range(groups):
        for turn in range(per_group):
            place = lax.rem(slot + turn, half) * own
            heads_here = []
            for which in range(2):
                begin = jnp.where(odd == which, 0, per_row) + place
                if own % 8 == 0:
                    heads_here.append(spread_ref[group, pl.ds(pl.multiple_of(begin, own), own), :])
                else:
                    heads_here.append(pltpu.roll(spread_ref[group], LANES - begin, 0)[:own])
            pieces.append(jnp.concatenate(heads_here, 1))
    attended = jnp.concatenate(pieces, 1)
    mean = jnp.sum(attended * attended, axis=-1, keepdims=True) * (1.0 / channels)
    normed = (attended * lax.rsqrt(mean + 1e-06)).astype(BF16)
    normed_ref[...] = normed

    def drain(pair, _):
        to_twin(pair).wait_send()
        for step in range(1, row_count):
            for copy in to_row(pair, step):
                copy.wait_send()
        return 0

    lax.fori_loop(0, pairs, drain, 0)

    def asked_drain(step, _):
        share(step).wait_send()
        return 0

    lax.fori_loop(mine_from, mine_to, asked_drain, 0)
    for group in range(groups):
        for step in range(1, half):
            for copy in to_col(group, step):
                copy.wait_send()
    for number, (down, across, _, _) in enumerate(moves):
        @pl.when(inside(down, across))
        def _(number=number):
            shift(number).wait_send()


def embed_attend(pixels, tissue, patch_weight, conv_weight, kv_weight, query_weight, latents):
    tile_rows, tile_cols, patch_in = pixels.shape
    tokens = tile_rows * tile_cols
    row_count, col_count = lax.axis_size("rows"), lax.axis_size("cols")
    half = col_count // 2
    latent_count = latents.shape[0]
    channels = query_weight.shape[1]
    own = latent_count // (row_count * col_count)
    pairs = HEADS // 2
    head_dim = channels // HEADS
    groups = max(1, pairs * 2 * own // LANES)
    side_count = latent_count // 2
    leave = pl.BlockSpec(memory_space=pl.ANY)
    latents = latents.reshape(row_count, half, 2, own, latents.shape[1])
    borders = 2 * tile_cols + 2 * (tile_rows + 2 * CORNER)

    def like(array):
        return pltpu.VMEM(array.shape, array.dtype)

    def blocks(*extent):
        return [
            pltpu.VMEM(extent + (head_dim, LANES), BF16), pltpu.VMEM(extent + (2, LANES), F32)
        ]

    def sems(*extent):
        return [pltpu.SemaphoreType.DMA(extent)] * 2

    return pl.pallas_call(
        functools.partial(slide, HEADS),
        out_shape=(
            pltpu.VMEM((tokens, channels), BF16),
            pltpu.VMEM((own, channels), BF16),
        ),
        in_specs=[pl.BlockSpec(memory_space=pltpu.HBM)] * 7,
        out_specs=(pl.BlockSpec(memory_space=pltpu.VMEM),) * 2,
        scratch_shapes=[
            like(array)
            for array in (pixels, tissue, patch_weight, conv_weight, kv_weight, query_weight)
        ]
        + [
            pltpu.VMEM((2, row_count, half, own, latents.shape[-1]), BF16),
            pltpu.VMEM((borders, patch_in), BF16),
            pltpu.VMEM((2, tile_rows, patch_in), BF16),
            pltpu.VMEM((tokens, channels), F32),
            pltpu.VMEM((4, tokens // 2, 3 * BLOCK), BF16),
            pltpu.VMEM((4, 3 * BLOCK, BLOCK), BF16),
            pltpu.VMEM((tokens, channels), F32),
            pltpu.VMEM((latent_count, channels), BF16),
            pltpu.VMEM((2 * pairs, tokens, LANES), BF16),
            pltpu.VMEM((2, head_dim + CORNER, tokens), BF16),
            pltpu.VMEM((tokens, LANES), BF16),
            pltpu.VMEM((tile_rows, LANES), F32),
            pltpu.VMEM((2, tokens, latent_count), F32),
            pltpu.VMEM((8, latent_count), F32),
            pltpu.VMEM((pairs + 1, 2, 2 * (head_dim + 8), side_count), F32),
            pltpu.VMEM((pairs + 1, 2 * (head_dim + 8), side_count), F32),
        ]
        + blocks(pairs + 1, row_count)
        + blocks(pairs + 1, row_count - 1)
        + [
            pltpu.VMEM((half, head_dim, LANES), F32),
            pltpu.VMEM((half, 2, LANES), F32),
            pltpu.VMEM((groups, LANES, head_dim), F32),
        ]
        + blocks(groups, half)
        + blocks(groups, half - 1)
        + [pltpu.SemaphoreType.DMA((7,)), pltpu.SemaphoreType.DMA((channels // BLOCK,))]
        + sems(channels // BLOCK)
        + sems(8)
        + sems(pairs)
        + sems(pairs, row_count - 1, 2)
        + sems(groups, half - 1, 2),
        compiler_params=pltpu.CompilerParams(
            collective_id=1, has_side_effects=True, vmem_limit_bytes=50 * 1024 * 1024
        ),
        name="slide",
    )(
        *(
            pltpu.with_memory_space_constraint(array, pltpu.HBM)
            for array in (
                pixels, tissue, patch_weight, conv_weight, kv_weight, query_weight, latents
            )
        )
    )


def finish(features_ref, normed_ref, weight_ref, features_hbm, out_ref, sem):
    store = pltpu.make_async_copy(features_ref, features_hbm, sem)
    store.start()
    out_ref[...] = dot(normed_ref[...], weight_ref[...]).astype(BF16)
    store.wait()


def place(features, normed, out_weight):
    vmem = pl.BlockSpec(memory_space=pltpu.VMEM)
    return pl.pallas_call(
        finish,
        out_shape=(
            jax.ShapeDtypeStruct(features.shape, BF16),
            jax.ShapeDtypeStruct((normed.shape[0], out_weight.shape[1]), BF16),
        ),
        in_specs=[vmem] * 3,
        out_specs=(pl.BlockSpec(memory_space=pl.ANY), vmem),
        scratch_shapes=[pltpu.SemaphoreType.DMA],
        compiler_params=pltpu.CompilerParams(vmem_limit_bytes=24 * 1024 * 1024),
        name="place",
    )(
        pltpu.with_memory_space_constraint(features, pltpu.VMEM),
        pltpu.with_memory_space_constraint(normed, pltpu.VMEM),
        pltpu.with_memory_space_constraint(out_weight, pltpu.VMEM),
    )


def shards(pixels, tissue, patch_weight, conv_weight, kv_weight, query_weight, out_weight, latents):
    tile_rows, tile_cols, _ = pixels.shape
    features, normed = embed_attend(
        pixels, tissue, patch_weight, conv_weight, kv_weight, query_weight, latents
    )
    features, latents_out = place(features, normed, out_weight)
    return (features.reshape(tile_rows, tile_cols, features.shape[1]), latents_out)


def solution(mesh):
    return jax.shard_map(
        shards,
        mesh=mesh,
        in_specs=(P("rows", "cols", None), P("rows", "cols"), P(), P(), P(), P(), P(), P()),
        out_specs=(P("rows", "cols", None), P(("rows", "cols"), None)),
        check_vma=False,
    )
```

```python
import functools

import jax
import jax.numpy as jnp
from jax import lax
from jax.experimental import pallas as pl
from jax.experimental.pallas import tpu as pltpu
from jax.sharding import PartitionSpec as P

HEADS = 16
BLOCK = 256
LANES = 128
PAD = 8
CORNER = 16
LAG = 6
PIECE = 32
LOG2_E = 1.4426950408889634
F32 = jnp.float32
BF16 = jnp.bfloat16
LOW = -1e30
MESH = pl.DeviceIdType.MESH


def dot(a, b):
    return jnp.dot(a, b, preferred_element_type=F32)


def merge(items, gain):
    top = functools.reduce(jnp.maximum, [peak for _, peak, _ in items])
    number, total = 0.0, 0.0
    for values, peak, whole in items:
        share = jnp.exp2((peak - top) * gain)
        number = number + share * values
        total = total + share * whole
    return number, top, total


def slide(
    heads,
    pixels_hbm, tissue_hbm, patch_hbm, conv_hbm, kv_hbm, ask_hbm, latent_hbm,
    features_ref, normed_ref,
    pixels_ref, tissue_ref, patch_ref, conv_ref, kv_ref, ask_ref, latent_ref,
    border_ref, side_ref, embedded_ref, wide_ref, taps_ref, summed_ref,
    query_ref, keys_ref, turned_ref, bias_ref, mask_ref, score_ref, peak_ref,
    part_ref, twin_ref, row_num, row_stat, got_num, got_stat,
    build_num, build_stat, spread_ref, col_num, col_stat, end_num, end_stat,
    load_sem, patch_sem, ask_send, ask_recv, halo_send, halo_recv,
    twin_send, twin_recv, row_send, row_recv, col_send, col_recv,
):
    tile_rows, tile_cols, patch_in = pixels_ref.shape
    tokens = tile_rows * tile_cols
    latent_count, channels = query_ref.shape
    pairs = heads // 2
    head_dim = channels // heads
    gain = LOG2_E * head_dim ** -0.5
    group_width = conv_ref.shape[1]
    row_count, col_count = lax.axis_size("rows"), lax.axis_size("cols")
    half = col_count // 2
    own = normed_ref.shape[0]
    side_count = latent_count // 2
    per_row = side_count // row_count
    groups = col_num.shape[0]
    per_group = pairs // groups
    row, col = lax.axis_index("rows"), lax.axis_index("cols")
    side, slot = lax.rem(col, 2), lax.div(col, 2)
    twin = (row, slot * 2 + (1 - side))
    row_peers = [(lax.rem(row + step, row_count), col) for step in range(1, row_count)]
    col_peers = [(row, lax.rem(slot + step, half) * 2 + side) for step in range(1, half)]

    fetches = {
        name: pltpu.make_async_copy(source, target, load_sem.at[number])
        for number, (name, source, target) in enumerate(
            (
                ("pixels", pixels_hbm, pixels_ref),
                ("low", latent_hbm.at[:, :, 0], latent_ref.at[0]),
                ("high", latent_hbm.at[:, :, 1], latent_ref.at[1]),
                ("ask", ask_hbm, ask_ref), ("conv", conv_hbm, conv_ref),
                ("tissue", tissue_hbm, tissue_ref), ("kv", kv_hbm, kv_ref),
            )
        )
    }
    blocks = channels // BLOCK

    def patch_load(step):
        at = pl.ds(pl.multiple_of(step * BLOCK, BLOCK), BLOCK)
        return pltpu.make_async_copy(
            patch_hbm.at[:, at], patch_ref.at[:, at], patch_sem.at[step]
        )

    fetches["tissue"].start()
    fetches["pixels"].start()
    for block in range(blocks):
        patch_load(block).start()

    low_cols, high_cols = slice(0, CORNER), slice(tile_cols - CORNER, tile_cols)
    top, bottom = 0, tile_cols
    left = 2 * tile_cols
    right = left + tile_rows + 2 * CORNER
    end = tile_rows - 1

    def landing(start, extent):
        return border_ref.at[start : start + extent]

    moves = (
        (1, 0, pixels_hbm.at[end], landing(top, tile_cols)),
        (-1, 0, pixels_hbm.at[0], landing(bottom, tile_cols)),
        (1, 1, pixels_hbm.at[end, high_cols], landing(left + tile_rows, CORNER)),
        (1, -1, pixels_hbm.at[end, low_cols], landing(right + tile_rows, CORNER)),
        (-1, 1, pixels_hbm.at[0, high_cols], landing(left + tile_rows + CORNER, CORNER)),
        (-1, -1, pixels_hbm.at[0, low_cols], landing(right + tile_rows + CORNER, CORNER)),
        (0, 1, side_ref.at[1], landing(left, tile_rows)),
        (0, -1, side_ref.at[0], landing(right, tile_rows)),
    )

    def inside(down, across):
        ok = None
        for at, step, count in ((row, down, row_count), (col, across, col_count)):
            if step:
                here = at + step < count if step > 0 else at + step >= 0
                ok = here if ok is None else jnp.logical_and(ok, here)
        return ok

    def shift(number):
        down, across, source, target = moves[number]
        return pltpu.make_async_remote_copy(
            src_ref=source, dst_ref=target,
            send_sem=halo_send.at[number], recv_sem=halo_recv.at[number],
            device_id=(row + down, col + across), device_id_type=MESH,
        )

    def remote(source, target, send, recv, peer):
        return pltpu.make_async_remote_copy(
            src_ref=source, dst_ref=target, send_sem=send, recv_sem=recv,
            device_id=peer, device_id_type=MESH,
        )

    barrier = pltpu.get_barrier_semaphore()
    for down, across, _, _ in moves:
        @pl.when(inside(down, across))
        def _(down=down, across=across):
            pl.semaphore_signal(
                barrier, inc=1, device_id=(row + down, col + across), device_id_type=MESH
            )
    for peer in [twin] + row_peers + col_peers:
        pl.semaphore_signal(barrier, inc=1, device_id=peer, device_id_type=MESH)
    tall = 1 + (row > 0).astype(jnp.int32) + (row < row_count - 1).astype(jnp.int32)
    broad = 1 + (col > 0).astype(jnp.int32) + (col < col_count - 1).astype(jnp.int32)
    turned_ref[:, head_dim:, :] = jnp.ones((2, CORNER, tokens), BF16)
    build_num[...] = jnp.zeros_like(build_num)
    build_stat[...] = jnp.zeros_like(build_stat)
    pl.semaphore_wait(barrier, tall * broad - 1 + 1 + len(row_peers) + len(col_peers))
    for number in range(6):
        @pl.when(inside(*moves[number][:2]))
        def _(number=number):
            shift(number).start()
    fetches["tissue"].wait()
    mask_ref[...] = jnp.zeros_like(mask_ref)
    mask_ref[:, :tile_cols] = jnp.where(tissue_ref[...] > 0, 0.0, LOW)
    spot = lax.broadcasted_iota(jnp.int32, (tile_cols, LANES), 0)
    spot = spot == lax.broadcasted_iota(jnp.int32, (tile_cols, LANES), 1)
    for tile_row in range(tile_rows):
        line = jnp.broadcast_to(mask_ref[tile_row : tile_row + 1, :], (tile_cols, LANES))
        bias_ref[tile_row * tile_cols : (tile_row + 1) * tile_cols, :] = jnp.where(
            spot, line, 0.0
        ).astype(BF16)
    fetches["pixels"].wait()
    side_ref[0] = pixels_ref[:, 0, :]
    side_ref[1] = pixels_ref[:, tile_cols - 1, :]
    for number in range(6, 8):
        @pl.when(inside(*moves[number][:2]))
        def _(number=number):
            shift(number).start()
    for name in ("low", "high", "ask", "conv", "kv"):
        fetches[name].start()

    def embed(step, _):
        at = pl.ds(pl.multiple_of(step * BLOCK, BLOCK), BLOCK)
        patch_load(step).wait()
        pixels = pixels_ref[...].reshape(tokens, patch_in)
        embedded_ref[:, at] = dot(pixels, patch_ref[:, at])
        return 0

    lax.fori_loop(0, blocks, embed, 0)
    for name in ("low", "high", "ask"):
        fetches[name].wait()
    shared = blocks
    mine_from = jnp.where(side == 0, 0, shared)
    mine_to = jnp.where(side == 0, shared, blocks)

    def share(step):
        at = pl.ds(pl.multiple_of(step * BLOCK, BLOCK), BLOCK)
        return remote(
            query_ref.at[:, at], query_ref.at[:, at], ask_send.at[step], ask_recv.at[step], twin
        )

    def ask(step, _):
        at = pl.ds(pl.multiple_of(step * BLOCK, BLOCK), BLOCK)
        latents = latent_ref[...].reshape(latent_count, ask_ref.shape[0])
        query_ref[:, at] = dot(latents, ask_ref[:, at]).astype(BF16)
        share(step).start()
        return 0

    lax.fori_loop(mine_from, mine_to, ask, 0)
    fetches["conv"].wait()
    for number, (down, across, _, target) in enumerate(moves):
        @pl.when(inside(-down, -across))
        def _(number=number):
            shift(number).wait_recv()

        @pl.when(jnp.logical_not(inside(-down, -across)))
        def _(target=target):
            target[...] = jnp.zeros(target.shape, BF16)

    rows_ext = tile_rows + 2
    col_ext = tile_cols + PAD
    same = (
        lax.broadcasted_iota(jnp.int32, (BLOCK, BLOCK), 0) // group_width
        == lax.broadcasted_iota(jnp.int32, (BLOCK, BLOCK), 1) // group_width
    )
    side_slot = lax.broadcasted_iota(jnp.int32, (rows_ext, PAD, BLOCK), 1)
    thin = (1, PAD, BLOCK)

    def border(values, upper, lower):
        return (
            jnp.broadcast_to(values[upper : upper + 1][:, None, :], thin),
            jnp.broadcast_to(values[:tile_rows][:, None, :], (tile_rows, PAD, BLOCK)),
            jnp.broadcast_to(values[lower : lower + 1][:, None, :], thin),
        )

    for block in range(blocks):
        lanes = slice(block * BLOCK, (block + 1) * BLOCK)
        edges = dot(border_ref[...], patch_ref[:, lanes])
        inner = jnp.concatenate(
            [edges[top:bottom], embedded_ref[:, lanes], edges[bottom:left]], 0
        )
        upper, middle, lower = border(
            edges[left:right], tile_rows + CORNER - 1, tile_rows + 2 * CORNER - 1
        )
        from_left = jnp.concatenate([middle, lower, upper], 0)
        upper, middle, lower = border(edges[right:], tile_rows, tile_rows + CORNER)
        from_right = jnp.concatenate([upper, middle, lower], 0)
        flank = jnp.where(side_slot == PAD - 1, from_left, from_right)
        full = jnp.concatenate(
            [inner.reshape(rows_ext, tile_cols, BLOCK), flank], 1
        ).reshape(rows_ext * col_ext, BLOCK)
        for col_shift in range(3):
            moved = inner
            if col_shift != 1:
                moved = pltpu.roll(full, 1 if col_shift == 0 else rows_ext * col_ext - 1, 0)
                moved = moved.reshape(rows_ext, col_ext, BLOCK)[:, :tile_cols]
            moved = moved.astype(BF16).reshape(rows_ext // 2, 2, tile_cols, BLOCK)
            even, odd = moved[:, 0], moved[:, 1]
            near, far, here, after = even[:-1], even[1:], odd[:-1], odd[1:]
            if col_shift == 1:
                centres = [here, far]
            at = slice(col_shift * BLOCK, (col_shift + 1) * BLOCK)
            for number, mixed in enumerate((near - far, here + far, far - here, here - after)):
                wide_ref[number, :, at] = mixed.reshape(tokens // 2, BLOCK)
            ends = [conv_ref[3 * line + col_shift, :, lanes].astype(F32) for line in range(3)]
            outer = ends[0] + ends[2]
            for number, small in enumerate(
                (ends[0], (outer + ends[1]) * 0.5, (outer - ends[1]) * 0.5, ends[2])
            ):
                tiled = jnp.concatenate([small.astype(BF16)] * (BLOCK // group_width), 0)
                taps_ref[number, at, :] = jnp.where(same, tiled, jnp.zeros_like(tiled))
        parts = [dot(wide_ref[number], taps_ref[number]) for number in range(4)]
        upper = (parts[1] + parts[2]) + parts[0]
        lower = parts[1] - parts[2] - parts[3]
        split = (tile_rows // 2, tile_cols, BLOCK)
        both = [
            half_rows.reshape(split) + centre.astype(F32)
            for half_rows, centre in zip((upper, lower), centres)
        ]
        summed_ref[:, lanes] = jnp.stack(both, 1).reshape(tokens, BLOCK)

    inverse = 1.0 / channels

    def normalise(step, _):
        for part in range(LANES // PIECE):
            at = pl.ds(pl.multiple_of(step * LANES + part * PIECE, PIECE), PIECE)
            values = summed_ref[at, :]
            centred = values - jnp.sum(values, axis=-1, keepdims=True) * inverse
            variance = jnp.sum(centred * centred, axis=-1, keepdims=True) * inverse
            features_ref[at, :] = (centred * lax.rsqrt(variance + 1e-05)).astype(BF16)
        return 0

    def project(step, _):
        at = pl.ds(pl.multiple_of(step * BLOCK, BLOCK), BLOCK)
        found = dot(features_ref[...], kv_ref[:, at]).astype(BF16)
        for inner in range(BLOCK // LANES):
            keys_ref[step * (BLOCK // LANES) + inner] = found[
                :, inner * LANES : (inner + 1) * LANES
            ]
        return 0

    lax.fori_loop(0, tokens // LANES, normalise, 0)
    fetches["kv"].wait()
    lax.fori_loop(0, 2 * channels // BLOCK, project, 0)

    lane = lax.broadcasted_iota(jnp.int32, (1, LANES), 1)
    low = lane < head_dim
    query_low = lax.broadcasted_iota(jnp.int32, (latent_count, LANES), 1) < head_dim
    ones = jnp.ones((latent_count, LANES), BF16)
    chunk = tokens // 2
    fresh = jnp.full((8, latent_count), -3e38, F32)

    def ordered(pair, which):
        at = pl.ds(pl.multiple_of(pair * LANES, LANES), LANES)
        turn = lax.rem(pair, per_group)
        pieces = []
        for line in range(2 * row_count):
            start = (line if which == 0 else line ^ 1) * per_row
            if own % CORNER == 0:
                for place in range(half):
                    source = start + lax.rem(place - turn + half, half) * own
                    pieces.append(query_ref[pl.ds(pl.multiple_of(source, own), own), at])
            else:
                block = query_ref[start : start + per_row, at].astype(F32)
                pieces.append(pltpu.roll(block, turn * own, 0).astype(BF16))
        return jnp.concatenate(pieces, 0)

    def asked(pair, which):
        queries = ordered(pair, which)
        mine = query_low if which == 0 else jnp.logical_not(query_low)
        return jnp.concatenate([jnp.where(mine, queries, jnp.zeros_like(queries)), ones], 1)

    def score(pair, part, queries, which, peak):
        at = slice(part * chunk, (part + 1) * chunk)
        keys = jnp.concatenate([keys_ref[pair, at, :], bias_ref[at, :]], 1)
        scores = lax.dot_general(
            keys, queries, (((1,), (1,)), ((), ())), preferred_element_type=F32
        )
        score_ref[which, at, :] = scores
        return jnp.maximum(peak, jnp.max(scores.reshape(chunk // 8, 8, latent_count), 0))

    def weigh(part, which, peak, total):
        at = slice(part * chunk, (part + 1) * chunk)
        weights = jnp.exp2((score_ref[which, at, :] - peak) * gain).astype(BF16)
        return total + dot(turned_ref[which, :, at], weights)

    def to_twin(pair):
        return remote(
            part_ref.at[pair, 1 - side], twin_ref.at[pair],
            twin_send.at[pair], twin_recv.at[pair], twin,
        )

    def to_row(pair, step):
        target = lax.rem(row + step, row_count)
        return [
            remote(
                source.at[pair, target], landing.at[pair, step - 1],
                row_send.at[pair, step - 1, kind], row_recv.at[pair, step - 1, kind],
                row_peers[step - 1],
            )
            for kind, (source, landing) in enumerate(((row_num, got_num), (row_stat, got_stat)))
        ]

    def to_col(group, step):
        target = lax.rem(slot + step, half)
        return [
            remote(
                source.at[group, target], landing.at[group, step - 1],
                col_send.at[group, step - 1, kind], col_recv.at[group, step - 1, kind],
                col_peers[step - 1],
            )
            for kind, (source, landing) in enumerate(((col_num, end_num), (col_stat, end_stat)))
        ]

    first_line = lax.broadcasted_iota(jnp.int32, (2, LANES), 0) == 0
    region = lax.div(lax.rem(lane, per_row), own)
    extent = head_dim + 8

    def with_twin(pair):
        merged = []
        for which in range(2):
            base = which * extent
            items = []
            for values in (part_ref.at[pair, side], twin_ref.at[pair]):
                stat = values[base + head_dim : base + extent, :]
                items.append((values[base : base + head_dim, :], stat[0:1], stat[1:2]))
            merged.append(merge(items, gain))
        for target in range(row_count):
            tile = target * per_row // LANES
            at = slice(tile * LANES, (tile + 1) * LANES)
            begin, after = merged if target % 2 == 0 else merged[::-1]
            number, peak, total = [
                jnp.where(low, one[:, at], two[:, at]) for one, two in zip(begin, after)
            ]
            row_num[pair, target] = number.astype(BF16)
            row_stat[pair, target] = jnp.where(first_line, peak, total)

    def with_rows(pair):
        items = []
        for values, stat in [(row_num[pair, row], row_stat[pair, row])] + [
            (got_num[pair, step], got_stat[pair, step]) for step in range(row_count - 1)
        ]:
            items.append((values.astype(F32), stat[0:1], stat[1:2]))
        number, peak, total = merge(items, gain)
        stat = jnp.where(first_line, peak, total)
        turn = lax.rem(pair, per_group)
        for target in range(half):
            here = region == lax.rem(turn + target, half)
            build_num[target] = jnp.where(here, number, build_num[target])
            build_stat[target] = jnp.where(here, stat, build_stat[target])

    def send_rows(pair):
        for step in range(1, row_count):
            for copy in to_row(pair, step):
                copy.start()

    def wait_rows(pair):
        for step in range(1, row_count):
            for copy in to_row(pair, step):
                copy.wait_recv()

    def send_cols(group):
        col_num[group] = build_num[...].astype(BF16)
        col_stat[group] = build_stat[...]
        for step in range(1, half):
            for copy in to_col(group, step):
                copy.start()

    def asked_wait(step, _):
        share(step).wait_recv()
        return 0

    lax.fori_loop(0, mine_from, asked_wait, 0)
    lax.fori_loop(mine_to, blocks, asked_wait, 0)
    peak = fresh
    queries = asked(0, 0)
    for part in range(2):
        peak = score(0, part, queries, 0, peak)
    peak_ref[...] = peak

    def attend(pair, final):
        turned = keys_ref[pairs + pair].T
        for which in range(2):
            turned_ref[which, :head_dim, :] = turned[which * head_dim : (which + 1) * head_dim]
        current = peak_ref[...]
        for which in range(2):
            following = pair if which == 0 else pair + 1
            ahead = not (final and which == 1)
            if ahead:
                queries = asked(following, 1 - which)
            if which == 0:
                with_twin(jnp.where(pair >= 2, pair - 2, pairs))
            else:
                with_rows(jnp.where(pair >= LAG, pair - LAG, pairs))
            top = jnp.max(current, 0, keepdims=True)
            total = jnp.zeros((head_dim + CORNER, latent_count), F32)
            peak = fresh
            for part in range(2):
                if ahead:
                    peak = score(following, part, queries, 1 - which, peak)
                total = weigh(part, which, top, total)
            line = lax.broadcasted_iota(jnp.int32, (8, latent_count), 0) == 0
            stat = jnp.where(line, top, total[head_dim : head_dim + 8])
            for half_at in range(2):
                at = slice(half_at * side_count, (half_at + 1) * side_count)
                part_ref[pair, half_at, which * extent : which * extent + head_dim, :] = total[
                    :head_dim, at
                ]
                part_ref[
                    pair, half_at, which * extent + head_dim : (which + 1) * extent, :
                ] = stat[:, at]
            current = peak
        peak_ref[...] = current
        to_twin(pair).start()

    def step(pair, _):
        @pl.when(pair >= 2)
        def _():
            to_twin(pair - 2).wait_recv()

        @pl.when(pair >= LAG)
        def _():
            wait_rows(pair - LAG)

        attend(pair, False)

        @pl.when(pair >= 2)
        def _():
            send_rows(pair - 2)

        @pl.when(jnp.logical_and(pair >= LAG, lax.rem(pair - LAG, per_group) == per_group - 1))
        def _():
            send_cols(lax.div(pair - LAG, per_group))

        return 0

    def late_rows(pair):
        wait_rows(pair)
        with_rows(pair)
        if pair % per_group == per_group - 1:
            send_cols(pair // per_group)

    lax.fori_loop(0, pairs - 1, step, 0)
    to_twin(pairs - 3).wait_recv()
    wait_rows(pairs - 1 - LAG)
    attend(pairs - 1, True)
    send_rows(pairs - 3)
    to_twin(pairs - 2).wait_recv()
    with_twin(pairs - 2)
    send_rows(pairs - 2)
    for pair in range(pairs - LAG, pairs - 3):
        late_rows(pair)
    to_twin(pairs - 1).wait_recv()
    with_twin(pairs - 1)
    send_rows(pairs - 1)
    for pair in range(pairs - 3, pairs):
        late_rows(pair)

    def drain(pair, _):
        to_twin(pair).wait_send()
        for step in range(1, row_count):
            for copy in to_row(pair, step):
                copy.wait_send()
        return 0

    lax.fori_loop(0, pairs, drain, 0)

    def asked_drain(step, _):
        share(step).wait_send()
        return 0

    lax.fori_loop(mine_from, mine_to, asked_drain, 0)
    for number, (down, across, _, _) in enumerate(moves):
        @pl.when(inside(down, across))
        def _(number=number):
            shift(number).wait_send()
    pieces = []
    for group in range(groups):
        items = []
        for step in range(1, half):
            for copy in to_col(group, step):
                copy.wait_recv()
        for values, stat in [(col_num[group, slot], col_stat[group, slot])] + [
            (end_num[group, step], end_stat[group, step]) for step in range(half - 1)
        ]:
            items.append((values.astype(F32), stat[0:1], stat[1:2]))
        number, _, total = merge(items, gain)
        spread_ref[group] = (number / total).T
    odd = lax.rem(row, 2)
    for group in range(groups):
        for turn in range(per_group):
            place = lax.rem(slot + turn, half) * own
            heads_here = []
            for which in range(2):
                begin = jnp.where(odd == which, 0, per_row) + place
                if own % 8 == 0:
                    heads_here.append(spread_ref[group, pl.ds(pl.multiple_of(begin, own), own), :])
                else:
                    heads_here.append(pltpu.roll(spread_ref[group], LANES - begin, 0)[:own])
            pieces.append(jnp.concatenate(heads_here, 1))
    attended = jnp.concatenate(pieces, 1)
    mean = jnp.sum(attended * attended, axis=-1, keepdims=True) * (1.0 / channels)
    normed = (attended * lax.rsqrt(mean + 1e-06)).astype(BF16)
    normed_ref[...] = normed

    for group in range(groups):
        for step in range(1, half):
            for copy in to_col(group, step):
                copy.wait_send()


def embed_attend(pixels, tissue, patch_weight, conv_weight, kv_weight, query_weight, latents):
    tile_rows, tile_cols, patch_in = pixels.shape
    tokens = tile_rows * tile_cols
    row_count, col_count = lax.axis_size("rows"), lax.axis_size("cols")
    half = col_count // 2
    latent_count = latents.shape[0]
    channels = query_weight.shape[1]
    own = latent_count // (row_count * col_count)
    pairs = HEADS // 2
    head_dim = channels // HEADS
    groups = max(1, pairs * 2 * own // LANES)
    side_count = latent_count // 2
    leave = pl.BlockSpec(memory_space=pl.ANY)
    latents = latents.reshape(row_count, half, 2, own, latents.shape[1])
    borders = 2 * tile_cols + 2 * (tile_rows + 2 * CORNER)

    def like(array):
        return pltpu.VMEM(array.shape, array.dtype)

    def blocks(*extent):
        return [
            pltpu.VMEM(extent + (head_dim, LANES), BF16), pltpu.VMEM(extent + (2, LANES), F32)
        ]

    def sems(*extent):
        return [pltpu.SemaphoreType.DMA(extent)] * 2

    return pl.pallas_call(
        functools.partial(slide, HEADS),
        out_shape=(
            pltpu.VMEM((tokens, channels), BF16),
            pltpu.VMEM((own, channels), BF16),
        ),
        in_specs=[pl.BlockSpec(memory_space=pltpu.HBM)] * 7,
        out_specs=(pl.BlockSpec(memory_space=pltpu.VMEM),) * 2,
        scratch_shapes=[
            like(array)
            for array in (pixels, tissue, patch_weight, conv_weight, kv_weight, query_weight)
        ]
        + [
            pltpu.VMEM((2, row_count, half, own, latents.shape[-1]), BF16),
            pltpu.VMEM((borders, patch_in), BF16),
            pltpu.VMEM((2, tile_rows, patch_in), BF16),
            pltpu.VMEM((tokens, channels), F32),
            pltpu.VMEM((4, tokens // 2, 3 * BLOCK), BF16),
            pltpu.VMEM((4, 3 * BLOCK, BLOCK), BF16),
            pltpu.VMEM((tokens, channels), F32),
            pltpu.VMEM((latent_count, channels), BF16),
            pltpu.VMEM((2 * pairs, tokens, LANES), BF16),
            pltpu.VMEM((2, head_dim + CORNER, tokens), BF16),
            pltpu.VMEM((tokens, LANES), BF16),
            pltpu.VMEM((tile_rows, LANES), F32),
            pltpu.VMEM((2, tokens, latent_count), F32),
            pltpu.VMEM((8, latent_count), F32),
            pltpu.VMEM((pairs + 1, 2, 2 * (head_dim + 8), side_count), F32),
            pltpu.VMEM((pairs + 1, 2 * (head_dim + 8), side_count), F32),
        ]
        + blocks(pairs + 1, row_count)
        + blocks(pairs + 1, row_count - 1)
        + [
            pltpu.VMEM((half, head_dim, LANES), F32),
            pltpu.VMEM((half, 2, LANES), F32),
            pltpu.VMEM((groups, LANES, head_dim), F32),
        ]
        + blocks(groups, half)
        + blocks(groups, half - 1)
        + [pltpu.SemaphoreType.DMA((7,)), pltpu.SemaphoreType.DMA((channels // BLOCK,))]
        + sems(channels // BLOCK)
        + sems(8)
        + sems(pairs)
        + sems(pairs, row_count - 1, 2)
        + sems(groups, half - 1, 2),
        compiler_params=pltpu.CompilerParams(
            collective_id=1, has_side_effects=True, vmem_limit_bytes=50 * 1024 * 1024
        ),
        name="slide",
    )(
        *(
            pltpu.with_memory_space_constraint(array, pltpu.HBM)
            for array in (
                pixels, tissue, patch_weight, conv_weight, kv_weight, query_weight, latents
            )
        )
    )


def finish(features_ref, normed_ref, weight_ref, features_hbm, out_ref, sem):
    store = pltpu.make_async_copy(features_ref, features_hbm, sem)
    store.start()
    out_ref[...] = dot(normed_ref[...], weight_ref[...]).astype(BF16)
    store.wait()


def place(features, normed, out_weight):
    vmem = pl.BlockSpec(memory_space=pltpu.VMEM)
    return pl.pallas_call(
        finish,
        out_shape=(
            jax.ShapeDtypeStruct(features.shape, BF16),
            jax.ShapeDtypeStruct((normed.shape[0], out_weight.shape[1]), BF16),
        ),
        in_specs=[vmem] * 3,
        out_specs=(pl.BlockSpec(memory_space=pl.ANY), vmem),
        scratch_shapes=[pltpu.SemaphoreType.DMA],
        compiler_params=pltpu.CompilerParams(vmem_limit_bytes=24 * 1024 * 1024),
        name="place",
    )(
        pltpu.with_memory_space_constraint(features, pltpu.VMEM),
        pltpu.with_memory_space_constraint(normed, pltpu.VMEM),
        pltpu.with_memory_space_constraint(out_weight, pltpu.VMEM),
    )


def shards(pixels, tissue, patch_weight, conv_weight, kv_weight, query_weight, out_weight, latents):
    tile_rows, tile_cols, _ = pixels.shape
    features, normed = embed_attend(
        pixels, tissue, patch_weight, conv_weight, kv_weight, query_weight, latents
    )
    features, latents_out = place(features, normed, out_weight)
    return (features.reshape(tile_rows, tile_cols, features.shape[1]), latents_out)


def solution(mesh):
    return jax.shard_map(
        shards,
        mesh=mesh,
        in_specs=(P("rows", "cols", None), P("rows", "cols"), P(), P(), P(), P(), P(), P()),
        out_specs=(P("rows", "cols", None), P(("rows", "cols"), None)),
        check_vma=False,
    )
```

```python
import functools

import jax
import jax.numpy as jnp
from jax import lax
from jax.experimental import pallas as pl
from jax.experimental.pallas import tpu as pltpu
from jax.sharding import PartitionSpec as P

HEADS = 16
BLOCK = 256
LANES = 128
PAD = 8
CORNER = 16
LAG = 6
PIECE = 32
LOG2_E = 1.4426950408889634
F32 = jnp.float32
BF16 = jnp.bfloat16
LOW = -1e30
MESH = pl.DeviceIdType.MESH


def dot(a, b):
    return jnp.dot(a, b, preferred_element_type=F32)


def merge(items, gain):
    top = functools.reduce(jnp.maximum, [peak for _, peak, _ in items])
    number, total = 0.0, 0.0
    for values, peak, whole in items:
        share = jnp.exp2((peak - top) * gain)
        number = number + share * values
        total = total + share * whole
    return number, top, total


def slide(
    heads,
    pixels_hbm, tissue_hbm, patch_hbm, conv_hbm, kv_hbm, ask_hbm, latent_hbm, last_hbm,
    features_ref, normed_ref, last_ref,
    pixels_ref, tissue_ref, patch_ref, conv_ref, kv_ref, ask_ref, latent_ref,
    border_ref, side_ref, embedded_ref, wide_ref, taps_ref, summed_ref,
    query_ref, keys_ref, turned_ref, bias_ref, mask_ref, score_ref, peak_ref,
    part_ref, twin_ref, row_num, row_stat, got_num, got_stat,
    build_num, build_stat, spread_ref, col_num, col_stat, end_num, end_stat,
    load_sem, patch_sem, ask_send, ask_recv, halo_send, halo_recv,
    twin_send, twin_recv, row_send, row_recv, col_send, col_recv,
):
    tile_rows, tile_cols, patch_in = pixels_ref.shape
    tokens = tile_rows * tile_cols
    latent_count, channels = query_ref.shape
    pairs = heads // 2
    head_dim = channels // heads
    gain = LOG2_E * head_dim ** -0.5
    group_width = conv_ref.shape[1]
    row_count, col_count = lax.axis_size("rows"), lax.axis_size("cols")
    half = col_count // 2
    own = normed_ref.shape[0]
    side_count = latent_count // 2
    per_row = side_count // row_count
    groups = col_num.shape[0]
    per_group = pairs // groups
    row, col = lax.axis_index("rows"), lax.axis_index("cols")
    side, slot = lax.rem(col, 2), lax.div(col, 2)
    twin = (row, slot * 2 + (1 - side))
    row_peers = [(lax.rem(row + step, row_count), col) for step in range(1, row_count)]
    col_peers = [(row, lax.rem(slot + step, half) * 2 + side) for step in range(1, half)]

    fetches = {
        name: pltpu.make_async_copy(source, target, load_sem.at[number])
        for number, (name, source, target) in enumerate(
            (
                ("pixels", pixels_hbm, pixels_ref),
                ("low", latent_hbm.at[:, :, 0], latent_ref.at[0]),
                ("high", latent_hbm.at[:, :, 1], latent_ref.at[1]),
                ("ask", ask_hbm, ask_ref), ("conv", conv_hbm, conv_ref),
                ("tissue", tissue_hbm, tissue_ref), ("kv", kv_hbm, kv_ref),
                ("last", last_hbm, last_ref),
            )
        )
    }
    blocks = channels // BLOCK

    def patch_load(step):
        at = pl.ds(pl.multiple_of(step * BLOCK, BLOCK), BLOCK)
        return pltpu.make_async_copy(
            patch_hbm.at[:, at], patch_ref.at[:, at], patch_sem.at[step]
        )

    fetches["tissue"].start()
    fetches["pixels"].start()
    for block in range(blocks):
        patch_load(block).start()

    low_cols, high_cols = slice(0, CORNER), slice(tile_cols - CORNER, tile_cols)
    top, bottom = 0, tile_cols
    left = 2 * tile_cols
    right = left + tile_rows + 2 * CORNER
    end = tile_rows - 1

    def landing(start, extent):
        return border_ref.at[start : start + extent]

    moves = (
        (1, 0, pixels_hbm.at[end], landing(top, tile_cols)),
        (-1, 0, pixels_hbm.at[0], landing(bottom, tile_cols)),
        (1, 1, pixels_hbm.at[end, high_cols], landing(left + tile_rows, CORNER)),
        (1, -1, pixels_hbm.at[end, low_cols], landing(right + tile_rows, CORNER)),
        (-1, 1, pixels_hbm.at[0, high_cols], landing(left + tile_rows + CORNER, CORNER)),
        (-1, -1, pixels_hbm.at[0, low_cols], landing(right + tile_rows + CORNER, CORNER)),
        (0, 1, side_ref.at[1], landing(left, tile_rows)),
        (0, -1, side_ref.at[0], landing(right, tile_rows)),
    )

    def inside(down, across):
        ok = None
        for at, step, count in ((row, down, row_count), (col, across, col_count)):
            if step:
                here = at + step < count if step > 0 else at + step >= 0
                ok = here if ok is None else jnp.logical_and(ok, here)
        return ok

    def shift(number):
        down, across, source, target = moves[number]
        return pltpu.make_async_remote_copy(
            src_ref=source, dst_ref=target,
            send_sem=halo_send.at[number], recv_sem=halo_recv.at[number],
            device_id=(row + down, col + across), device_id_type=MESH,
        )

    def remote(source, target, send, recv, peer):
        return pltpu.make_async_remote_copy(
            src_ref=source, dst_ref=target, send_sem=send, recv_sem=recv,
            device_id=peer, device_id_type=MESH,
        )

    barrier = pltpu.get_barrier_semaphore()
    for down, across, _, _ in moves:
        @pl.when(inside(down, across))
        def _(down=down, across=across):
            pl.semaphore_signal(
                barrier, inc=1, device_id=(row + down, col + across), device_id_type=MESH
            )
    for peer in [twin] + row_peers + col_peers:
        pl.semaphore_signal(barrier, inc=1, device_id=peer, device_id_type=MESH)
    tall = 1 + (row > 0).astype(jnp.int32) + (row < row_count - 1).astype(jnp.int32)
    broad = 1 + (col > 0).astype(jnp.int32) + (col < col_count - 1).astype(jnp.int32)
    turned_ref[:, head_dim:, :] = jnp.ones((2, CORNER, tokens), BF16)
    build_num[...] = jnp.zeros_like(build_num)
    build_stat[...] = jnp.zeros_like(build_stat)
    pl.semaphore_wait(barrier, tall * broad - 1 + 1 + len(row_peers) + len(col_peers))
    for number in range(6):
        @pl.when(inside(*moves[number][:2]))
        def _(number=number):
            shift(number).start()
    fetches["tissue"].wait()
    mask_ref[...] = jnp.zeros_like(mask_ref)
    mask_ref[:, :tile_cols] = jnp.where(tissue_ref[...] > 0, 0.0, LOW)
    spot = lax.broadcasted_iota(jnp.int32, (tile_cols, LANES), 0)
    spot = spot == lax.broadcasted_iota(jnp.int32, (tile_cols, LANES), 1)
    for tile_row in range(tile_rows):
        line = jnp.broadcast_to(mask_ref[tile_row : tile_row + 1, :], (tile_cols, LANES))
        bias_ref[tile_row * tile_cols : (tile_row + 1) * tile_cols, :] = jnp.where(
            spot, line, 0.0
        ).astype(BF16)
    fetches["pixels"].wait()
    side_ref[0] = pixels_ref[:, 0, :]
    side_ref[1] = pixels_ref[:, tile_cols - 1, :]
    for number in range(6, 8):
        @pl.when(inside(*moves[number][:2]))
        def _(number=number):
            shift(number).start()
    for name in ("low", "high", "ask", "conv", "kv", "last"):
        fetches[name].start()

    def embed(step, _):
        at = pl.ds(pl.multiple_of(step * BLOCK, BLOCK), BLOCK)
        patch_load(step).wait()
        pixels = pixels_ref[...].reshape(tokens, patch_in)
        embedded_ref[:, at] = dot(pixels, patch_ref[:, at])
        return 0

    lax.fori_loop(0, blocks, embed, 0)
    for name in ("low", "high", "ask"):
        fetches[name].wait()
    shared = blocks
    mine_from = jnp.where(side == 0, 0, shared)
    mine_to = jnp.where(side == 0, shared, blocks)

    def share(step):
        at = pl.ds(pl.multiple_of(step * BLOCK, BLOCK), BLOCK)
        return remote(
            query_ref.at[:, at], query_ref.at[:, at], ask_send.at[step], ask_recv.at[step], twin
        )

    def ask(step, _):
        at = pl.ds(pl.multiple_of(step * BLOCK, BLOCK), BLOCK)
        latents = latent_ref[...].reshape(latent_count, ask_ref.shape[0])
        query_ref[:, at] = dot(latents, ask_ref[:, at]).astype(BF16)
        share(step).start()
        return 0

    lax.fori_loop(mine_from, mine_to, ask, 0)
    fetches["conv"].wait()
    for number, (down, across, _, target) in enumerate(moves):
        @pl.when(inside(-down, -across))
        def _(number=number):
            shift(number).wait_recv()

        @pl.when(jnp.logical_not(inside(-down, -across)))
        def _(target=target):
            target[...] = jnp.zeros(target.shape, BF16)

    rows_ext = tile_rows + 2
    col_ext = tile_cols + PAD
    same = (
        lax.broadcasted_iota(jnp.int32, (BLOCK, BLOCK), 0) // group_width
        == lax.broadcasted_iota(jnp.int32, (BLOCK, BLOCK), 1) // group_width
    )
    side_slot = lax.broadcasted_iota(jnp.int32, (rows_ext, PAD, BLOCK), 1)
    thin = (1, PAD, BLOCK)

    def border(values, upper, lower):
        return (
            jnp.broadcast_to(values[upper : upper + 1][:, None, :], thin),
            jnp.broadcast_to(values[:tile_rows][:, None, :], (tile_rows, PAD, BLOCK)),
            jnp.broadcast_to(values[lower : lower + 1][:, None, :], thin),
        )

    for block in range(blocks):
        lanes = slice(block * BLOCK, (block + 1) * BLOCK)
        edges = dot(border_ref[...], patch_ref[:, lanes])
        inner = jnp.concatenate(
            [edges[top:bottom], embedded_ref[:, lanes], edges[bottom:left]], 0
        )
        upper, middle, lower = border(
            edges[left:right], tile_rows + CORNER - 1, tile_rows + 2 * CORNER - 1
        )
        from_left = jnp.concatenate([middle, lower, upper], 0)
        upper, middle, lower = border(edges[right:], tile_rows, tile_rows + CORNER)
        from_right = jnp.concatenate([upper, middle, lower], 0)
        flank = jnp.where(side_slot == PAD - 1, from_left, from_right)
        full = jnp.concatenate(
            [inner.reshape(rows_ext, tile_cols, BLOCK), flank], 1
        ).reshape(rows_ext * col_ext, BLOCK)
        for col_shift in range(3):
            moved = inner
            if col_shift != 1:
                moved = pltpu.roll(full, 1 if col_shift == 0 else rows_ext * col_ext - 1, 0)
                moved = moved.reshape(rows_ext, col_ext, BLOCK)[:, :tile_cols]
            moved = moved.astype(BF16).reshape(rows_ext // 2, 2, tile_cols, BLOCK)
            even, odd = moved[:, 0], moved[:, 1]
            near, far, here, after = even[:-1], even[1:], odd[:-1], odd[1:]
            if col_shift == 1:
                centres = [here, far]
            at = slice(col_shift * BLOCK, (col_shift + 1) * BLOCK)
            for number, mixed in enumerate((near - far, here + far, far - here, here - after)):
                wide_ref[number, :, at] = mixed.reshape(tokens // 2, BLOCK)
            ends = [conv_ref[3 * line + col_shift, :, lanes].astype(F32) for line in range(3)]
            outer = ends[0] + ends[2]
            for number, small in enumerate(
                (ends[0], (outer + ends[1]) * 0.5, (outer - ends[1]) * 0.5, ends[2])
            ):
                tiled = jnp.concatenate([small.astype(BF16)] * (BLOCK // group_width), 0)
                taps_ref[number, at, :] = jnp.where(same, tiled, jnp.zeros_like(tiled))
        parts = [dot(wide_ref[number], taps_ref[number]) for number in range(4)]
        upper = (parts[1] + parts[2]) + parts[0]
        lower = parts[1] - parts[2] - parts[3]
        split = (tile_rows // 2, tile_cols, BLOCK)
        both = [
            half_rows.reshape(split) + centre.astype(F32)
            for half_rows, centre in zip((upper, lower), centres)
        ]
        summed_ref[:, lanes] = jnp.stack(both, 1).reshape(tokens, BLOCK)

    inverse = 1.0 / channels

    def normalise(step, _):
        for part in range(LANES // PIECE):
            at = pl.ds(pl.multiple_of(step * LANES + part * PIECE, PIECE), PIECE)
            values = summed_ref[at, :]
            centred = values - jnp.sum(values, axis=-1, keepdims=True) * inverse
            variance = jnp.sum(centred * centred, axis=-1, keepdims=True) * inverse
            features_ref[at, :] = (centred * lax.rsqrt(variance + 1e-05)).astype(BF16)
        return 0

    def project(step, _):
        at = pl.ds(pl.multiple_of(step * BLOCK, BLOCK), BLOCK)
        found = dot(features_ref[...], kv_ref[:, at]).astype(BF16)
        for inner in range(BLOCK // LANES):
            keys_ref[step * (BLOCK // LANES) + inner] = found[
                :, inner * LANES : (inner + 1) * LANES
            ]
        return 0

    lax.fori_loop(0, tokens // LANES, normalise, 0)
    fetches["kv"].wait()
    lax.fori_loop(0, 2 * channels // BLOCK, project, 0)

    lane = lax.broadcasted_iota(jnp.int32, (1, LANES), 1)
    low = lane < head_dim
    query_low = lax.broadcasted_iota(jnp.int32, (latent_count, LANES), 1) < head_dim
    ones = jnp.ones((latent_count, LANES), BF16)
    chunk = tokens // 2
    fresh = jnp.full((8, latent_count), -3e38, F32)

    def ordered(pair, which):
        at = pl.ds(pl.multiple_of(pair * LANES, LANES), LANES)
        turn = lax.rem(pair, per_group)
        pieces = []
        for line in range(2 * row_count):
            start = (line if which == 0 else line ^ 1) * per_row
            if own % CORNER == 0:
                for place in range(half):
                    source = start + lax.rem(place - turn + half, half) * own
                    pieces.append(query_ref[pl.ds(pl.multiple_of(source, own), own), at])
            else:
                block = query_ref[start : start + per_row, at].astype(F32)
                pieces.append(pltpu.roll(block, turn * own, 0).astype(BF16))
        return jnp.concatenate(pieces, 0)

    def asked(pair, which):
        queries = ordered(pair, which)
        mine = query_low if which == 0 else jnp.logical_not(query_low)
        return jnp.concatenate([jnp.where(mine, queries, jnp.zeros_like(queries)), ones], 1)

    def score(pair, part, queries, which, peak):
        at = slice(part * chunk, (part + 1) * chunk)
        keys = jnp.concatenate([keys_ref[pair, at, :], bias_ref[at, :]], 1)
        scores = lax.dot_general(
            keys, queries, (((1,), (1,)), ((), ())), preferred_element_type=F32
        )
        score_ref[which, at, :] = scores
        return jnp.maximum(peak, jnp.max(scores.reshape(chunk // 8, 8, latent_count), 0))

    def weigh(part, which, peak, total):
        at = slice(part * chunk, (part + 1) * chunk)
        weights = jnp.exp2((score_ref[which, at, :] - peak) * gain).astype(BF16)
        return total + dot(turned_ref[which, :, at], weights)

    def to_twin(pair):
        return remote(
            part_ref.at[pair, 1 - side], twin_ref.at[pair],
            twin_send.at[pair], twin_recv.at[pair], twin,
        )

    def to_row(pair, step):
        target = lax.rem(row + step, row_count)
        return [
            remote(
                source.at[pair, target], landing.at[pair, step - 1],
                row_send.at[pair, step - 1, kind], row_recv.at[pair, step - 1, kind],
                row_peers[step - 1],
            )
            for kind, (source, landing) in enumerate(((row_num, got_num), (row_stat, got_stat)))
        ]

    def to_col(group, step):
        target = lax.rem(slot + step, half)
        return [
            remote(
                source.at[group, target], landing.at[group, step - 1],
                col_send.at[group, step - 1, kind], col_recv.at[group, step - 1, kind],
                col_peers[step - 1],
            )
            for kind, (source, landing) in enumerate(((col_num, end_num), (col_stat, end_stat)))
        ]

    first_line = lax.broadcasted_iota(jnp.int32, (2, LANES), 0) == 0
    region = lax.div(lax.rem(lane, per_row), own)
    extent = head_dim + 8

    def with_twin(pair):
        merged = []
        for which in range(2):
            base = which * extent
            items = []
            for values in (part_ref.at[pair, side], twin_ref.at[pair]):
                stat = values[base + head_dim : base + extent, :]
                items.append((values[base : base + head_dim, :], stat[0:1], stat[1:2]))
            merged.append(merge(items, gain))
        for target in range(row_count):
            tile = target * per_row // LANES
            at = slice(tile * LANES, (tile + 1) * LANES)
            begin, after = merged if target % 2 == 0 else merged[::-1]
            number, peak, total = [
                jnp.where(low, one[:, at], two[:, at]) for one, two in zip(begin, after)
            ]
            row_num[pair, target] = number.astype(BF16)
            row_stat[pair, target] = jnp.where(first_line, peak, total)

    def with_rows(pair):
        items = []
        for values, stat in [(row_num[pair, row], row_stat[pair, row])] + [
            (got_num[pair, step], got_stat[pair, step]) for step in range(row_count - 1)
        ]:
            items.append((values.astype(F32), stat[0:1], stat[1:2]))
        number, peak, total = merge(items, gain)
        stat = jnp.where(first_line, peak, total)
        turn = lax.rem(pair, per_group)
        for target in range(half):
            here = region == lax.rem(turn + target, half)
            build_num[target] = jnp.where(here, number, build_num[target])
            build_stat[target] = jnp.where(here, stat, build_stat[target])

    def send_rows(pair):
        for step in range(1, row_count):
            for copy in to_row(pair, step):
                copy.start()

    def wait_rows(pair):
        for step in range(1, row_count):
            for copy in to_row(pair, step):
                copy.wait_recv()

    def send_cols(group):
        col_num[group] = build_num[...].astype(BF16)
        col_stat[group] = build_stat[...]
        for step in range(1, half):
            for copy in to_col(group, step):
                copy.start()

    def asked_wait(step, _):
        share(step).wait_recv()
        return 0

    lax.fori_loop(0, mine_from, asked_wait, 0)
    lax.fori_loop(mine_to, blocks, asked_wait, 0)
    peak = fresh
    queries = asked(0, 0)
    for part in range(2):
        peak = score(0, part, queries, 0, peak)
    peak_ref[...] = peak

    def attend(pair, final):
        turned = keys_ref[pairs + pair].T
        for which in range(2):
            turned_ref[which, :head_dim, :] = turned[which * head_dim : (which + 1) * head_dim]
        current = peak_ref[...]
        for which in range(2):
            following = pair if which == 0 else pair + 1
            ahead = not (final and which == 1)
            if ahead:
                queries = asked(following, 1 - which)
            if which == 0:
                with_twin(jnp.where(pair >= 2, pair - 2, pairs))
            else:
                with_rows(jnp.where(pair >= LAG, pair - LAG, pairs))
            top = jnp.max(current, 0, keepdims=True)
            total = jnp.zeros((head_dim + CORNER, latent_count), F32)
            peak = fresh
            for part in range(2):
                if ahead:
                    peak = score(following, part, queries, 1 - which, peak)
                total = weigh(part, which, top, total)
            line = lax.broadcasted_iota(jnp.int32, (8, latent_count), 0) == 0
            stat = jnp.where(line, top, total[head_dim : head_dim + 8])
            for half_at in range(2):
                at = slice(half_at * side_count, (half_at + 1) * side_count)
                part_ref[pair, half_at, which * extent : which * extent + head_dim, :] = total[
                    :head_dim, at
                ]
                part_ref[
                    pair, half_at, which * extent + head_dim : (which + 1) * extent, :
                ] = stat[:, at]
            current = peak
        peak_ref[...] = current
        to_twin(pair).start()

    def step(pair, _):
        @pl.when(pair >= 2)
        def _():
            to_twin(pair - 2).wait_recv()

        @pl.when(pair >= LAG)
        def _():
            wait_rows(pair - LAG)

        attend(pair, False)

        @pl.when(pair >= 2)
        def _():
            send_rows(pair - 2)

        @pl.when(jnp.logical_and(pair >= LAG, lax.rem(pair - LAG, per_group) == per_group - 1))
        def _():
            send_cols(lax.div(pair - LAG, per_group))

        return 0

    def late_rows(pair):
        wait_rows(pair)
        with_rows(pair)
        if pair % per_group == per_group - 1:
            send_cols(pair // per_group)

    lax.fori_loop(0, pairs - 1, step, 0)
    to_twin(pairs - 3).wait_recv()
    wait_rows(pairs - 1 - LAG)
    attend(pairs - 1, True)
    send_rows(pairs - 3)
    to_twin(pairs - 2).wait_recv()
    with_twin(pairs - 2)
    send_rows(pairs - 2)
    for pair in range(pairs - LAG, pairs - 3):
        late_rows(pair)
    to_twin(pairs - 1).wait_recv()
    with_twin(pairs - 1)
    send_rows(pairs - 1)
    for pair in range(pairs - 3, pairs):
        late_rows(pair)

    def drain(pair, _):
        to_twin(pair).wait_send()
        for step in range(1, row_count):
            for copy in to_row(pair, step):
                copy.wait_send()
        return 0

    lax.fori_loop(0, pairs, drain, 0)

    def asked_drain(step, _):
        share(step).wait_send()
        return 0

    lax.fori_loop(mine_from, mine_to, asked_drain, 0)
    for number, (down, across, _, _) in enumerate(moves):
        @pl.when(inside(down, across))
        def _(number=number):
            shift(number).wait_send()
    fetches["last"].wait()
    pieces = []
    for group in range(groups):
        items = []
        for step in range(1, half):
            for copy in to_col(group, step):
                copy.wait_recv()
        for values, stat in [(col_num[group, slot], col_stat[group, slot])] + [
            (end_num[group, step], end_stat[group, step]) for step in range(half - 1)
        ]:
            items.append((values.astype(F32), stat[0:1], stat[1:2]))
        number, _, total = merge(items, gain)
        spread_ref[group] = (number / total).T
    odd = lax.rem(row, 2)
    for group in range(groups):
        for turn in range(per_group):
            place = lax.rem(slot + turn, half) * own
            heads_here = []
            for which in range(2):
                begin = jnp.where(odd == which, 0, per_row) + place
                if own % 8 == 0:
                    heads_here.append(spread_ref[group, pl.ds(pl.multiple_of(begin, own), own), :])
                else:
                    heads_here.append(pltpu.roll(spread_ref[group], LANES - begin, 0)[:own])
            pieces.append(jnp.concatenate(heads_here, 1))
    attended = jnp.concatenate(pieces, 1)
    mean = jnp.sum(attended * attended, axis=-1, keepdims=True) * (1.0 / channels)
    normed = (attended * lax.rsqrt(mean + 1e-06)).astype(BF16)
    normed_ref[...] = normed

    for group in range(groups):
        for step in range(1, half):
            for copy in to_col(group, step):
                copy.wait_send()


def embed_attend(
    pixels, tissue, patch_weight, conv_weight, kv_weight, query_weight, latents, out_weight
):
    tile_rows, tile_cols, patch_in = pixels.shape
    tokens = tile_rows * tile_cols
    row_count, col_count = lax.axis_size("rows"), lax.axis_size("cols")
    half = col_count // 2
    latent_count = latents.shape[0]
    channels = query_weight.shape[1]
    own = latent_count // (row_count * col_count)
    pairs = HEADS // 2
    head_dim = channels // HEADS
    groups = max(1, pairs * 2 * own // LANES)
    side_count = latent_count // 2
    leave = pl.BlockSpec(memory_space=pl.ANY)
    latents = latents.reshape(row_count, half, 2, own, latents.shape[1])
    borders = 2 * tile_cols + 2 * (tile_rows + 2 * CORNER)

    def like(array):
        return pltpu.VMEM(array.shape, array.dtype)

    def blocks(*extent):
        return [
            pltpu.VMEM(extent + (head_dim, LANES), BF16), pltpu.VMEM(extent + (2, LANES), F32)
        ]

    def sems(*extent):
        return [pltpu.SemaphoreType.DMA(extent)] * 2

    return pl.pallas_call(
        functools.partial(slide, HEADS),
        out_shape=(
            pltpu.VMEM((tokens, channels), BF16),
            pltpu.VMEM((own, channels), BF16),
            pltpu.VMEM(out_weight.shape, BF16),
        ),
        in_specs=[pl.BlockSpec(memory_space=pltpu.HBM)] * 8,
        out_specs=(pl.BlockSpec(memory_space=pltpu.VMEM),) * 3,
        scratch_shapes=[
            like(array)
            for array in (pixels, tissue, patch_weight, conv_weight, kv_weight, query_weight)
        ]
        + [
            pltpu.VMEM((2, row_count, half, own, latents.shape[-1]), BF16),
            pltpu.VMEM((borders, patch_in), BF16),
            pltpu.VMEM((2, tile_rows, patch_in), BF16),
            pltpu.VMEM((tokens, channels), F32),
            pltpu.VMEM((4, tokens // 2, 3 * BLOCK), BF16),
            pltpu.VMEM((4, 3 * BLOCK, BLOCK), BF16),
            pltpu.VMEM((tokens, channels), F32),
            pltpu.VMEM((latent_count, channels), BF16),
            pltpu.VMEM((2 * pairs, tokens, LANES), BF16),
            pltpu.VMEM((2, head_dim + CORNER, tokens), BF16),
            pltpu.VMEM((tokens, LANES), BF16),
            pltpu.VMEM((tile_rows, LANES), F32),
            pltpu.VMEM((2, tokens, latent_count), F32),
            pltpu.VMEM((8, latent_count), F32),
            pltpu.VMEM((pairs + 1, 2, 2 * (head_dim + 8), side_count), F32),
            pltpu.VMEM((pairs + 1, 2 * (head_dim + 8), side_count), F32),
        ]
        + blocks(pairs + 1, row_count)
        + blocks(pairs + 1, row_count - 1)
        + [
            pltpu.VMEM((half, head_dim, LANES), F32),
            pltpu.VMEM((half, 2, LANES), F32),
            pltpu.VMEM((groups, LANES, head_dim), F32),
        ]
        + blocks(groups, half)
        + blocks(groups, half - 1)
        + [pltpu.SemaphoreType.DMA((8,)), pltpu.SemaphoreType.DMA((channels // BLOCK,))]
        + sems(channels // BLOCK)
        + sems(8)
        + sems(pairs)
        + sems(pairs, row_count - 1, 2)
        + sems(groups, half - 1, 2),
        compiler_params=pltpu.CompilerParams(
            collective_id=1, has_side_effects=True, vmem_limit_bytes=50 * 1024 * 1024
        ),
        name="slide",
    )(
        *(
            pltpu.with_memory_space_constraint(array, pltpu.HBM)
            for array in (
                pixels, tissue, patch_weight, conv_weight, kv_weight, query_weight, latents,
                out_weight,
            )
        )
    )


def finish(features_ref, normed_ref, weight_ref, features_hbm, out_hbm, out_ref, sem):
    store = pltpu.make_async_copy(features_ref, features_hbm, sem.at[0])
    store.start()
    out_ref[...] = dot(normed_ref[...], weight_ref[...]).astype(BF16)
    last = pltpu.make_async_copy(out_ref, out_hbm, sem.at[1])
    last.start()
    last.wait()
    store.wait()


def place(features, normed, out_weight):
    vmem = pl.BlockSpec(memory_space=pltpu.VMEM)
    return pl.pallas_call(
        finish,
        out_shape=(
            jax.ShapeDtypeStruct(features.shape, BF16),
            jax.ShapeDtypeStruct((normed.shape[0], out_weight.shape[1]), BF16),
        ),
        in_specs=[vmem] * 3,
        out_specs=(pl.BlockSpec(memory_space=pl.ANY),) * 2,
        scratch_shapes=[
            pltpu.VMEM((normed.shape[0], out_weight.shape[1]), BF16),
            pltpu.SemaphoreType.DMA((2,)),
        ],
        compiler_params=pltpu.CompilerParams(vmem_limit_bytes=24 * 1024 * 1024),
        name="place",
    )(
        pltpu.with_memory_space_constraint(features, pltpu.VMEM),
        pltpu.with_memory_space_constraint(normed, pltpu.VMEM),
        pltpu.with_memory_space_constraint(out_weight, pltpu.VMEM),
    )


def shards(pixels, tissue, patch_weight, conv_weight, kv_weight, query_weight, out_weight, latents):
    tile_rows, tile_cols, _ = pixels.shape
    features, normed, out_weight = embed_attend(
        pixels, tissue, patch_weight, conv_weight, kv_weight, query_weight, latents, out_weight
    )
    features, latents_out = place(features, normed, out_weight)
    return (features.reshape(tile_rows, tile_cols, features.shape[1]), latents_out)


def solution(mesh):
    return jax.shard_map(
        shards,
        mesh=mesh,
        in_specs=(P("rows", "cols", None), P("rows", "cols"), P(), P(), P(), P(), P(), P()),
        out_specs=(P("rows", "cols", None), P(("rows", "cols"), None)),
        check_vma=False,
    )
```

```python
import functools

import jax
import jax.numpy as jnp
from jax import lax
from jax.experimental import pallas as pl
from jax.experimental.pallas import tpu as pltpu
from jax.sharding import PartitionSpec as P

HEADS = 16
BLOCK = 256
LANES = 128
PAD = 8
CORNER = 16
LAG = 6
PIECE = 32
LOG2_E = 1.4426950408889634
F32 = jnp.float32
BF16 = jnp.bfloat16
LOW = -1e30
MESH = pl.DeviceIdType.MESH


def dot(a, b):
    return jnp.dot(a, b, preferred_element_type=F32)


def merge(items, gain):
    top = functools.reduce(jnp.maximum, [peak for _, peak, _ in items])
    number, total = 0.0, 0.0
    for values, peak, whole in items:
        share = jnp.exp2((peak - top) * gain)
        number = number + share * values
        total = total + share * whole
    return number, top, total


def slide(
    heads,
    pixels_hbm, tissue_hbm, patch_hbm, conv_hbm, kv_hbm, ask_hbm, latent_hbm, last_hbm,
    features_ref, normed_ref, last_ref,
    pixels_ref, tissue_ref, patch_ref, conv_ref, kv_ref, ask_ref, latent_ref,
    border_ref, side_ref, embedded_ref, wide_ref, taps_ref, summed_ref,
    query_ref, keys_ref, turned_ref, bias_ref, mask_ref, score_ref, peak_ref,
    part_ref, twin_ref, row_num, row_stat, got_num, got_stat,
    build_num, build_stat, spread_ref, col_num, col_stat, end_num, end_stat,
    load_sem, patch_sem, ask_send, ask_recv, halo_send, halo_recv,
    twin_send, twin_recv, row_send, row_recv, col_send, col_recv,
):
    tile_rows, tile_cols, patch_in = pixels_ref.shape
    tokens = tile_rows * tile_cols
    latent_count, channels = query_ref.shape
    pairs = heads // 2
    head_dim = channels // heads
    gain = LOG2_E * head_dim ** -0.5
    group_width = conv_ref.shape[1]
    row_count, col_count = lax.axis_size("rows"), lax.axis_size("cols")
    half = col_count // 2
    own = normed_ref.shape[0]
    side_count = latent_count // 2
    per_row = side_count // row_count
    groups = col_num.shape[0]
    per_group = pairs // groups
    row, col = lax.axis_index("rows"), lax.axis_index("cols")
    side, slot = lax.rem(col, 2), lax.div(col, 2)
    twin = (row, slot * 2 + (1 - side))
    row_peers = [(lax.rem(row + step, row_count), col) for step in range(1, row_count)]
    col_peers = [(row, lax.rem(slot + step, half) * 2 + side) for step in range(1, half)]

    fetches = {
        name: pltpu.make_async_copy(source, target, load_sem.at[number])
        for number, (name, source, target) in enumerate(
            (
                ("pixels", pixels_hbm, pixels_ref),
                ("low", latent_hbm.at[:, :, 0], latent_ref.at[0]),
                ("high", latent_hbm.at[:, :, 1], latent_ref.at[1]),
                ("ask", ask_hbm, ask_ref), ("conv", conv_hbm, conv_ref),
                ("tissue", tissue_hbm, tissue_ref), ("kv", kv_hbm, kv_ref),
                ("last", last_hbm, last_ref),
            )
        )
    }
    blocks = channels // BLOCK

    def patch_load(step):
        at = pl.ds(pl.multiple_of(step * BLOCK, BLOCK), BLOCK)
        return pltpu.make_async_copy(
            patch_hbm.at[:, at], patch_ref.at[:, at], patch_sem.at[step]
        )

    fetches["tissue"].start()
    fetches["pixels"].start()
    for block in range(blocks):
        patch_load(block).start()

    low_cols, high_cols = slice(0, CORNER), slice(tile_cols - CORNER, tile_cols)
    top, bottom = 0, tile_cols
    left = 2 * tile_cols
    right = left + tile_rows + 2 * CORNER
    end = tile_rows - 1

    def landing(start, extent):
        return border_ref.at[start : start + extent]

    moves = (
        (1, 0, pixels_hbm.at[end], landing(top, tile_cols)),
        (-1, 0, pixels_hbm.at[0], landing(bottom, tile_cols)),
        (1, 1, pixels_hbm.at[end, high_cols], landing(left + tile_rows, CORNER)),
        (1, -1, pixels_hbm.at[end, low_cols], landing(right + tile_rows, CORNER)),
        (-1, 1, pixels_hbm.at[0, high_cols], landing(left + tile_rows + CORNER, CORNER)),
        (-1, -1, pixels_hbm.at[0, low_cols], landing(right + tile_rows + CORNER, CORNER)),
        (0, 1, side_ref.at[1], landing(left, tile_rows)),
        (0, -1, side_ref.at[0], landing(right, tile_rows)),
    )

    def inside(down, across):
        ok = None
        for at, step, count in ((row, down, row_count), (col, across, col_count)):
            if step:
                here = at + step < count if step > 0 else at + step >= 0
                ok = here if ok is None else jnp.logical_and(ok, here)
        return ok

    def shift(number):
        down, across, source, target = moves[number]
        return pltpu.make_async_remote_copy(
            src_ref=source, dst_ref=target,
            send_sem=halo_send.at[number], recv_sem=halo_recv.at[number],
            device_id=(row + down, col + across), device_id_type=MESH,
        )

    def remote(source, target, send, recv, peer):
        return pltpu.make_async_remote_copy(
            src_ref=source, dst_ref=target, send_sem=send, recv_sem=recv,
            device_id=peer, device_id_type=MESH,
        )

    barrier = pltpu.get_barrier_semaphore()
    for down, across, _, _ in moves:
        @pl.when(inside(down, across))
        def _(down=down, across=across):
            pl.semaphore_signal(
                barrier, inc=1, device_id=(row + down, col + across), device_id_type=MESH
            )
    for peer in [twin] + row_peers + col_peers:
        pl.semaphore_signal(barrier, inc=1, device_id=peer, device_id_type=MESH)
    tall = 1 + (row > 0).astype(jnp.int32) + (row < row_count - 1).astype(jnp.int32)
    broad = 1 + (col > 0).astype(jnp.int32) + (col < col_count - 1).astype(jnp.int32)
    turned_ref[:, head_dim:, :] = jnp.ones((2, CORNER, tokens), BF16)
    build_num[...] = jnp.zeros_like(build_num)
    build_stat[...] = jnp.zeros_like(build_stat)
    pl.semaphore_wait(barrier, tall * broad - 1 + 1 + len(row_peers) + len(col_peers))
    for number in range(6):
        @pl.when(inside(*moves[number][:2]))
        def _(number=number):
            shift(number).start()
    fetches["tissue"].wait()
    mask_ref[...] = jnp.zeros_like(mask_ref)
    mask_ref[:, :tile_cols] = jnp.where(tissue_ref[...] > 0, 0.0, LOW)
    spot = lax.broadcasted_iota(jnp.int32, (tile_cols, LANES), 0)
    spot = spot == lax.broadcasted_iota(jnp.int32, (tile_cols, LANES), 1)
    for tile_row in range(tile_rows):
        line = jnp.broadcast_to(mask_ref[tile_row : tile_row + 1, :], (tile_cols, LANES))
        bias_ref[tile_row * tile_cols : (tile_row + 1) * tile_cols, :] = jnp.where(
            spot, line, 0.0
        ).astype(BF16)
    fetches["pixels"].wait()
    side_ref[0] = pixels_ref[:, 0, :]
    side_ref[1] = pixels_ref[:, tile_cols - 1, :]
    for number in range(6, 8):
        @pl.when(inside(*moves[number][:2]))
        def _(number=number):
            shift(number).start()
    for name in ("low", "high", "ask", "conv", "kv", "last"):
        fetches[name].start()

    def embed(step, _):
        at = pl.ds(pl.multiple_of(step * BLOCK, BLOCK), BLOCK)
        patch_load(step).wait()
        pixels = pixels_ref[...].reshape(tokens, patch_in)
        embedded_ref[:, at] = dot(pixels, patch_ref[:, at])
        return 0

    lax.fori_loop(0, blocks, embed, 0, unroll=4)
    for name in ("low", "high", "ask"):
        fetches[name].wait()
    shared = blocks
    mine_from = jnp.where(side == 0, 0, shared)
    mine_to = jnp.where(side == 0, shared, blocks)

    def share(step):
        at = pl.ds(pl.multiple_of(step * BLOCK, BLOCK), BLOCK)
        return remote(
            query_ref.at[:, at], query_ref.at[:, at], ask_send.at[step], ask_recv.at[step], twin
        )

    def ask(step, _):
        at = pl.ds(pl.multiple_of(step * BLOCK, BLOCK), BLOCK)
        latents = latent_ref[...].reshape(latent_count, ask_ref.shape[0])
        query_ref[:, at] = dot(latents, ask_ref[:, at]).astype(BF16)
        share(step).start()
        return 0

    lax.fori_loop(mine_from, mine_to, ask, 0)
    fetches["conv"].wait()
    for number, (down, across, _, target) in enumerate(moves):
        @pl.when(inside(-down, -across))
        def _(number=number):
            shift(number).wait_recv()

        @pl.when(jnp.logical_not(inside(-down, -across)))
        def _(target=target):
            target[...] = jnp.zeros(target.shape, BF16)

    rows_ext = tile_rows + 2
    col_ext = tile_cols + PAD
    same = (
        lax.broadcasted_iota(jnp.int32, (BLOCK, BLOCK), 0) // group_width
        == lax.broadcasted_iota(jnp.int32, (BLOCK, BLOCK), 1) // group_width
    )
    side_slot = lax.broadcasted_iota(jnp.int32, (rows_ext, PAD, BLOCK), 1)
    thin = (1, PAD, BLOCK)

    def border(values, upper, lower):
        return (
            jnp.broadcast_to(values[upper : upper + 1][:, None, :], thin),
            jnp.broadcast_to(values[:tile_rows][:, None, :], (tile_rows, PAD, BLOCK)),
            jnp.broadcast_to(values[lower : lower + 1][:, None, :], thin),
        )

    for block in range(blocks):
        lanes = slice(block * BLOCK, (block + 1) * BLOCK)
        edges = dot(border_ref[...], patch_ref[:, lanes])
        inner = jnp.concatenate(
            [edges[top:bottom], embedded_ref[:, lanes], edges[bottom:left]], 0
        )
        upper, middle, lower = border(
            edges[left:right], tile_rows + CORNER - 1, tile_rows + 2 * CORNER - 1
        )
        from_left = jnp.concatenate([middle, lower, upper], 0)
        upper, middle, lower = border(edges[right:], tile_rows, tile_rows + CORNER)
        from_right = jnp.concatenate([upper, middle, lower], 0)
        flank = jnp.where(side_slot == PAD - 1, from_left, from_right)
        full = jnp.concatenate(
            [inner.reshape(rows_ext, tile_cols, BLOCK), flank], 1
        ).reshape(rows_ext * col_ext, BLOCK)
        for col_shift in range(3):
            moved = inner
            if col_shift != 1:
                moved = pltpu.roll(full, 1 if col_shift == 0 else rows_ext * col_ext - 1, 0)
                moved = moved.reshape(rows_ext, col_ext, BLOCK)[:, :tile_cols]
            moved = moved.astype(BF16).reshape(rows_ext // 2, 2, tile_cols, BLOCK)
            even, odd = moved[:, 0], moved[:, 1]
            near, far, here, after = even[:-1], even[1:], odd[:-1], odd[1:]
            if col_shift == 1:
                centres = [here, far]
            at = slice(col_shift * BLOCK, (col_shift + 1) * BLOCK)
            for number, mixed in enumerate((near - far, here + far, far - here, here - after)):
                wide_ref[number, :, at] = mixed.reshape(tokens // 2, BLOCK)
            ends = [conv_ref[3 * line + col_shift, :, lanes].astype(F32) for line in range(3)]
            outer = ends[0] + ends[2]
            for number, small in enumerate(
                (ends[0], (outer + ends[1]) * 0.5, (outer - ends[1]) * 0.5, ends[2])
            ):
                tiled = jnp.concatenate([small.astype(BF16)] * (BLOCK // group_width), 0)
                taps_ref[number, at, :] = jnp.where(same, tiled, jnp.zeros_like(tiled))
        parts = [dot(wide_ref[number], taps_ref[number]) for number in range(4)]
        upper = (parts[1] + parts[2]) + parts[0]
        lower = parts[1] - parts[2] - parts[3]
        split = (tile_rows // 2, tile_cols, BLOCK)
        both = [
            half_rows.reshape(split) + centre.astype(F32)
            for half_rows, centre in zip((upper, lower), centres)
        ]
        summed_ref[:, lanes] = jnp.stack(both, 1).reshape(tokens, BLOCK)

    inverse = 1.0 / channels

    def normalise(step, _):
        for part in range(LANES // PIECE):
            at = pl.ds(pl.multiple_of(step * LANES + part * PIECE, PIECE), PIECE)
            values = summed_ref[at, :]
            centred = values - jnp.sum(values, axis=-1, keepdims=True) * inverse
            variance = jnp.sum(centred * centred, axis=-1, keepdims=True) * inverse
            features_ref[at, :] = (centred * lax.rsqrt(variance + 1e-05)).astype(BF16)
        return 0

    def project(step, _):
        at = pl.ds(pl.multiple_of(step * BLOCK, BLOCK), BLOCK)
        found = dot(features_ref[...], kv_ref[:, at]).astype(BF16)
        for inner in range(BLOCK // LANES):
            keys_ref[step * (BLOCK // LANES) + inner] = found[
                :, inner * LANES : (inner + 1) * LANES
            ]
        return 0

    lax.fori_loop(0, tokens // LANES, normalise, 0, unroll=4)
    fetches["kv"].wait()
    lax.fori_loop(0, 2 * channels // BLOCK, project, 0, unroll=4)

    lane = lax.broadcasted_iota(jnp.int32, (1, LANES), 1)
    low = lane < head_dim
    query_low = lax.broadcasted_iota(jnp.int32, (latent_count, LANES), 1) < head_dim
    ones = jnp.ones((latent_count, LANES), BF16)
    chunk = tokens // 2
    fresh = jnp.full((8, latent_count), -3e38, F32)

    def ordered(pair, which):
        at = pl.ds(pl.multiple_of(pair * LANES, LANES), LANES)
        turn = lax.rem(pair, per_group)
        pieces = []
        for line in range(2 * row_count):
            start = (line if which == 0 else line ^ 1) * per_row
            if own % CORNER == 0:
                for place in range(half):
                    source = start + lax.rem(place - turn + half, half) * own
                    pieces.append(query_ref[pl.ds(pl.multiple_of(source, own), own), at])
            else:
                block = query_ref[start : start + per_row, at].astype(F32)
                pieces.append(pltpu.roll(block, turn * own, 0).astype(BF16))
        return jnp.concatenate(pieces, 0)

    def asked(pair, which):
        queries = ordered(pair, which)
        mine = query_low if which == 0 else jnp.logical_not(query_low)
        return jnp.concatenate([jnp.where(mine, queries, jnp.zeros_like(queries)), ones], 1)

    def score(pair, part, queries, which, peak):
        at = slice(part * chunk, (part + 1) * chunk)
        keys = jnp.concatenate([keys_ref[pair, at, :], bias_ref[at, :]], 1)
        scores = lax.dot_general(
            keys, queries, (((1,), (1,)), ((), ())), preferred_element_type=F32
        )
        score_ref[which, at, :] = scores
        return jnp.maximum(peak, jnp.max(scores.reshape(chunk // 8, 8, latent_count), 0))

    def weigh(part, which, peak, total):
        at = slice(part * chunk, (part + 1) * chunk)
        weights = jnp.exp2((score_ref[which, at, :] - peak) * gain).astype(BF16)
        return total + dot(turned_ref[which, :, at], weights)

    def to_twin(pair):
        return remote(
            part_ref.at[pair, 1 - side], twin_ref.at[pair],
            twin_send.at[pair], twin_recv.at[pair], twin,
        )

    def to_row(pair, step):
        target = lax.rem(row + step, row_count)
        return [
            remote(
                source.at[pair, target], landing.at[pair, step - 1],
                row_send.at[pair, step - 1, kind], row_recv.at[pair, step - 1, kind],
                row_peers[step - 1],
            )
            for kind, (source, landing) in enumerate(((row_num, got_num), (row_stat, got_stat)))
        ]

    def to_col(group, step):
        target = lax.rem(slot + step, half)
        return [
            remote(
                source.at[group, target], landing.at[group, step - 1],
                col_send.at[group, step - 1, kind], col_recv.at[group, step - 1, kind],
                col_peers[step - 1],
            )
            for kind, (source, landing) in enumerate(((col_num, end_num), (col_stat, end_stat)))
        ]

    first_line = lax.broadcasted_iota(jnp.int32, (2, LANES), 0) == 0
    region = lax.div(lax.rem(lane, per_row), own)
    extent = head_dim + 8

    def with_twin(pair):
        merged = []
        for which in range(2):
            base = which * extent
            items = []
            for values in (part_ref.at[pair, side], twin_ref.at[pair]):
                stat = values[base + head_dim : base + extent, :]
                items.append((values[base : base + head_dim, :], stat[0:1], stat[1:2]))
            merged.append(merge(items, gain))
        for target in range(row_count):
            tile = target * per_row // LANES
            at = slice(tile * LANES, (tile + 1) * LANES)
            begin, after = merged if target % 2 == 0 else merged[::-1]
            number, peak, total = [
                jnp.where(low, one[:, at], two[:, at]) for one, two in zip(begin, after)
            ]
            row_num[pair, target] = number.astype(BF16)
            row_stat[pair, target] = jnp.where(first_line, peak, total)

    def with_rows(pair):
        items = []
        for values, stat in [(row_num[pair, row], row_stat[pair, row])] + [
            (got_num[pair, step], got_stat[pair, step]) for step in range(row_count - 1)
        ]:
            items.append((values.astype(F32), stat[0:1], stat[1:2]))
        number, peak, total = merge(items, gain)
        stat = jnp.where(first_line, peak, total)
        turn = lax.rem(pair, per_group)
        for target in range(half):
            here = region == lax.rem(turn + target, half)
            build_num[target] = jnp.where(here, number, build_num[target])
            build_stat[target] = jnp.where(here, stat, build_stat[target])

    def send_rows(pair):
        for step in range(1, row_count):
            for copy in to_row(pair, step):
                copy.start()

    def wait_rows(pair):
        for step in range(1, row_count):
            for copy in to_row(pair, step):
                copy.wait_recv()

    def send_cols(group):
        col_num[group] = build_num[...].astype(BF16)
        col_stat[group] = build_stat[...]
        for step in range(1, half):
            for copy in to_col(group, step):
                copy.start()

    def asked_wait(step, _):
        share(step).wait_recv()
        return 0

    lax.fori_loop(0, mine_from, asked_wait, 0)
    lax.fori_loop(mine_to, blocks, asked_wait, 0)
    peak = fresh
    queries = asked(0, 0)
    for part in range(2):
        peak = score(0, part, queries, 0, peak)
    peak_ref[...] = peak

    def attend(pair, final):
        turned = keys_ref[pairs + pair].T
        for which in range(2):
            turned_ref[which, :head_dim, :] = turned[which * head_dim : (which + 1) * head_dim]
        current = peak_ref[...]
        for which in range(2):
            following = pair if which == 0 else pair + 1
            ahead = not (final and which == 1)
            if ahead:
                queries = asked(following, 1 - which)
            if which == 0:
                with_twin(jnp.where(pair >= 2, pair - 2, pairs))
            else:
                with_rows(jnp.where(pair >= LAG, pair - LAG, pairs))
            top = jnp.max(current, 0, keepdims=True)
            total = jnp.zeros((head_dim + CORNER, latent_count), F32)
            peak = fresh
            for part in range(2):
                if ahead:
                    peak = score(following, part, queries, 1 - which, peak)
                total = weigh(part, which, top, total)
            line = lax.broadcasted_iota(jnp.int32, (8, latent_count), 0) == 0
            stat = jnp.where(line, top, total[head_dim : head_dim + 8])
            for half_at in range(2):
                at = slice(half_at * side_count, (half_at + 1) * side_count)
                part_ref[pair, half_at, which * extent : which * extent + head_dim, :] = total[
                    :head_dim, at
                ]
                part_ref[
                    pair, half_at, which * extent + head_dim : (which + 1) * extent, :
                ] = stat[:, at]
            current = peak
        peak_ref[...] = current
        to_twin(pair).start()

    def step(pair, _):
        @pl.when(pair >= 2)
        def _():
            to_twin(pair - 2).wait_recv()

        @pl.when(pair >= LAG)
        def _():
            wait_rows(pair - LAG)

        attend(pair, False)

        @pl.when(pair >= 2)
        def _():
            send_rows(pair - 2)

        @pl.when(jnp.logical_and(pair >= LAG, lax.rem(pair - LAG, per_group) == per_group - 1))
        def _():
            send_cols(lax.div(pair - LAG, per_group))

        return 0

    def late_rows(pair):
        wait_rows(pair)
        with_rows(pair)
        if pair % per_group == per_group - 1:
            send_cols(pair // per_group)

    lax.fori_loop(0, pairs - 1, step, 0)
    to_twin(pairs - 3).wait_recv()
    wait_rows(pairs - 1 - LAG)
    attend(pairs - 1, True)
    send_rows(pairs - 3)
    to_twin(pairs - 2).wait_recv()
    with_twin(pairs - 2)
    send_rows(pairs - 2)
    for pair in range(pairs - LAG, pairs - 3):
        late_rows(pair)
    to_twin(pairs - 1).wait_recv()
    with_twin(pairs - 1)
    send_rows(pairs - 1)
    for pair in range(pairs - 3, pairs):
        late_rows(pair)

    def drain(pair, _):
        to_twin(pair).wait_send()
        for step in range(1, row_count):
            for copy in to_row(pair, step):
                copy.wait_send()
        return 0

    lax.fori_loop(0, pairs, drain, 0)

    def asked_drain(step, _):
        share(step).wait_send()
        return 0

    lax.fori_loop(mine_from, mine_to, asked_drain, 0)
    for number, (down, across, _, _) in enumerate(moves):
        @pl.when(inside(down, across))
        def _(number=number):
            shift(number).wait_send()
    fetches["last"].wait()
    pieces = []
    for group in range(groups):
        items = []
        for step in range(1, half):
            for copy in to_col(group, step):
                copy.wait_recv()
        for values, stat in [(col_num[group, slot], col_stat[group, slot])] + [
            (end_num[group, step], end_stat[group, step]) for step in range(half - 1)
        ]:
            items.append((values.astype(F32), stat[0:1], stat[1:2]))
        number, _, total = merge(items, gain)
        spread_ref[group] = (number / total).T
    odd = lax.rem(row, 2)
    for group in range(groups):
        for turn in range(per_group):
            place = lax.rem(slot + turn, half) * own
            heads_here = []
            for which in range(2):
                begin = jnp.where(odd == which, 0, per_row) + place
                if own % 8 == 0:
                    heads_here.append(spread_ref[group, pl.ds(pl.multiple_of(begin, own), own), :])
                else:
                    heads_here.append(pltpu.roll(spread_ref[group], LANES - begin, 0)[:own])
            pieces.append(jnp.concatenate(heads_here, 1))
    attended = jnp.concatenate(pieces, 1)
    mean = jnp.sum(attended * attended, axis=-1, keepdims=True) * (1.0 / channels)
    normed = (attended * lax.rsqrt(mean + 1e-06)).astype(BF16)
    normed_ref[...] = normed

    for group in range(groups):
        for step in range(1, half):
            for copy in to_col(group, step):
                copy.wait_send()


def embed_attend(
    pixels, tissue, patch_weight, conv_weight, kv_weight, query_weight, latents, out_weight
):
    tile_rows, tile_cols, patch_in = pixels.shape
    tokens = tile_rows * tile_cols
    row_count, col_count = lax.axis_size("rows"), lax.axis_size("cols")
    half = col_count // 2
    latent_count = latents.shape[0]
    channels = query_weight.shape[1]
    own = latent_count // (row_count * col_count)
    pairs = HEADS // 2
    head_dim = channels // HEADS
    groups = max(1, pairs * 2 * own // LANES)
    side_count = latent_count // 2
    leave = pl.BlockSpec(memory_space=pl.ANY)
    latents = latents.reshape(row_count, half, 2, own, latents.shape[1])
    borders = 2 * tile_cols + 2 * (tile_rows + 2 * CORNER)

    def like(array):
        return pltpu.VMEM(array.shape, array.dtype)

    def blocks(*extent):
        return [
            pltpu.VMEM(extent + (head_dim, LANES), BF16), pltpu.VMEM(extent + (2, LANES), F32)
        ]

    def sems(*extent):
        return [pltpu.SemaphoreType.DMA(extent)] * 2

    return pl.pallas_call(
        functools.partial(slide, HEADS),
        out_shape=(
            pltpu.VMEM((tokens, channels), BF16),
            pltpu.VMEM((own, channels), BF16),
            pltpu.VMEM(out_weight.shape, BF16),
        ),
        in_specs=[pl.BlockSpec(memory_space=pltpu.HBM)] * 8,
        out_specs=(pl.BlockSpec(memory_space=pltpu.VMEM),) * 3,
        scratch_shapes=[
            like(array)
            for array in (pixels, tissue, patch_weight, conv_weight, kv_weight, query_weight)
        ]
        + [
            pltpu.VMEM((2, row_count, half, own, latents.shape[-1]), BF16),
            pltpu.VMEM((borders, patch_in), BF16),
            pltpu.VMEM((2, tile_rows, patch_in), BF16),
            pltpu.VMEM((tokens, channels), F32),
            pltpu.VMEM((4, tokens // 2, 3 * BLOCK), BF16),
            pltpu.VMEM((4, 3 * BLOCK, BLOCK), BF16),
            pltpu.VMEM((tokens, channels), F32),
            pltpu.VMEM((latent_count, channels), BF16),
            pltpu.VMEM((2 * pairs, tokens, LANES), BF16),
            pltpu.VMEM((2, head_dim + CORNER, tokens), BF16),
            pltpu.VMEM((tokens, LANES), BF16),
            pltpu.VMEM((tile_rows, LANES), F32),
            pltpu.VMEM((2, tokens, latent_count), F32),
            pltpu.VMEM((8, latent_count), F32),
            pltpu.VMEM((pairs + 1, 2, 2 * (head_dim + 8), side_count), F32),
            pltpu.VMEM((pairs + 1, 2 * (head_dim + 8), side_count), F32),
        ]
        + blocks(pairs + 1, row_count)
        + blocks(pairs + 1, row_count - 1)
        + [
            pltpu.VMEM((half, head_dim, LANES), F32),
            pltpu.VMEM((half, 2, LANES), F32),
            pltpu.VMEM((groups, LANES, head_dim), F32),
        ]
        + blocks(groups, half)
        + blocks(groups, half - 1)
        + [pltpu.SemaphoreType.DMA((8,)), pltpu.SemaphoreType.DMA((channels // BLOCK,))]
        + sems(channels // BLOCK)
        + sems(8)
        + sems(pairs)
        + sems(pairs, row_count - 1, 2)
        + sems(groups, half - 1, 2),
        compiler_params=pltpu.CompilerParams(
            collective_id=1, has_side_effects=True, vmem_limit_bytes=50 * 1024 * 1024
        ),
        name="slide",
    )(
        *(
            pltpu.with_memory_space_constraint(array, pltpu.HBM)
            for array in (
                pixels, tissue, patch_weight, conv_weight, kv_weight, query_weight, latents,
                out_weight,
            )
        )
    )


def finish(features_ref, normed_ref, weight_ref, features_hbm, out_hbm, out_ref, sem):
    store = pltpu.make_async_copy(features_ref, features_hbm, sem.at[0])
    store.start()
    out_ref[...] = dot(normed_ref[...], weight_ref[...]).astype(BF16)
    last = pltpu.make_async_copy(out_ref, out_hbm, sem.at[1])
    last.start()
    last.wait()
    store.wait()


def place(features, normed, out_weight):
    vmem = pl.BlockSpec(memory_space=pltpu.VMEM)
    return pl.pallas_call(
        finish,
        out_shape=(
            jax.ShapeDtypeStruct(features.shape, BF16),
            jax.ShapeDtypeStruct((normed.shape[0], out_weight.shape[1]), BF16),
        ),
        in_specs=[vmem] * 3,
        out_specs=(pl.BlockSpec(memory_space=pl.ANY),) * 2,
        scratch_shapes=[
            pltpu.VMEM((normed.shape[0], out_weight.shape[1]), BF16),
            pltpu.SemaphoreType.DMA((2,)),
        ],
        compiler_params=pltpu.CompilerParams(vmem_limit_bytes=24 * 1024 * 1024),
        name="place",
    )(
        pltpu.with_memory_space_constraint(features, pltpu.VMEM),
        pltpu.with_memory_space_constraint(normed, pltpu.VMEM),
        pltpu.with_memory_space_constraint(out_weight, pltpu.VMEM),
    )


def shards(pixels, tissue, patch_weight, conv_weight, kv_weight, query_weight, out_weight, latents):
    tile_rows, tile_cols, _ = pixels.shape
    features, normed, out_weight = embed_attend(
        pixels, tissue, patch_weight, conv_weight, kv_weight, query_weight, latents, out_weight
    )
    features, latents_out = place(features, normed, out_weight)
    return (features.reshape(tile_rows, tile_cols, features.shape[1]), latents_out)


def solution(mesh):
    return jax.shard_map(
        shards,
        mesh=mesh,
        in_specs=(P("rows", "cols", None), P("rows", "cols"), P(), P(), P(), P(), P(), P()),
        out_specs=(P("rows", "cols", None), P(("rows", "cols"), None)),
        check_vma=False,
    )
```
